512 devices in a mesh: wa: 4 (over x), vert: 128 (over y, z, core).
Axes of the slice: x: 4, y: 4, z: 16, core: 2. Of those that a mesh axis runs over, the one named last changes fastest.
Arguments:
- hidden: bfloat16 [16384, 1024], P('vert', 'wa'), as said below
- norm_gain: bfloat16 [1024], P('wa'), may hold values from 0.5 to 1.5
- head_weight: bfloat16 [1024, 32128], P('wa', 'vert'), as said below
- target_ids: int32 [16384], P('vert'), may hold values from 0 to 32127
- seq_lengths: int32 [65], replicated, may hold values from 1 to 8192, as said below
Outputs:
- token_logprob: float32 [16384], P('vert')
- token_entropy: float32 [16384], P('vert')
The draws below stay inside these ranges and needn't reach their ends.
Inputs may be any that keep to these rules, and one draw needn't show every extreme that they name: `seq_lengths`: entry 0 equals 8192; every other entry lies between 1 and 128, and at least one of them equals 128. `hidden`: hidden states of any scale per slot; the norm removes it. `head_weight`: entries of order 3 / sqrt(1024) times a per-column scale.
All inputs are finite; a program needn't handle non-finite values.
Results may differ from the reference program's by a relative error of at most 0.012.
The reference program's roundings to bfloat16 on the way (of `normed`) count: a program that leaves them out, or rounds other values in their place, can miss the bound.
Values may be sent and summed in bfloat16 or wider, within the bound.
A program may use at most 64 MiB of HBM per device.

```python
import math
import jax
import jax.numpy as jnp
from jax import lax

D = 1024
VOCAB = 32128
SHORT = 128
TOKENS = 16384
LONG = 8192
SHORTS = 64


def weight_table(key):
    base_key = jax.random.fold_in(key, 7301)
    key_base, key_scale = jax.random.split(base_key)
    base = jax.random.normal(key_base, (D, VOCAB), jnp.float32) * (3.0 / math.sqrt(D))
    col_scale = jnp.exp(jax.random.uniform(key_scale, (1, VOCAB), jnp.float32, math.log(0.5), math.log(5.0)))
    table = base * col_scale
    return table


def draw_head_weight(key, part):
    return weight_table(key).astype(jnp.bfloat16)


def draw_hidden(key, part):
    own_key = jax.random.fold_in(key, 5119)
    key_main = jax.random.fold_in(own_key, 0)
    values = jax.random.normal(key_main, (TOKENS, D), jnp.float32)
    return values.astype(jnp.bfloat16)


def draw_seq_lengths(key, part):
    own_key = jax.random.fold_in(key, 2203)
    key_short = jax.random.fold_in(own_key, 11)
    key_place = jax.random.fold_in(own_key, 23)
    long_length = jnp.full((1,), LONG, jnp.int32)
    short_lengths = jax.random.randint(key_short, (SHORTS,), 1, SHORT + 1, jnp.int32)
    full_place = jax.random.randint(key_place, (), 0, SHORTS, jnp.int32)
    slot_index = jnp.arange(SHORTS, dtype=jnp.int32)
    short_lengths = jnp.where(slot_index == full_place, SHORT, short_lengths).astype(jnp.int32)
    return jnp.concatenate([long_length, short_lengths]).astype(jnp.int32)


def touch_ends(values, key, low, high):
    extent = values.shape
    spot = [jax.random.randint(jax.random.fold_in(key, axis), (), 0, extent[axis]) for axis in range(len(extent))]
    values = values.at[tuple(spot)].set(low)
    longest = extent.index(max(extent))
    spot[longest] = (spot[longest] + 1) % extent[longest]
    return values.at[tuple(spot)].set(high)


def setup_inputs(seed: int = 0) -> dict:
    key_list = jax.random.split(jax.random.key(seed), 6)
    hidden = draw_hidden(jax.random.fold_in(key_list[5], 71), 0)
    norm_gain = jnp.clip(1.0 + 0.1 * jax.random.normal(key_list[1], (D,), jnp.float32), 0.5, 1.5).astype(jnp.bfloat16)
    head_weight = draw_head_weight(jax.random.fold_in(key_list[5], 71), 0)
    target_ids = touch_ends(jax.random.randint(key_list[3], (TOKENS,), 0, VOCAB), jax.random.fold_in(key_list[3], 1), 0, VOCAB - 1).astype(jnp.int32)
    seq_lengths = draw_seq_lengths(jax.random.fold_in(key_list[5], 71), 0)
    return dict(hidden=hidden, norm_gain=norm_gain, head_weight=head_weight, target_ids=target_ids, seq_lengths=seq_lengths)


norm_epsilon = 1e-06

def live_mask(positions, seq_lengths, long_len, short_len):
    is_long = positions < long_len
    beyond = jnp.maximum(positions - long_len, 0)
    seq_index = jnp.where(is_long, 0, 1 + beyond // short_len).astype(jnp.int32)
    offset = jnp.where(is_long, positions, beyond % short_len)
    return offset < jnp.take(seq_lengths, seq_index)

def reference(hidden, norm_gain, head_weight, target_ids, seq_lengths):
    values = hidden.astype(jnp.float32)
    squares = lax.optimization_barrier(jnp.mean(values * values, axis=1, keepdims=True))
    normed = (values * lax.rsqrt(squares + norm_epsilon) * norm_gain.astype(jnp.float32)).astype(jnp.bfloat16)
    block_rows = math.gcd(TOKENS, 512)
    block_count = TOKENS // block_rows
    column_ids = jnp.arange(VOCAB, dtype=jnp.int32)

    def score_block(operands):
        row_block, block_ids = operands
        logits = jnp.dot(row_block, head_weight, preferred_element_type=jnp.float32)
        row_peak = lax.optimization_barrier(jnp.max(logits, axis=1, keepdims=True))
        log_norm = row_peak[:, 0] + jnp.log(lax.optimization_barrier(jnp.sum(jnp.exp(logits - row_peak), axis=1)))
        probs = jnp.exp(logits - log_norm[:, None])
        entropy = log_norm - lax.optimization_barrier(jnp.sum(probs * logits, axis=1))
        picked = lax.optimization_barrier(jnp.sum(jnp.where(column_ids[None, :] == block_ids[:, None], logits, 0.0), axis=1))
        return (picked - log_norm, entropy)
    logprob, entropy = lax.map(score_block, (normed.reshape(block_count, block_rows, D), target_ids.reshape(block_count, block_rows)))
    positions = jnp.arange(TOKENS, dtype=jnp.int32)
    live_rows = live_mask(positions, seq_lengths, LONG, SHORT)
    return (jnp.where(live_rows, logprob.reshape(-1), 0.0), jnp.where(live_rows, entropy.reshape(-1), 0.0))
```

```python
import jax
import jax.numpy as jnp
from jax import lax
from jax.sharding import Mesh
from jax.sharding import PartitionSpec as P

D = 1024
SHORT = 128


norm_epsilon = 1e-06

VERT = ("y", "z", "c")
TOKEN_AXES = ("z", "c")


def live_mask(positions, seq_lengths, long_len, short_len):
    is_long = positions < long_len
    beyond = jnp.maximum(positions - long_len, 0)
    seq_index = jnp.where(is_long, 0, 1 + beyond // short_len)
    offset = jnp.where(is_long, positions, beyond % short_len)
    return offset < jnp.take(seq_lengths, seq_index)


def per_device(hidden, norm_gain, head_weight, target_ids, seq_lengths):
    x_count = lax.axis_size("x")
    y_count = lax.axis_size("y")
    z_count = lax.axis_size("z")
    c_count = lax.axis_size("c")
    x_index = lax.axis_index("x")
    y_index = lax.axis_index("y")
    z_index = lax.axis_index("z")
    c_index = lax.axis_index("c")
    vert_count = y_count * z_count * c_count
    vert_index = (y_index * z_count + z_index) * c_count + c_index
    tok_local = hidden.shape[0]
    quarter = tok_local // x_count
    vocab_local = head_weight.shape[1]
    group_count = z_count * c_count

    rows = lax.all_to_all(hidden, "x", split_axis=0, concat_axis=1, tiled=True)
    gain_full = lax.all_gather(norm_gain, "x", axis=0, tiled=True)
    values = rows.astype(jnp.float32)
    squares = jnp.sum(values * values, axis=1, keepdims=True)
    normed = (
        values * lax.rsqrt(squares / D + norm_epsilon) * gain_full.astype(jnp.float32)
    ).astype(jnp.bfloat16)

    group_rows = lax.all_gather(normed, TOKEN_AXES, axis=0, tiled=True)
    group_ids = lax.all_gather(target_ids, TOKEN_AXES, axis=0)
    group_ids = lax.dynamic_slice_in_dim(group_ids, x_index * quarter, quarter, 1).reshape(-1)

    weight = lax.all_gather(head_weight, ("x", "y"), axis=0)
    weight = weight.reshape(x_count, y_count, D // x_count, vocab_local)
    logits = jnp.einsum(
        "txd,xyde->tye",
        group_rows.reshape(-1, x_count, D // x_count),
        weight,
        preferred_element_type=jnp.float32,
    )
    block_of = (lax.broadcasted_iota(jnp.int32, (1, y_count, vocab_local), 1) * z_count + z_index) * c_count + c_index
    column_ids = block_of * vocab_local + lax.broadcasted_iota(jnp.int32, (1, y_count, vocab_local), 2)
    row_peak = jnp.max(logits, axis=(1, 2))
    scaled = jnp.exp(logits - row_peak[:, None, None])
    row_sum = jnp.sum(scaled, axis=(1, 2))
    row_weighted = jnp.sum(scaled * logits, axis=(1, 2))
    row_picked = jnp.sum(jnp.where(column_ids == group_ids[:, None, None], logits, 0.0), axis=(1, 2))
    stats = jnp.stack([row_peak, row_sum, row_weighted, row_picked]).reshape(4, group_count, quarter)

    parts = lax.all_to_all(stats, TOKEN_AXES, split_axis=1, concat_axis=1, tiled=True)
    part_peak, part_sum, part_weighted, part_picked = parts[0], parts[1], parts[2], parts[3]
    highest = jnp.max(part_peak, axis=0)
    factor = jnp.exp(part_peak - highest[None, :])
    totals = jnp.sum(part_sum * factor, axis=0)
    weighted = jnp.sum(part_weighted * factor, axis=0)
    picked = jnp.sum(part_picked, axis=0)
    log_norm = highest + jnp.log(totals)
    logprob = picked - log_norm
    entropy = log_norm - weighted / totals
    full_logprob, full_entropy = (
        lax.all_gather(logprob, "x", axis=0, tiled=True),
        lax.all_gather(entropy, "x", axis=0, tiled=True),
    )
    positions = vert_index * tok_local + jnp.arange(tok_local, dtype=jnp.int32)
    live_rows = live_mask(positions, seq_lengths, vert_count * tok_local // 2, SHORT)
    return (jnp.where(live_rows, full_logprob, 0.0), jnp.where(live_rows, full_entropy, 0.0))


def solution(mesh):
    wa_count, vert_count = mesh.devices.shape
    y_count = 4
    c_count = 2
    z_count = vert_count // (y_count * c_count)
    fine = Mesh(mesh.devices.reshape(wa_count, y_count, z_count, c_count), ("x",) + VERT)
    in_specs = (P(VERT, "x"), P("x"), P("x", VERT), P(VERT), P())
    out_specs = (P(VERT), P(VERT))
    return jax.shard_map(
        per_device, mesh=fine, in_specs=in_specs, out_specs=out_specs, check_vma=False
    )
```

```python
import jax
import jax.numpy as jnp
from jax import lax
from jax.experimental import pallas as pl
from jax.experimental.pallas import tpu as pltpu
from jax.sharding import Mesh
from jax.sharding import PartitionSpec as P

D = 1024
SHORT = 128


norm_epsilon = 1e-06

VERT = ("y", "z", "c")
TOKEN_AXES = ("z", "c")


def live_mask(positions, seq_lengths, long_len, short_len):
    is_long = positions < long_len
    beyond = jnp.maximum(positions - long_len, 0)
    seq_index = jnp.where(is_long, 0, 1 + beyond // short_len)
    offset = jnp.where(is_long, positions, beyond % short_len)
    return offset < jnp.take(seq_lengths, seq_index)


MESH_IDS = pl.DeviceIdType.MESH


def gather_kernel(
    normed_ref, weight_ref, ids_ref, normed_out, weight_out, ids_out,
    row_send, row_recv, weight_send, weight_recv, id_send, id_recv, own_sems,
):
    x_count = lax.axis_size("x")
    y_count = lax.axis_size("y")
    z_count = lax.axis_size("z")
    c_count = lax.axis_size("c")
    x_index = lax.axis_index("x")
    y_index = lax.axis_index("y")
    z_index = lax.axis_index("z")
    c_index = lax.axis_index("c")
    row_group = z_count * c_count
    weight_group = x_count * y_count
    row_rank = z_index * c_count + c_index
    weight_rank = x_index * y_count + y_index

    def row_peer(step):
        rank = lax.rem(row_rank + step, row_group)
        return rank, (x_index, y_index, rank // c_count, rank % c_count)

    def weight_peer(step):
        rank = lax.rem(weight_rank + step, weight_group)
        return rank, (rank // y_count, rank % y_count, z_index, c_index)

    barrier = pltpu.get_barrier_semaphore()
    for step in range(1, row_group):
        pl.semaphore_signal(barrier, inc=1, device_id=row_peer(step)[1], device_id_type=MESH_IDS)
    for step in range(1, weight_group):
        pl.semaphore_signal(barrier, inc=1, device_id=weight_peer(step)[1], device_id_type=MESH_IDS)
    pl.semaphore_wait(barrier, row_group - 1 + weight_group - 1)

    own = [
        pltpu.make_async_copy(normed_ref, normed_out.at[row_rank], own_sems.at[0]),
        pltpu.make_async_copy(weight_ref, weight_out.at[weight_rank], own_sems.at[1]),
        pltpu.make_async_copy(ids_ref, ids_out.at[row_rank], own_sems.at[2]),
    ]
    for copy in own:
        copy.start()

    sends = []
    for step in range(1, weight_group):
        _, device = weight_peer(step)
        copy = pltpu.make_async_remote_copy(
            src_ref=weight_ref, dst_ref=weight_out.at[weight_rank],
            send_sem=weight_send.at[step - 1], recv_sem=weight_recv.at[weight_rank],
            device_id=device, device_id_type=MESH_IDS,
        )
        copy.start()
        sends.append(copy)
    for step in range(1, row_group):
        _, device = row_peer(step)
        for src, dst, send_sem, recv_sem in (
            (ids_ref, ids_out, id_send, id_recv),
            (normed_ref, normed_out, row_send, row_recv),
        ):
            copy = pltpu.make_async_remote_copy(
                src_ref=src, dst_ref=dst.at[row_rank],
                send_sem=send_sem.at[step - 1], recv_sem=recv_sem.at[row_rank],
                device_id=device, device_id_type=MESH_IDS,
            )
            copy.start()
            sends.append(copy)

    for copy in own:
        copy.wait()
    for copy in sends:
        copy.wait_send()
    for step in range(1, weight_group):
        source = lax.rem(weight_rank + weight_group - step, weight_group)
        pltpu.make_async_remote_copy(
            src_ref=weight_ref, dst_ref=weight_out.at[source],
            send_sem=weight_send.at[0], recv_sem=weight_recv.at[source],
            device_id=weight_peer(step)[1], device_id_type=MESH_IDS,
        ).wait_recv()
    for step in range(1, row_group):
        source = lax.rem(row_rank + row_group - step, row_group)
        for src, dst, send_sem, recv_sem in (
            (ids_ref, ids_out, id_send, id_recv),
            (normed_ref, normed_out, row_send, row_recv),
        ):
            pltpu.make_async_remote_copy(
                src_ref=src, dst_ref=dst.at[source],
                send_sem=send_sem.at[0], recv_sem=recv_sem.at[source],
                device_id=row_peer(step)[1], device_id_type=MESH_IDS,
            ).wait_recv()


def gather_groups(normed, weight, ids, row_group, weight_group):
    any_spec = pl.BlockSpec(memory_space=pl.ANY)
    return pl.pallas_call(
        gather_kernel,
        out_shape=(
            jax.ShapeDtypeStruct((row_group,) + normed.shape, normed.dtype),
            jax.ShapeDtypeStruct((weight_group,) + weight.shape, weight.dtype),
            jax.ShapeDtypeStruct((row_group,) + ids.shape, ids.dtype),
        ),
        in_specs=[any_spec] * 3,
        out_specs=(any_spec, any_spec, any_spec),
        scratch_shapes=[
            pltpu.SemaphoreType.DMA((row_group - 1,)),
            pltpu.SemaphoreType.DMA((row_group,)),
            pltpu.SemaphoreType.DMA((weight_group - 1,)),
            pltpu.SemaphoreType.DMA((weight_group,)),
            pltpu.SemaphoreType.DMA((row_group - 1,)),
            pltpu.SemaphoreType.DMA((row_group,)),
            pltpu.SemaphoreType.DMA((3,)),
        ],
        compiler_params=pltpu.CompilerParams(collective_id=0, has_side_effects=True),
    )(normed, weight, ids)


def per_device(hidden, norm_gain, head_weight, target_ids, seq_lengths):
    x_count = lax.axis_size("x")
    y_count = lax.axis_size("y")
    z_count = lax.axis_size("z")
    c_count = lax.axis_size("c")
    x_index = lax.axis_index("x")
    y_index = lax.axis_index("y")
    z_index = lax.axis_index("z")
    c_index = lax.axis_index("c")
    vert_count = y_count * z_count * c_count
    vert_index = (y_index * z_count + z_index) * c_count + c_index
    tok_local = hidden.shape[0]
    quarter = tok_local // x_count
    vocab_local = head_weight.shape[1]
    group_count = z_count * c_count

    rows = lax.all_to_all(hidden, "x", split_axis=0, concat_axis=1, tiled=True)
    gain_full = lax.all_gather(norm_gain, "x", axis=0, tiled=True)
    values = rows.astype(jnp.float32)
    squares = jnp.sum(values * values, axis=1, keepdims=True)
    normed = (
        values * lax.rsqrt(squares / D + norm_epsilon) * gain_full.astype(jnp.float32)
    ).astype(jnp.bfloat16)

    group_rows, weight, group_ids = gather_groups(
        normed, head_weight, target_ids.reshape(1, -1), group_count, x_count * y_count
    )
    group_rows = group_rows.reshape(-1, D)
    group_ids = lax.dynamic_slice_in_dim(group_ids[:, 0, :], x_index * quarter, quarter, 1).reshape(-1)
    weight = weight.reshape(x_count, y_count, D // x_count, vocab_local)
    logits = jnp.einsum(
        "txd,xyde->tye",
        group_rows.reshape(-1, x_count, D // x_count),
        weight,
        preferred_element_type=jnp.float32,
    )
    block_of = (lax.broadcasted_iota(jnp.int32, (1, y_count, vocab_local), 1) * z_count + z_index) * c_count + c_index
    column_ids = block_of * vocab_local + lax.broadcasted_iota(jnp.int32, (1, y_count, vocab_local), 2)
    row_peak = jnp.max(logits, axis=(1, 2))
    scaled = jnp.exp(logits - row_peak[:, None, None])
    row_sum = jnp.sum(scaled, axis=(1, 2))
    row_weighted = jnp.sum(scaled * logits, axis=(1, 2))
    row_picked = jnp.sum(jnp.where(column_ids == group_ids[:, None, None], logits, 0.0), axis=(1, 2))
    stats = jnp.stack([row_peak, row_sum, row_weighted, row_picked]).reshape(4, group_count, quarter)

    parts = lax.all_to_all(stats, TOKEN_AXES, split_axis=1, concat_axis=1, tiled=True)
    part_peak, part_sum, part_weighted, part_picked = parts[0], parts[1], parts[2], parts[3]
    highest = jnp.max(part_peak, axis=0)
    factor = jnp.exp(part_peak - highest[None, :])
    totals = jnp.sum(part_sum * factor, axis=0)
    weighted = jnp.sum(part_weighted * factor, axis=0)
    picked = jnp.sum(part_picked, axis=0)
    log_norm = highest + jnp.log(totals)
    logprob = picked - log_norm
    entropy = log_norm - weighted / totals
    full_logprob, full_entropy = (
        lax.all_gather(logprob, "x", axis=0, tiled=True),
        lax.all_gather(entropy, "x", axis=0, tiled=True),
    )
    positions = vert_index * tok_local + jnp.arange(tok_local, dtype=jnp.int32)
    live_rows = live_mask(positions, seq_lengths, vert_count * tok_local // 2, SHORT)
    return (jnp.where(live_rows, full_logprob, 0.0), jnp.where(live_rows, full_entropy, 0.0))


def solution(mesh):
    wa_count, vert_count = mesh.devices.shape
    y_count = 4
    c_count = 2
    z_count = vert_count // (y_count * c_count)
    fine = Mesh(mesh.devices.reshape(wa_count, y_count, z_count, c_count), ("x",) + VERT)
    in_specs = (P(VERT, "x"), P("x"), P("x", VERT), P(VERT), P())
    out_specs = (P(VERT), P(VERT))
    return jax.shard_map(
        per_device, mesh=fine, in_specs=in_specs, out_specs=out_specs, check_vma=False
    )
```

```python
import jax
import jax.numpy as jnp
from jax import lax
from jax.experimental import pallas as pl
from jax.experimental.pallas import tpu as pltpu
from jax.sharding import Mesh
from jax.sharding import PartitionSpec as P

D = 1024
SHORT = 128


norm_epsilon = 1e-06

VERT = ("y", "z", "c")
TOKEN_AXES = ("z", "c")


def live_mask(positions, seq_lengths, long_len, short_len):
    is_long = positions < long_len
    beyond = jnp.maximum(positions - long_len, 0)
    seq_index = jnp.where(is_long, 0, 1 + beyond // short_len)
    offset = jnp.where(is_long, positions, beyond % short_len)
    return offset < jnp.take(seq_lengths, seq_index)


MESH_IDS = pl.DeviceIdType.MESH


def gather_kernel(
    normed_ref, weight_ref, ids_ref, normed_out, weight_out, ids_out,
    row_send, row_recv, weight_send, weight_recv, id_send, id_recv, own_sems,
):
    x_count = lax.axis_size("x")
    y_count = lax.axis_size("y")
    z_count = lax.axis_size("z")
    c_count = lax.axis_size("c")
    x_index = lax.axis_index("x")
    y_index = lax.axis_index("y")
    z_index = lax.axis_index("z")
    c_index = lax.axis_index("c")
    row_group = z_count * c_count
    weight_group = x_count * y_count
    row_rank = z_index * c_count + c_index
    weight_rank = x_index * y_count + y_index
    other_core = 1 - c_index

    def row_peer(step):
        rank = lax.rem(row_rank + step, row_group)
        return (x_index, y_index, rank // c_count, rank % c_count)

    def weight_peer(step):
        rank = lax.rem(weight_rank + step, weight_group)
        return rank, (rank // y_count, rank % y_count, z_index, c_index)

    def ring_z(shift):
        return lax.rem(z_index + shift + z_count, z_count)

    barrier = pltpu.get_barrier_semaphore()
    for step in range(1, row_group):
        pl.semaphore_signal(barrier, inc=1, device_id=row_peer(step), device_id_type=MESH_IDS)
    for step in range(1, weight_group):
        pl.semaphore_signal(barrier, inc=1, device_id=weight_peer(step)[1], device_id_type=MESH_IDS)
    pl.semaphore_wait(barrier, row_group - 1 + weight_group - 1)

    own = [
        pltpu.make_async_copy(normed_ref, normed_out.at[row_rank], own_sems.at[0]),
        pltpu.make_async_copy(weight_ref, weight_out.at[weight_rank], own_sems.at[1]),
        pltpu.make_async_copy(ids_ref, ids_out.at[row_rank], own_sems.at[2]),
    ]
    for copy in own:
        copy.start()

    sends = []

    def send_row(source_z, device, sem_index, from_input):
        slot = source_z * c_count + c_index
        copy = pltpu.make_async_remote_copy(
            src_ref=normed_ref if from_input else normed_out.at[slot],
            dst_ref=normed_out.at[slot],
            send_sem=row_send.at[sem_index], recv_sem=row_recv.at[slot],
            device_id=device, device_id_type=MESH_IDS,
        )
        copy.start()
        sends.append(copy)

    def wait_row(source_z, source_core):
        slot = source_z * c_count + source_core
        pltpu.make_async_remote_copy(
            src_ref=normed_ref, dst_ref=normed_out.at[slot],
            send_sem=row_send.at[0], recv_sem=row_recv.at[slot],
            device_id=(x_index, y_index, z_index, other_core), device_id_type=MESH_IDS,
        ).wait_recv()

    right = (x_index, y_index, ring_z(1), c_index)
    left = (x_index, y_index, ring_z(-1), c_index)
    partner = (x_index, y_index, z_index, other_core)
    right_steps = z_count // 2
    left_steps = z_count - 1 - right_steps
    sem_count = [0]

    def next_sem():
        sem_count[0] += 1
        return sem_count[0] - 1

    send_row(z_index, right, next_sem(), True)
    if left_steps > 0:
        send_row(z_index, left, next_sem(), True)
    send_row(z_index, partner, next_sem(), True)

    for step in range(1, weight_group):
        _, device = weight_peer(step)
        copy = pltpu.make_async_remote_copy(
            src_ref=weight_ref, dst_ref=weight_out.at[weight_rank],
            send_sem=weight_send.at[step - 1], recv_sem=weight_recv.at[weight_rank],
            device_id=device, device_id_type=MESH_IDS,
        )
        copy.start()
        sends.append(copy)
    for step in range(1, row_group):
        copy = pltpu.make_async_remote_copy(
            src_ref=ids_ref, dst_ref=ids_out.at[row_rank],
            send_sem=id_send.at[step - 1], recv_sem=id_recv.at[row_rank],
            device_id=row_peer(step), device_id_type=MESH_IDS,
        )
        copy.start()
        sends.append(copy)

    for step in range(1, right_steps + 1):
        from_left = ring_z(-step)
        wait_row(from_left, c_index)
        if step < right_steps:
            send_row(from_left, right, next_sem(), False)
        send_row(from_left, partner, next_sem(), False)
        if step <= left_steps:
            from_right = ring_z(step)
            wait_row(from_right, c_index)
            if step < left_steps:
                send_row(from_right, left, next_sem(), False)
            send_row(from_right, partner, next_sem(), False)

    for copy in own:
        copy.wait()
    for step in range(z_count):
        wait_row(lax.rem(z_index + step, z_count), other_core)
    for step in range(1, weight_group):
        source = lax.rem(weight_rank + weight_group - step, weight_group)
        pltpu.make_async_remote_copy(
            src_ref=weight_ref, dst_ref=weight_out.at[source],
            send_sem=weight_send.at[0], recv_sem=weight_recv.at[source],
            device_id=weight_peer(step)[1], device_id_type=MESH_IDS,
        ).wait_recv()
    for step in range(1, row_group):
        source = lax.rem(row_rank + row_group - step, row_group)
        pltpu.make_async_remote_copy(
            src_ref=ids_ref, dst_ref=ids_out.at[source],
            send_sem=id_send.at[0], recv_sem=id_recv.at[source],
            device_id=row_peer(step), device_id_type=MESH_IDS,
        ).wait_recv()
    for copy in sends:
        copy.wait_send()


def gather_groups(normed, weight, ids, row_group, weight_group):
    any_spec = pl.BlockSpec(memory_space=pl.ANY)
    return pl.pallas_call(
        gather_kernel,
        out_shape=(
            jax.ShapeDtypeStruct((row_group,) + normed.shape, normed.dtype),
            jax.ShapeDtypeStruct((weight_group,) + weight.shape, weight.dtype),
            jax.ShapeDtypeStruct((row_group,) + ids.shape, ids.dtype),
        ),
        in_specs=[any_spec] * 3,
        out_specs=(any_spec, any_spec, any_spec),
        scratch_shapes=[
            pltpu.SemaphoreType.DMA((row_group - 1,)),
            pltpu.SemaphoreType.DMA((row_group,)),
            pltpu.SemaphoreType.DMA((weight_group - 1,)),
            pltpu.SemaphoreType.DMA((weight_group,)),
            pltpu.SemaphoreType.DMA((row_group - 1,)),
            pltpu.SemaphoreType.DMA((row_group,)),
            pltpu.SemaphoreType.DMA((3,)),
        ],
        compiler_params=pltpu.CompilerParams(collective_id=0, has_side_effects=True),
    )(normed, weight, ids)


def per_device(hidden, norm_gain, head_weight, target_ids, seq_lengths):
    x_count = lax.axis_size("x")
    y_count = lax.axis_size("y")
    z_count = lax.axis_size("z")
    c_count = lax.axis_size("c")
    x_index = lax.axis_index("x")
    y_index = lax.axis_index("y")
    z_index = lax.axis_index("z")
    c_index = lax.axis_index("c")
    vert_count = y_count * z_count * c_count
    vert_index = (y_index * z_count + z_index) * c_count + c_index
    tok_local = hidden.shape[0]
    quarter = tok_local // x_count
    vocab_local = head_weight.shape[1]
    group_count = z_count * c_count

    pieces = hidden.reshape(x_count, quarter, -1)
    gain_rows = jnp.broadcast_to(norm_gain[None, None, :], (x_count, 1, norm_gain.shape[0]))
    pieces = jnp.concatenate([pieces, gain_rows], axis=1)
    rows = lax.all_to_all(pieces, "x", split_axis=0, concat_axis=2, tiled=True)[0]
    gain_full = rows[quarter]
    values = rows[:quarter].astype(jnp.float32)
    squares = jnp.sum(values * values, axis=1, keepdims=True)
    normed = (
        values * lax.rsqrt(squares / D + norm_epsilon) * gain_full.astype(jnp.float32)
    ).astype(jnp.bfloat16)

    group_rows, weight, group_ids = gather_groups(
        normed, head_weight, target_ids.reshape(1, -1), group_count, x_count * y_count
    )
    group_rows = group_rows.reshape(-1, D)
    group_ids = lax.dynamic_slice_in_dim(group_ids[:, 0, :], x_index * quarter, quarter, 1).reshape(-1)
    weight = weight.reshape(x_count, y_count, D // x_count, vocab_local)
    logits = jnp.einsum(
        "txd,xyde->tye",
        group_rows.reshape(-1, x_count, D // x_count),
        weight,
        preferred_element_type=jnp.float32,
    )
    block_of = (lax.broadcasted_iota(jnp.int32, (1, y_count, vocab_local), 1) * z_count + z_index) * c_count + c_index
    column_ids = block_of * vocab_local + lax.broadcasted_iota(jnp.int32, (1, y_count, vocab_local), 2)
    row_peak = jnp.max(logits, axis=(1, 2))
    scaled = jnp.exp(logits - row_peak[:, None, None])
    row_sum = jnp.sum(scaled, axis=(1, 2))
    row_weighted = jnp.sum(scaled * logits, axis=(1, 2))
    row_picked = jnp.sum(jnp.where(column_ids == group_ids[:, None, None], logits, 0.0), axis=(1, 2))
    stats = jnp.stack([row_peak, row_sum, row_weighted, row_picked]).reshape(4, group_count, quarter)

    parts = lax.all_to_all(stats, TOKEN_AXES, split_axis=1, concat_axis=1, tiled=True)
    part_peak, part_sum, part_weighted, part_picked = parts[0], parts[1], parts[2], parts[3]
    highest = jnp.max(part_peak, axis=0)
    factor = jnp.exp(part_peak - highest[None, :])
    totals = jnp.sum(part_sum * factor, axis=0)
    weighted = jnp.sum(part_weighted * factor, axis=0)
    picked = jnp.sum(part_picked, axis=0)
    log_norm = highest + jnp.log(totals)
    logprob = picked - log_norm
    entropy = log_norm - weighted / totals
    full_logprob, full_entropy = (
        lax.all_gather(logprob, "x", axis=0, tiled=True),
        lax.all_gather(entropy, "x", axis=0, tiled=True),
    )
    positions = vert_index * tok_local + jnp.arange(tok_local, dtype=jnp.int32)
    live_rows = live_mask(positions, seq_lengths, vert_count * tok_local // 2, SHORT)
    return (jnp.where(live_rows, full_logprob, 0.0), jnp.where(live_rows, full_entropy, 0.0))


def solution(mesh):
    wa_count, vert_count = mesh.devices.shape
    y_count = 4
    c_count = 2
    z_count = vert_count // (y_count * c_count)
    fine = Mesh(mesh.devices.reshape(wa_count, y_count, z_count, c_count), ("x",) + VERT)
    in_specs = (P(VERT, "x"), P("x"), P("x", VERT), P(VERT), P())
    out_specs = (P(VERT), P(VERT))
    return jax.shard_map(
        per_device, mesh=fine, in_specs=in_specs, out_specs=out_specs, check_vma=False
    )
```

```python
import jax
import jax.numpy as jnp
from jax import lax
from jax.experimental import pallas as pl
from jax.experimental.pallas import tpu as pltpu
from jax.sharding import Mesh
from jax.sharding import PartitionSpec as P

D = 1024
SHORT = 128


norm_epsilon = 1e-06

VERT = ("y", "z", "c")
TOKEN_AXES = ("z", "c")


def live_mask(positions, seq_lengths, long_len, short_len):
    is_long = positions < long_len
    beyond = jnp.maximum(positions - long_len, 0)
    seq_index = jnp.where(is_long, 0, 1 + beyond // short_len)
    offset = jnp.where(is_long, positions, beyond % short_len)
    return offset < jnp.take(seq_lengths, seq_index)


MESH_IDS = pl.DeviceIdType.MESH


def gather_kernel(
    normed_ref, weight_ref, ids_ref, normed_out, weight_out, ids_out,
    row_send, row_recv, weight_send, weight_recv, id_send, id_recv, own_sems,
):
    x_count = lax.axis_size("x")
    y_count = lax.axis_size("y")
    z_count = lax.axis_size("z")
    c_count = lax.axis_size("c")
    x_index = lax.axis_index("x")
    y_index = lax.axis_index("y")
    z_index = lax.axis_index("z")
    c_index = lax.axis_index("c")
    row_group = z_count * c_count
    weight_group = x_count * y_count
    row_rank = z_index * c_count + c_index
    weight_rank = x_index * y_count + y_index
    other_core = 1 - c_index

    def row_peer(step):
        rank = lax.rem(row_rank + step, row_group)
        return (x_index, y_index, rank // c_count, rank % c_count)

    def weight_peer(step):
        rank = lax.rem(weight_rank + step, weight_group)
        return rank, (rank // y_count, rank % y_count, z_index, c_index)

    def ring_z(shift):
        return lax.rem(z_index + shift + z_count, z_count)

    barrier = pltpu.get_barrier_semaphore()
    for step in range(1, row_group):
        pl.semaphore_signal(barrier, inc=1, device_id=row_peer(step), device_id_type=MESH_IDS)
    for step in range(1, weight_group):
        pl.semaphore_signal(barrier, inc=1, device_id=weight_peer(step)[1], device_id_type=MESH_IDS)
    pl.semaphore_wait(barrier, row_group - 1 + weight_group - 1)

    own = [
        pltpu.make_async_copy(normed_ref, normed_out.at[row_rank], own_sems.at[0]),
        pltpu.make_async_copy(weight_ref, weight_out.at[weight_rank], own_sems.at[1]),
        pltpu.make_async_copy(ids_ref, ids_out.at[row_rank], own_sems.at[2]),
    ]
    for copy in own:
        copy.start()

    sends = []

    def send_row(source_z, device, sem_index, from_input):
        slot = source_z * c_count + c_index
        copy = pltpu.make_async_remote_copy(
            src_ref=normed_ref if from_input else normed_out.at[slot],
            dst_ref=normed_out.at[slot],
            send_sem=row_send.at[sem_index], recv_sem=row_recv.at[slot],
            device_id=device, device_id_type=MESH_IDS,
        )
        copy.start()
        sends.append(copy)

    def wait_row(source_z, source_core):
        slot = source_z * c_count + source_core
        pltpu.make_async_remote_copy(
            src_ref=normed_ref, dst_ref=normed_out.at[slot],
            send_sem=row_send.at[0], recv_sem=row_recv.at[slot],
            device_id=(x_index, y_index, z_index, other_core), device_id_type=MESH_IDS,
        ).wait_recv()

    right = (x_index, y_index, ring_z(1), c_index)
    left = (x_index, y_index, ring_z(-1), c_index)
    partner = (x_index, y_index, z_index, other_core)
    right_steps = z_count // 2
    left_steps = z_count - 1 - right_steps
    sem_count = [0]

    def next_sem():
        sem_count[0] += 1
        return sem_count[0] - 1

    send_row(z_index, right, next_sem(), True)
    if left_steps > 0:
        send_row(z_index, left, next_sem(), True)
    send_row(z_index, partner, next_sem(), True)

    for step in range(1, weight_group):
        _, device = weight_peer(step)
        copy = pltpu.make_async_remote_copy(
            src_ref=weight_ref, dst_ref=weight_out.at[weight_rank],
            send_sem=weight_send.at[step - 1], recv_sem=weight_recv.at[weight_rank],
            device_id=device, device_id_type=MESH_IDS,
        )
        copy.start()
        sends.append(copy)
    for step in range(1, row_group):
        copy = pltpu.make_async_remote_copy(
            src_ref=ids_ref, dst_ref=ids_out.at[row_rank],
            send_sem=id_send.at[step - 1], recv_sem=id_recv.at[row_rank],
            device_id=row_peer(step), device_id_type=MESH_IDS,
        )
        copy.start()
        sends.append(copy)

    for step in range(1, right_steps + 1):
        from_left = ring_z(-step)
        wait_row(from_left, c_index)
        if step < right_steps:
            send_row(from_left, right, next_sem(), False)
        send_row(from_left, partner, next_sem(), False)
        if step <= left_steps:
            from_right = ring_z(step)
            wait_row(from_right, c_index)
            if step < left_steps:
                send_row(from_right, left, next_sem(), False)
            send_row(from_right, partner, next_sem(), False)

    for copy in own:
        copy.wait()
    for step in range(z_count):
        wait_row(lax.rem(z_index + step, z_count), other_core)
    for step in range(1, weight_group):
        source = lax.rem(weight_rank + weight_group - step, weight_group)
        pltpu.make_async_remote_copy(
            src_ref=weight_ref, dst_ref=weight_out.at[source],
            send_sem=weight_send.at[0], recv_sem=weight_recv.at[source],
            device_id=weight_peer(step)[1], device_id_type=MESH_IDS,
        ).wait_recv()
    for step in range(1, row_group):
        source = lax.rem(row_rank + row_group - step, row_group)
        pltpu.make_async_remote_copy(
            src_ref=ids_ref, dst_ref=ids_out.at[source],
            send_sem=id_send.at[0], recv_sem=id_recv.at[source],
            device_id=row_peer(step), device_id_type=MESH_IDS,
        ).wait_recv()
    for copy in sends:
        copy.wait_send()


def gather_groups(normed, weight, ids, row_group, weight_group):
    any_spec = pl.BlockSpec(memory_space=pl.ANY)
    return pl.pallas_call(
        gather_kernel,
        out_shape=(
            jax.ShapeDtypeStruct((row_group,) + normed.shape, normed.dtype),
            jax.ShapeDtypeStruct((weight_group,) + weight.shape, weight.dtype),
            jax.ShapeDtypeStruct((row_group,) + ids.shape, ids.dtype),
        ),
        in_specs=[any_spec] * 3,
        out_specs=(any_spec, any_spec, any_spec),
        scratch_shapes=[
            pltpu.SemaphoreType.DMA((row_group - 1,)),
            pltpu.SemaphoreType.DMA((row_group,)),
            pltpu.SemaphoreType.DMA((weight_group - 1,)),
            pltpu.SemaphoreType.DMA((weight_group,)),
            pltpu.SemaphoreType.DMA((row_group - 1,)),
            pltpu.SemaphoreType.DMA((row_group,)),
            pltpu.SemaphoreType.DMA((3,)),
        ],
        compiler_params=pltpu.CompilerParams(collective_id=0, has_side_effects=True),
    )(normed, weight, ids)


def stats_kernel(stats_ref, parts_out, send_sems, recv_sems, own_sem):
    x_count = lax.axis_size("x")
    z_count = lax.axis_size("z")
    c_count = lax.axis_size("c")
    x_index = lax.axis_index("x")
    y_index = lax.axis_index("y")
    z_index = lax.axis_index("z")
    c_index = lax.axis_index("c")
    group = z_count * c_count
    total = x_count * group
    rank = z_index * c_count + c_index
    flat = x_index * group + rank

    def peer(step):
        other = lax.rem(flat + step, total)
        member = other % group
        return member, (other // group, y_index, member // c_count, member % c_count)

    barrier = pltpu.get_barrier_semaphore()

    def greet(step, carry):
        pl.semaphore_signal(barrier, inc=1, device_id=peer(step)[1], device_id_type=MESH_IDS)
        return carry

    lax.fori_loop(1, total, greet, 0)
    pl.semaphore_wait(barrier, total - 1)

    own = pltpu.make_async_copy(stats_ref.at[rank], parts_out.at[x_index, rank], own_sem.at[0])
    own.start()

    def send_copy(step):
        member, device = peer(step)
        return pltpu.make_async_remote_copy(
            src_ref=stats_ref.at[member], dst_ref=parts_out.at[x_index, rank],
            send_sem=send_sems.at[step - 1], recv_sem=recv_sems.at[x_index, rank],
            device_id=device, device_id_type=MESH_IDS,
        )

    def start(step, carry):
        send_copy(step).start()
        return carry

    lax.fori_loop(1, total, start, 0)
    own.wait()

    def finish(step, carry):
        send_copy(step).wait_send()
        source = lax.rem(flat + total - step, total)
        source_x = source // group
        source_rank = source % group
        pltpu.make_async_remote_copy(
            src_ref=stats_ref.at[source_rank], dst_ref=parts_out.at[source_x, source_rank],
            send_sem=send_sems.at[step - 1], recv_sem=recv_sems.at[source_x, source_rank],
            device_id=peer(step)[1], device_id_type=MESH_IDS,
        ).wait_recv()
        return carry

    lax.fori_loop(1, total, finish, 0)


def exchange_stats(stats, x_count):
    group = stats.shape[0]
    any_spec = pl.BlockSpec(memory_space=pl.ANY)
    return pl.pallas_call(
        stats_kernel,
        out_shape=jax.ShapeDtypeStruct((x_count,) + stats.shape, stats.dtype),
        in_specs=[any_spec],
        out_specs=any_spec,
        scratch_shapes=[
            pltpu.SemaphoreType.DMA((x_count * group - 1,)),
            pltpu.SemaphoreType.DMA((x_count, group)),
            pltpu.SemaphoreType.DMA((1,)),
        ],
        compiler_params=pltpu.CompilerParams(collective_id=1, has_side_effects=True),
    )(stats)


def per_device(hidden, norm_gain, head_weight, target_ids, seq_lengths):
    x_count = lax.axis_size("x")
    y_count = lax.axis_size("y")
    z_count = lax.axis_size("z")
    c_count = lax.axis_size("c")
    x_index = lax.axis_index("x")
    y_index = lax.axis_index("y")
    z_index = lax.axis_index("z")
    c_index = lax.axis_index("c")
    vert_count = y_count * z_count * c_count
    vert_index = (y_index * z_count + z_index) * c_count + c_index
    tok_local = hidden.shape[0]
    quarter = tok_local // x_count
    vocab_local = head_weight.shape[1]
    group_count = z_count * c_count

    pieces = hidden.reshape(x_count, quarter, -1)
    gain_rows = jnp.broadcast_to(norm_gain[None, None, :], (x_count, 1, norm_gain.shape[0]))
    pieces = jnp.concatenate([pieces, gain_rows], axis=1)
    rows = lax.all_to_all(pieces, "x", split_axis=0, concat_axis=2, tiled=True)[0]
    gain_full = rows[quarter]
    values = rows[:quarter].astype(jnp.float32)
    squares = jnp.sum(values * values, axis=1, keepdims=True)
    normed = (
        values * lax.rsqrt(squares / D + norm_epsilon) * gain_full.astype(jnp.float32)
    ).astype(jnp.bfloat16)

    group_rows, weight, group_ids = gather_groups(
        normed, head_weight, target_ids.reshape(1, -1), group_count, x_count * y_count
    )
    group_rows = group_rows.reshape(-1, D)
    group_ids = lax.dynamic_slice_in_dim(group_ids[:, 0, :], x_index * quarter, quarter, 1).reshape(-1)
    weight = weight.reshape(x_count, y_count, D // x_count, vocab_local)
    logits = jnp.einsum(
        "txd,xyde->tye",
        group_rows.reshape(-1, x_count, D // x_count),
        weight,
        preferred_element_type=jnp.float32,
    )
    block_of = (lax.broadcasted_iota(jnp.int32, (1, y_count, vocab_local), 1) * z_count + z_index) * c_count + c_index
    column_ids = block_of * vocab_local + lax.broadcasted_iota(jnp.int32, (1, y_count, vocab_local), 2)
    row_peak = jnp.max(logits, axis=(1, 2))
    scaled = jnp.exp(logits - row_peak[:, None, None])
    row_sum = jnp.sum(scaled, axis=(1, 2))
    row_weighted = jnp.sum(scaled * logits, axis=(1, 2))
    row_picked = jnp.sum(jnp.where(column_ids == group_ids[:, None, None], logits, 0.0), axis=(1, 2))
    stats = jnp.stack([row_peak, row_sum, row_weighted, row_picked]).reshape(4, group_count, quarter)

    parts = exchange_stats(stats.transpose(1, 0, 2), x_count)
    part_peak, part_sum, part_weighted, part_picked = (parts[:, :, k] for k in range(4))
    highest = jnp.max(part_peak, axis=1)
    factor = jnp.exp(part_peak - highest[:, None])
    totals = jnp.sum(part_sum * factor, axis=1)
    weighted = jnp.sum(part_weighted * factor, axis=1)
    picked = jnp.sum(part_picked, axis=1)
    log_norm = highest + jnp.log(totals)
    full_logprob = (picked - log_norm).reshape(-1)
    full_entropy = (log_norm - weighted / totals).reshape(-1)
    positions = vert_index * tok_local + jnp.arange(tok_local, dtype=jnp.int32)
    live_rows = live_mask(positions, seq_lengths, vert_count * tok_local // 2, SHORT)
    return (jnp.where(live_rows, full_logprob, 0.0), jnp.where(live_rows, full_entropy, 0.0))


def solution(mesh):
    wa_count, vert_count = mesh.devices.shape
    y_count = 4
    c_count = 2
    z_count = vert_count // (y_count * c_count)
    fine = Mesh(mesh.devices.reshape(wa_count, y_count, z_count, c_count), ("x",) + VERT)
    in_specs = (P(VERT, "x"), P("x"), P("x", VERT), P(VERT), P())
    out_specs = (P(VERT), P(VERT))
    return jax.shard_map(
        per_device, mesh=fine, in_specs=in_specs, out_specs=out_specs, check_vma=False
    )
```

```python
import jax
import jax.numpy as jnp
from jax import lax
from jax.experimental import pallas as pl
from jax.experimental.pallas import tpu as pltpu
from jax.sharding import Mesh
from jax.sharding import PartitionSpec as P

D = 1024
SHORT = 128


norm_epsilon = 1e-06

VERT = ("y", "z", "c")
TOKEN_AXES = ("z", "c")


def live_mask(positions, seq_lengths, long_len, short_len):
    is_long = positions < long_len
    beyond = jnp.maximum(positions - long_len, 0)
    seq_index = jnp.where(is_long, 0, 1 + beyond // short_len)
    offset = jnp.where(is_long, positions, beyond % short_len)
    return offset < jnp.take(seq_lengths, seq_index)


MESH_IDS = pl.DeviceIdType.MESH


def gather_kernel(
    normed_ref, weight_ref, ids_ref, normed_out, weight_out, ids_out,
    row_send, row_recv, weight_send, weight_recv, id_send, id_recv, own_sems,
):
    x_count = lax.axis_size("x")
    y_count = lax.axis_size("y")
    z_count = lax.axis_size("z")
    c_count = lax.axis_size("c")
    x_index = lax.axis_index("x")
    y_index = lax.axis_index("y")
    z_index = lax.axis_index("z")
    c_index = lax.axis_index("c")
    row_group = z_count * c_count
    weight_group = x_count * y_count
    row_rank = z_index * c_count + c_index
    weight_rank = x_index * y_count + y_index
    other_core = 1 - c_index

    def row_peer(step):
        rank = lax.rem(row_rank + step, row_group)
        return (x_index, y_index, rank // c_count, rank % c_count)

    def weight_peer(step):
        rank = lax.rem(weight_rank + step, weight_group)
        return rank, (rank // y_count, rank % y_count, z_index, c_index)

    def ring_z(shift):
        return lax.rem(z_index + shift + z_count, z_count)

    barrier = pltpu.get_barrier_semaphore()
    for step in range(1, row_group):
        pl.semaphore_signal(barrier, inc=1, device_id=row_peer(step), device_id_type=MESH_IDS)
    for step in range(1, weight_group):
        pl.semaphore_signal(barrier, inc=1, device_id=weight_peer(step)[1], device_id_type=MESH_IDS)
    pl.semaphore_wait(barrier, row_group - 1 + weight_group - 1)

    own = [
        pltpu.make_async_copy(normed_ref, normed_out.at[row_rank], own_sems.at[0]),
        pltpu.make_async_copy(weight_ref, weight_out.at[weight_rank], own_sems.at[1]),
        pltpu.make_async_copy(ids_ref, ids_out.at[row_rank], own_sems.at[2]),
    ]
    for copy in own:
        copy.start()

    sends = []

    def send_row(source_z, device, sem_index, from_input):
        slot = source_z * c_count + c_index
        copy = pltpu.make_async_remote_copy(
            src_ref=normed_ref if from_input else normed_out.at[slot],
            dst_ref=normed_out.at[slot],
            send_sem=row_send.at[sem_index], recv_sem=row_recv.at[slot],
            device_id=device, device_id_type=MESH_IDS,
        )
        copy.start()
        sends.append(copy)

    def wait_row(source_z, source_core):
        slot = source_z * c_count + source_core
        pltpu.make_async_remote_copy(
            src_ref=normed_ref, dst_ref=normed_out.at[slot],
            send_sem=row_send.at[0], recv_sem=row_recv.at[slot],
            device_id=(x_index, y_index, z_index, other_core), device_id_type=MESH_IDS,
        ).wait_recv()

    right = (x_index, y_index, ring_z(1), c_index)
    left = (x_index, y_index, ring_z(-1), c_index)
    partner = (x_index, y_index, z_index, other_core)
    right_steps = z_count // 2
    left_steps = z_count - 1 - right_steps
    sem_count = [0]

    def next_sem():
        sem_count[0] += 1
        return sem_count[0] - 1

    send_row(z_index, right, next_sem(), True)
    if left_steps > 0:
        send_row(z_index, left, next_sem(), True)
    send_row(z_index, partner, next_sem(), True)

    for step in range(1, weight_group):
        _, device = weight_peer(step)
        copy = pltpu.make_async_remote_copy(
            src_ref=weight_ref, dst_ref=weight_out.at[weight_rank],
            send_sem=weight_send.at[step - 1], recv_sem=weight_recv.at[weight_rank],
            device_id=device, device_id_type=MESH_IDS,
        )
        copy.start()
        sends.append(copy)
    for step in range(1, row_group):
        copy = pltpu.make_async_remote_copy(
            src_ref=ids_ref, dst_ref=ids_out.at[row_rank],
            send_sem=id_send.at[step - 1], recv_sem=id_recv.at[row_rank],
            device_id=row_peer(step), device_id_type=MESH_IDS,
        )
        copy.start()
        sends.append(copy)

    for step in range(1, right_steps + 1):
        from_left = ring_z(-step)
        wait_row(from_left, c_index)
        if step < right_steps:
            send_row(from_left, right, next_sem(), False)
        send_row(from_left, partner, next_sem(), False)
        if step <= left_steps:
            from_right = ring_z(step)
            wait_row(from_right, c_index)
            if step < left_steps:
                send_row(from_right, left, next_sem(), False)
            send_row(from_right, partner, next_sem(), False)

    for copy in own:
        copy.wait()
    for step in range(z_count):
        wait_row(lax.rem(z_index + step, z_count), other_core)
    for step in range(1, weight_group):
        source = lax.rem(weight_rank + weight_group - step, weight_group)
        pltpu.make_async_remote_copy(
            src_ref=weight_ref, dst_ref=weight_out.at[source],
            send_sem=weight_send.at[0], recv_sem=weight_recv.at[source],
            device_id=weight_peer(step)[1], device_id_type=MESH_IDS,
        ).wait_recv()
    for step in range(1, row_group):
        source = lax.rem(row_rank + row_group - step, row_group)
        pltpu.make_async_remote_copy(
            src_ref=ids_ref, dst_ref=ids_out.at[source],
            send_sem=id_send.at[0], recv_sem=id_recv.at[source],
            device_id=row_peer(step), device_id_type=MESH_IDS,
        ).wait_recv()
    for copy in sends:
        copy.wait_send()


def gather_groups(normed, weight, ids, row_group, weight_group):
    any_spec = pl.BlockSpec(memory_space=pl.ANY)
    return pl.pallas_call(
        gather_kernel,
        out_shape=(
            jax.ShapeDtypeStruct((row_group,) + normed.shape, normed.dtype),
            jax.ShapeDtypeStruct((weight_group,) + weight.shape, weight.dtype),
            jax.ShapeDtypeStruct((row_group,) + ids.shape, ids.dtype),
        ),
        in_specs=[any_spec] * 3,
        out_specs=(any_spec, any_spec, any_spec),
        scratch_shapes=[
            pltpu.SemaphoreType.DMA((row_group - 1,)),
            pltpu.SemaphoreType.DMA((row_group,)),
            pltpu.SemaphoreType.DMA((weight_group - 1,)),
            pltpu.SemaphoreType.DMA((weight_group,)),
            pltpu.SemaphoreType.DMA((row_group - 1,)),
            pltpu.SemaphoreType.DMA((row_group,)),
            pltpu.SemaphoreType.DMA((3,)),
        ],
        compiler_params=pltpu.CompilerParams(collective_id=0, has_side_effects=True),
    )(normed, weight, ids)


def stats_kernel(stats_ref, parts_out, merged, first_send, first_recv, second_send, second_recv, own_sems):
    x_count = lax.axis_size("x")
    z_count = lax.axis_size("z")
    c_count = lax.axis_size("c")
    x_index = lax.axis_index("x")
    y_index = lax.axis_index("y")
    z_index = lax.axis_index("z")
    c_index = lax.axis_index("c")
    group = z_count * c_count
    rank = z_index * c_count + c_index

    def row_peer(step):
        member = lax.rem(rank + step, group)
        return member, (x_index, y_index, member // c_count, member % c_count)

    def x_peer(step):
        return (lax.rem(x_index + step, x_count), y_index, z_index, c_index)

    barrier = pltpu.get_barrier_semaphore()

    def greet(step, carry):
        pl.semaphore_signal(barrier, inc=1, device_id=row_peer(step)[1], device_id_type=MESH_IDS)
        return carry

    lax.fori_loop(1, group, greet, 0)
    for step in range(1, x_count):
        pl.semaphore_signal(barrier, inc=1, device_id=x_peer(step), device_id_type=MESH_IDS)
    pl.semaphore_wait(barrier, group - 1 + x_count - 1)

    own = pltpu.make_async_copy(stats_ref.at[rank], merged.at[rank], own_sems.at[0])
    own.start()

    def first_copy(step):
        member, device = row_peer(step)
        return pltpu.make_async_remote_copy(
            src_ref=stats_ref.at[member], dst_ref=merged.at[rank],
            send_sem=first_send.at[step - 1], recv_sem=first_recv.at[rank],
            device_id=device, device_id_type=MESH_IDS,
        )

    def start(step, carry):
        first_copy(step).start()
        return carry

    lax.fori_loop(1, group, start, 0)
    own.wait()

    def finish(step, carry):
        first_copy(step).wait_send()
        source = lax.rem(rank + group - step, group)
        pltpu.make_async_remote_copy(
            src_ref=stats_ref.at[source], dst_ref=merged.at[source],
            send_sem=first_send.at[step - 1], recv_sem=first_recv.at[source],
            device_id=row_peer(step)[1], device_id_type=MESH_IDS,
        ).wait_recv()
        return carry

    lax.fori_loop(1, group, finish, 0)

    mine = pltpu.make_async_copy(merged, parts_out.at[x_index], own_sems.at[1])
    mine.start()
    copies = []
    for step in range(1, x_count):
        copy = pltpu.make_async_remote_copy(
            src_ref=merged, dst_ref=parts_out.at[x_index],
            send_sem=second_send.at[step - 1], recv_sem=second_recv.at[x_index],
            device_id=x_peer(step), device_id_type=MESH_IDS,
        )
        copy.start()
        copies.append(copy)
    mine.wait()
    for step in range(1, x_count):
        copies[step - 1].wait_send()
        source = lax.rem(x_index + x_count - step, x_count)
        pltpu.make_async_remote_copy(
            src_ref=merged, dst_ref=parts_out.at[source],
            send_sem=second_send.at[step - 1], recv_sem=second_recv.at[source],
            device_id=x_peer(x_count - step), device_id_type=MESH_IDS,
        ).wait_recv()


def exchange_stats(stats, x_count):
    group = stats.shape[0]
    any_spec = pl.BlockSpec(memory_space=pl.ANY)
    return pl.pallas_call(
        stats_kernel,
        out_shape=jax.ShapeDtypeStruct((x_count,) + stats.shape, stats.dtype),
        in_specs=[any_spec],
        out_specs=any_spec,
        scratch_shapes=[
            pltpu.VMEM(stats.shape, stats.dtype),
            pltpu.SemaphoreType.DMA((group - 1,)),
            pltpu.SemaphoreType.DMA((group,)),
            pltpu.SemaphoreType.DMA((x_count - 1,)),
            pltpu.SemaphoreType.DMA((x_count,)),
            pltpu.SemaphoreType.DMA((2,)),
        ],
        compiler_params=pltpu.CompilerParams(collective_id=1, has_side_effects=True),
    )(stats)


def per_device(hidden, norm_gain, head_weight, target_ids, seq_lengths):
    x_count = lax.axis_size("x")
    y_count = lax.axis_size("y")
    z_count = lax.axis_size("z")
    c_count = lax.axis_size("c")
    x_index = lax.axis_index("x")
    y_index = lax.axis_index("y")
    z_index = lax.axis_index("z")
    c_index = lax.axis_index("c")
    vert_count = y_count * z_count * c_count
    vert_index = (y_index * z_count + z_index) * c_count + c_index
    tok_local = hidden.shape[0]
    quarter = tok_local // x_count
    vocab_local = head_weight.shape[1]
    group_count = z_count * c_count

    pieces = hidden.reshape(x_count, quarter, -1)
    gain_rows = jnp.broadcast_to(norm_gain[None, None, :], (x_count, 1, norm_gain.shape[0]))
    pieces = jnp.concatenate([pieces, gain_rows], axis=1)
    rows = lax.all_to_all(pieces, "x", split_axis=0, concat_axis=2, tiled=True)[0]
    gain_full = rows[quarter]
    values = rows[:quarter].astype(jnp.float32)
    squares = jnp.sum(values * values, axis=1, keepdims=True)
    normed = (
        values * lax.rsqrt(squares / D + norm_epsilon) * gain_full.astype(jnp.float32)
    ).astype(jnp.bfloat16)

    group_rows, weight, group_ids = gather_groups(
        normed, head_weight, target_ids.reshape(1, -1), group_count, x_count * y_count
    )
    group_rows = group_rows.reshape(-1, D)
    group_ids = lax.dynamic_slice_in_dim(group_ids[:, 0, :], x_index * quarter, quarter, 1).reshape(-1)
    weight = weight.reshape(x_count, y_count, D // x_count, vocab_local)
    logits = jnp.einsum(
        "txd,xyde->tye",
        group_rows.reshape(-1, x_count, D // x_count),
        weight,
        preferred_element_type=jnp.float32,
    )
    block_of = (lax.broadcasted_iota(jnp.int32, (1, y_count, vocab_local), 1) * z_count + z_index) * c_count + c_index
    column_ids = block_of * vocab_local + lax.broadcasted_iota(jnp.int32, (1, y_count, vocab_local), 2)
    row_peak = jnp.max(logits, axis=(1, 2))
    scaled = jnp.exp(logits - row_peak[:, None, None])
    row_sum = jnp.sum(scaled, axis=(1, 2))
    row_weighted = jnp.sum(scaled * logits, axis=(1, 2))
    row_picked = jnp.sum(jnp.where(column_ids == group_ids[:, None, None], logits, 0.0), axis=(1, 2))
    stats = jnp.stack([row_peak, row_sum, row_weighted, row_picked]).reshape(4, group_count, quarter)

    parts = exchange_stats(stats.transpose(1, 0, 2), x_count)
    part_peak, part_sum, part_weighted, part_picked = (parts[:, :, k] for k in range(4))
    highest = jnp.max(part_peak, axis=1)
    factor = jnp.exp(part_peak - highest[:, None])
    totals = jnp.sum(part_sum * factor, axis=1)
    weighted = jnp.sum(part_weighted * factor, axis=1)
    picked = jnp.sum(part_picked, axis=1)
    log_norm = highest + jnp.log(totals)
    full_logprob = (picked - log_norm).reshape(-1)
    full_entropy = (log_norm - weighted / totals).reshape(-1)
    positions = vert_index * tok_local + jnp.arange(tok_local, dtype=jnp.int32)
    live_rows = live_mask(positions, seq_lengths, vert_count * tok_local // 2, SHORT)
    return (jnp.where(live_rows, full_logprob, 0.0), jnp.where(live_rows, full_entropy, 0.0))


def solution(mesh):
    wa_count, vert_count = mesh.devices.shape
    y_count = 4
    c_count = 2
    z_count = vert_count // (y_count * c_count)
    fine = Mesh(mesh.devices.reshape(wa_count, y_count, z_count, c_count), ("x",) + VERT)
    in_specs = (P(VERT, "x"), P("x"), P("x", VERT), P(VERT), P())
    out_specs = (P(VERT), P(VERT))
    return jax.shard_map(
        per_device, mesh=fine, in_specs=in_specs, out_specs=out_specs, check_vma=False
    )
```

```python
import jax
import jax.numpy as jnp
from jax import lax
from jax.experimental import pallas as pl
from jax.experimental.pallas import tpu as pltpu
from jax.sharding import Mesh
from jax.sharding import PartitionSpec as P

D = 1024
SHORT = 128


norm_epsilon = 1e-06

VERT = ("y", "z", "c")
TOKEN_AXES = ("z", "c")


def live_mask(positions, seq_lengths, long_len, short_len):
    is_long = positions < long_len
    beyond = jnp.maximum(positions - long_len, 0)
    seq_index = jnp.where(is_long, 0, 1 + beyond // short_len)
    offset = jnp.where(is_long, positions, beyond % short_len)
    return offset < jnp.take(seq_lengths, seq_index)


MESH_IDS = pl.DeviceIdType.MESH


def gather_kernel(
    hidden_ref, gain_ref, weight_ref, ids_ref, normed_out, weight_out, ids_out,
    piece_vmem, gain_vmem, normed_vmem, piece_send, piece_recv, gain_send, gain_recv,
    row_send, row_recv, weight_send, weight_recv, id_send, id_recv, own_sems,
):
    x_count = lax.axis_size("x")
    y_count = lax.axis_size("y")
    z_count = lax.axis_size("z")
    c_count = lax.axis_size("c")
    x_index = lax.axis_index("x")
    y_index = lax.axis_index("y")
    z_index = lax.axis_index("z")
    c_index = lax.axis_index("c")
    row_group = z_count * c_count
    weight_group = x_count * y_count
    row_rank = z_index * c_count + c_index
    weight_rank = x_index * y_count + y_index
    other_core = 1 - c_index

    def row_peer(step):
        rank = lax.rem(row_rank + step, row_group)
        return (x_index, y_index, rank // c_count, rank % c_count)

    def weight_peer(step):
        rank = lax.rem(weight_rank + step, weight_group)
        return rank, (rank // y_count, rank % y_count, z_index, c_index)

    def ring_z(shift):
        return lax.rem(z_index + shift + z_count, z_count)

    barrier = pltpu.get_barrier_semaphore()
    for step in range(1, row_group):
        pl.semaphore_signal(barrier, inc=1, device_id=row_peer(step), device_id_type=MESH_IDS)
    for step in range(1, weight_group):
        pl.semaphore_signal(barrier, inc=1, device_id=weight_peer(step)[1], device_id_type=MESH_IDS)
    pl.semaphore_wait(barrier, row_group - 1 + weight_group - 1)

    quarter = piece_vmem.shape[1]
    width = piece_vmem.shape[2]

    def x_peer(step):
        return (lax.rem(x_index + step, x_count), y_index, z_index, c_index)

    own_piece = pltpu.make_async_copy(
        hidden_ref.at[pl.ds(x_index * quarter, quarter)], piece_vmem.at[x_index], own_sems.at[3]
    )
    own_gain = pltpu.make_async_copy(gain_ref, gain_vmem.at[x_index], own_sems.at[4])
    own_piece.start()
    own_gain.start()
    piece_copies = []
    for step in range(1, x_count):
        target = lax.rem(x_index + step, x_count)
        for src, dst, send_sem, recv_sem in (
            (hidden_ref.at[pl.ds(target * quarter, quarter)], piece_vmem, piece_send, piece_recv),
            (gain_ref, gain_vmem, gain_send, gain_recv),
        ):
            copy = pltpu.make_async_remote_copy(
                src_ref=src, dst_ref=dst.at[x_index],
                send_sem=send_sem.at[step - 1], recv_sem=recv_sem.at[x_index],
                device_id=x_peer(step), device_id_type=MESH_IDS,
            )
            copy.start()
            piece_copies.append(copy)

    own = [
        pltpu.make_async_copy(weight_ref, weight_out.at[weight_rank], own_sems.at[1]),
        pltpu.make_async_copy(ids_ref, ids_out.at[row_rank], own_sems.at[2]),
    ]
    for copy in own:
        copy.start()

    sends = []

    def send_row(source_z, device, sem_index, from_input):
        slot = source_z * c_count + c_index
        copy = pltpu.make_async_remote_copy(
            src_ref=normed_out.at[slot],
            dst_ref=normed_out.at[slot],
            send_sem=row_send.at[sem_index], recv_sem=row_recv.at[slot],
            device_id=device, device_id_type=MESH_IDS,
        )
        copy.start()
        sends.append(copy)

    def wait_row(source_z, source_core):
        slot = source_z * c_count + source_core
        pltpu.make_async_remote_copy(
            src_ref=normed_out.at[slot], dst_ref=normed_out.at[slot],
            send_sem=row_send.at[0], recv_sem=row_recv.at[slot],
            device_id=(x_index, y_index, z_index, other_core), device_id_type=MESH_IDS,
        ).wait_recv()

    right = (x_index, y_index, ring_z(1), c_index)
    left = (x_index, y_index, ring_z(-1), c_index)
    partner = (x_index, y_index, z_index, other_core)
    right_steps = z_count // 2
    left_steps = z_count - 1 - right_steps
    sem_count = [0]

    def next_sem():
        sem_count[0] += 1
        return sem_count[0] - 1

    for step in range(1, weight_group):
        _, device = weight_peer(step)
        copy = pltpu.make_async_remote_copy(
            src_ref=weight_ref, dst_ref=weight_out.at[weight_rank],
            send_sem=weight_send.at[step - 1], recv_sem=weight_recv.at[weight_rank],
            device_id=device, device_id_type=MESH_IDS,
        )
        copy.start()
        sends.append(copy)
    for step in range(1, row_group):
        copy = pltpu.make_async_remote_copy(
            src_ref=ids_ref, dst_ref=ids_out.at[row_rank],
            send_sem=id_send.at[step - 1], recv_sem=id_recv.at[row_rank],
            device_id=row_peer(step), device_id_type=MESH_IDS,
        )
        copy.start()
        sends.append(copy)

    own_piece.wait()
    own_gain.wait()
    for step in range(1, x_count):
        source = lax.rem(x_index + x_count - step, x_count)
        for src, dst, send_sem, recv_sem in (
            (hidden_ref.at[pl.ds(0, quarter)], piece_vmem, piece_send, piece_recv),
            (gain_ref, gain_vmem, gain_send, gain_recv),
        ):
            pltpu.make_async_remote_copy(
                src_ref=src, dst_ref=dst.at[source],
                send_sem=send_sem.at[step - 1], recv_sem=recv_sem.at[source],
                device_id=x_peer(x_count - step), device_id_type=MESH_IDS,
            ).wait_recv()
    squares = jnp.zeros((quarter, 1), jnp.float32)
    for part in range(x_count):
        values = piece_vmem[part].astype(jnp.float32)
        squares = squares + jnp.sum(values * values, axis=1, keepdims=True)
    scale = lax.rsqrt(squares / (x_count * width) + norm_epsilon)
    for part in range(x_count):
        values = piece_vmem[part].astype(jnp.float32)
        gain = gain_vmem[part].astype(jnp.float32)
        normed_vmem[:, part * width:(part + 1) * width] = (values * scale * gain).astype(normed_vmem.dtype)
    own_row = pltpu.make_async_copy(normed_vmem, normed_out.at[row_rank], own_sems.at[0])
    own_row.start()
    own_row.wait()

    send_row(z_index, right, next_sem(), True)
    if left_steps > 0:
        send_row(z_index, left, next_sem(), True)
    send_row(z_index, partner, next_sem(), True)

    for step in range(1, right_steps + 1):
        from_left = ring_z(-step)
        wait_row(from_left, c_index)
        if step < right_steps:
            send_row(from_left, right, next_sem(), False)
        send_row(from_left, partner, next_sem(), False)
        if step <= left_steps:
            from_right = ring_z(step)
            wait_row(from_right, c_index)
            if step < left_steps:
                send_row(from_right, left, next_sem(), False)
            send_row(from_right, partner, next_sem(), False)

    for copy in own:
        copy.wait()
    for step in range(z_count):
        wait_row(lax.rem(z_index + step, z_count), other_core)
    for step in range(1, weight_group):
        source = lax.rem(weight_rank + weight_group - step, weight_group)
        pltpu.make_async_remote_copy(
            src_ref=weight_ref, dst_ref=weight_out.at[source],
            send_sem=weight_send.at[0], recv_sem=weight_recv.at[source],
            device_id=weight_peer(step)[1], device_id_type=MESH_IDS,
        ).wait_recv()
    for step in range(1, row_group):
        source = lax.rem(row_rank + row_group - step, row_group)
        pltpu.make_async_remote_copy(
            src_ref=ids_ref, dst_ref=ids_out.at[source],
            send_sem=id_send.at[0], recv_sem=id_recv.at[source],
            device_id=row_peer(step), device_id_type=MESH_IDS,
        ).wait_recv()
    for copy in sends + piece_copies:
        copy.wait_send()


def gather_groups(hidden, gain, weight, ids, x_count, row_group, weight_group):
    quarter = hidden.shape[0] // x_count
    width = hidden.shape[1]
    any_spec = pl.BlockSpec(memory_space=pl.ANY)
    return pl.pallas_call(
        gather_kernel,
        out_shape=(
            jax.ShapeDtypeStruct((row_group, quarter, x_count * width), hidden.dtype),
            jax.ShapeDtypeStruct((weight_group,) + weight.shape, weight.dtype),
            jax.ShapeDtypeStruct((row_group,) + ids.shape, ids.dtype),
        ),
        in_specs=[any_spec] * 4,
        out_specs=(any_spec, any_spec, any_spec),
        scratch_shapes=[
            pltpu.VMEM((x_count, quarter, width), hidden.dtype),
            pltpu.VMEM((x_count,) + gain.shape, gain.dtype),
            pltpu.VMEM((quarter, x_count * width), hidden.dtype),
            pltpu.SemaphoreType.DMA((x_count - 1,)),
            pltpu.SemaphoreType.DMA((x_count,)),
            pltpu.SemaphoreType.DMA((x_count - 1,)),
            pltpu.SemaphoreType.DMA((x_count,)),
            pltpu.SemaphoreType.DMA((row_group - 1,)),
            pltpu.SemaphoreType.DMA((row_group,)),
            pltpu.SemaphoreType.DMA((weight_group - 1,)),
            pltpu.SemaphoreType.DMA((weight_group,)),
            pltpu.SemaphoreType.DMA((row_group - 1,)),
            pltpu.SemaphoreType.DMA((row_group,)),
            pltpu.SemaphoreType.DMA((5,)),
        ],
        compiler_params=pltpu.CompilerParams(collective_id=0, has_side_effects=True),
    )(hidden, gain, weight, ids)


def stats_kernel(stats_ref, parts_out, merged, first_send, first_recv, second_send, second_recv, own_sems):
    x_count = lax.axis_size("x")
    z_count = lax.axis_size("z")
    c_count = lax.axis_size("c")
    x_index = lax.axis_index("x")
    y_index = lax.axis_index("y")
    z_index = lax.axis_index("z")
    c_index = lax.axis_index("c")
    group = z_count * c_count
    rank = z_index * c_count + c_index

    def row_peer(step):
        member = lax.rem(rank + step, group)
        return member, (x_index, y_index, member // c_count, member % c_count)

    def x_peer(step):
        return (lax.rem(x_index + step, x_count), y_index, z_index, c_index)

    barrier = pltpu.get_barrier_semaphore()

    def greet(step, carry):
        pl.semaphore_signal(barrier, inc=1, device_id=row_peer(step)[1], device_id_type=MESH_IDS)
        return carry

    lax.fori_loop(1, group, greet, 0)
    for step in range(1, x_count):
        pl.semaphore_signal(barrier, inc=1, device_id=x_peer(step), device_id_type=MESH_IDS)
    pl.semaphore_wait(barrier, group - 1 + x_count - 1)

    own = pltpu.make_async_copy(stats_ref.at[rank], merged.at[rank], own_sems.at[0])
    own.start()

    def first_copy(step):
        member, device = row_peer(step)
        return pltpu.make_async_remote_copy(
            src_ref=stats_ref.at[member], dst_ref=merged.at[rank],
            send_sem=first_send.at[step - 1], recv_sem=first_recv.at[rank],
            device_id=device, device_id_type=MESH_IDS,
        )

    def start(step, carry):
        first_copy(step).start()
        return carry

    lax.fori_loop(1, group, start, 0)
    own.wait()

    def finish(step, carry):
        first_copy(step).wait_send()
        source = lax.rem(rank + group - step, group)
        pltpu.make_async_remote_copy(
            src_ref=stats_ref.at[source], dst_ref=merged.at[source],
            send_sem=first_send.at[step - 1], recv_sem=first_recv.at[source],
            device_id=row_peer(step)[1], device_id_type=MESH_IDS,
        ).wait_recv()
        return carry

    lax.fori_loop(1, group, finish, 0)

    mine = pltpu.make_async_copy(merged, parts_out.at[x_index], own_sems.at[1])
    mine.start()
    copies = []
    for step in range(1, x_count):
        copy = pltpu.make_async_remote_copy(
            src_ref=merged, dst_ref=parts_out.at[x_index],
            send_sem=second_send.at[step - 1], recv_sem=second_recv.at[x_index],
            device_id=x_peer(step), device_id_type=MESH_IDS,
        )
        copy.start()
        copies.append(copy)
    mine.wait()
    for step in range(1, x_count):
        copies[step - 1].wait_send()
        source = lax.rem(x_index + x_count - step, x_count)
        pltpu.make_async_remote_copy(
            src_ref=merged, dst_ref=parts_out.at[source],
            send_sem=second_send.at[step - 1], recv_sem=second_recv.at[source],
            device_id=x_peer(x_count - step), device_id_type=MESH_IDS,
        ).wait_recv()


def exchange_stats(stats, x_count):
    group = stats.shape[0]
    any_spec = pl.BlockSpec(memory_space=pl.ANY)
    return pl.pallas_call(
        stats_kernel,
        out_shape=jax.ShapeDtypeStruct((x_count,) + stats.shape, stats.dtype),
        in_specs=[any_spec],
        out_specs=any_spec,
        scratch_shapes=[
            pltpu.VMEM(stats.shape, stats.dtype),
            pltpu.SemaphoreType.DMA((group - 1,)),
            pltpu.SemaphoreType.DMA((group,)),
            pltpu.SemaphoreType.DMA((x_count - 1,)),
            pltpu.SemaphoreType.DMA((x_count,)),
            pltpu.SemaphoreType.DMA((2,)),
        ],
        compiler_params=pltpu.CompilerParams(collective_id=1, has_side_effects=True),
    )(stats)


def per_device(hidden, norm_gain, head_weight, target_ids, seq_lengths):
    x_count = lax.axis_size("x")
    y_count = lax.axis_size("y")
    z_count = lax.axis_size("z")
    c_count = lax.axis_size("c")
    x_index = lax.axis_index("x")
    y_index = lax.axis_index("y")
    z_index = lax.axis_index("z")
    c_index = lax.axis_index("c")
    vert_count = y_count * z_count * c_count
    vert_index = (y_index * z_count + z_index) * c_count + c_index
    tok_local = hidden.shape[0]
    quarter = tok_local // x_count
    vocab_local = head_weight.shape[1]
    group_count = z_count * c_count

    group_rows, weight, group_ids = gather_groups(
        hidden, norm_gain.reshape(1, -1), head_weight, target_ids.reshape(1, -1),
        x_count, group_count, x_count * y_count,
    )
    group_rows = group_rows.reshape(-1, D)
    group_ids = lax.dynamic_slice_in_dim(group_ids[:, 0, :], x_index * quarter, quarter, 1).reshape(-1)
    weight = weight.reshape(x_count, y_count, D // x_count, vocab_local)
    logits = jnp.einsum(
        "txd,xyde->tye",
        group_rows.reshape(-1, x_count, D // x_count),
        weight,
        preferred_element_type=jnp.float32,
    )
    block_of = (lax.broadcasted_iota(jnp.int32, (1, y_count, vocab_local), 1) * z_count + z_index) * c_count + c_index
    column_ids = block_of * vocab_local + lax.broadcasted_iota(jnp.int32, (1, y_count, vocab_local), 2)
    row_peak = jnp.max(logits, axis=(1, 2))
    scaled = jnp.exp(logits - row_peak[:, None, None])
    row_sum = jnp.sum(scaled, axis=(1, 2))
    row_weighted = jnp.sum(scaled * logits, axis=(1, 2))
    row_picked = jnp.sum(jnp.where(column_ids == group_ids[:, None, None], logits, 0.0), axis=(1, 2))
    stats = jnp.stack([row_peak, row_sum, row_weighted, row_picked]).reshape(4, group_count, quarter)

    parts = exchange_stats(stats.transpose(1, 0, 2), x_count)
    part_peak, part_sum, part_weighted, part_picked = (parts[:, :, k] for k in range(4))
    highest = jnp.max(part_peak, axis=1)
    factor = jnp.exp(part_peak - highest[:, None])
    totals = jnp.sum(part_sum * factor, axis=1)
    weighted = jnp.sum(part_weighted * factor, axis=1)
    picked = jnp.sum(part_picked, axis=1)
    log_norm = highest + jnp.log(totals)
    full_logprob = (picked - log_norm).reshape(-1)
    full_entropy = (log_norm - weighted / totals).reshape(-1)
    positions = vert_index * tok_local + jnp.arange(tok_local, dtype=jnp.int32)
    live_rows = live_mask(positions, seq_lengths, vert_count * tok_local // 2, SHORT)
    return (jnp.where(live_rows, full_logprob, 0.0), jnp.where(live_rows, full_entropy, 0.0))


def solution(mesh):
    wa_count, vert_count = mesh.devices.shape
    y_count = 4
    c_count = 2
    z_count = vert_count // (y_count * c_count)
    fine = Mesh(mesh.devices.reshape(wa_count, y_count, z_count, c_count), ("x",) + VERT)
    in_specs = (P(VERT, "x"), P("x"), P("x", VERT), P(VERT), P())
    out_specs = (P(VERT), P(VERT))
    return jax.shard_map(
        per_device, mesh=fine, in_specs=in_specs, out_specs=out_specs, check_vma=False
    )
```

```python
import functools

import jax
import jax.numpy as jnp
from jax import lax
from jax.experimental import pallas as pl
from jax.experimental.pallas import tpu as pltpu
from jax.sharding import Mesh
from jax.sharding import PartitionSpec as P

D = 1024
SHORT = 128


norm_epsilon = 1e-06

VERT = ("y", "z", "c")
TOKEN_AXES = ("z", "c")


def live_mask(positions, seq_lengths, long_len, short_len):
    is_long = positions < long_len
    beyond = jnp.maximum(positions - long_len, 0)
    seq_index = jnp.where(is_long, 0, 1 + beyond // short_len)
    offset = jnp.where(is_long, positions, beyond % short_len)
    return offset < jnp.take(seq_lengths, seq_index)


MESH_IDS = pl.DeviceIdType.MESH


def gather_kernel(
    hidden_ref, gain_ref, weight_ref, ids_ref, normed_out, weight_out, ids_out,
    piece_vmem, gain_vmem, normed_vmem, piece_send, piece_recv, gain_send, gain_recv,
    row_send, row_recv, weight_send, weight_recv, id_send, id_recv, own_sems,
):
    x_count = lax.axis_size("x")
    y_count = lax.axis_size("y")
    z_count = lax.axis_size("z")
    c_count = lax.axis_size("c")
    x_index = lax.axis_index("x")
    y_index = lax.axis_index("y")
    z_index = lax.axis_index("z")
    c_index = lax.axis_index("c")
    row_group = z_count * c_count
    weight_group = x_count * y_count
    row_rank = z_index * c_count + c_index
    weight_rank = x_index * y_count + y_index
    other_core = 1 - c_index

    def row_peer(step):
        rank = lax.rem(row_rank + step, row_group)
        return (x_index, y_index, rank // c_count, rank % c_count)

    def weight_peer(step):
        rank = lax.rem(weight_rank + step, weight_group)
        return rank, (rank // y_count, rank % y_count, z_index, c_index)

    def ring_z(shift):
        return lax.rem(z_index + shift + z_count, z_count)

    barrier = pltpu.get_barrier_semaphore()
    for step in range(1, row_group):
        pl.semaphore_signal(barrier, inc=1, device_id=row_peer(step), device_id_type=MESH_IDS)
    for step in range(1, weight_group):
        pl.semaphore_signal(barrier, inc=1, device_id=weight_peer(step)[1], device_id_type=MESH_IDS)
    pl.semaphore_wait(barrier, row_group - 1 + weight_group - 1)

    quarter = piece_vmem.shape[1]
    width = piece_vmem.shape[2]

    def x_peer(step):
        return (lax.rem(x_index + step, x_count), y_index, z_index, c_index)

    own_piece = pltpu.make_async_copy(
        hidden_ref.at[pl.ds(x_index * quarter, quarter)], piece_vmem.at[x_index], own_sems.at[3]
    )
    own_gain = pltpu.make_async_copy(gain_ref, gain_vmem.at[x_index], own_sems.at[4])
    own_piece.start()
    own_gain.start()
    piece_copies = []
    for step in range(1, x_count):
        target = lax.rem(x_index + step, x_count)
        for src, dst, send_sem, recv_sem in (
            (hidden_ref.at[pl.ds(target * quarter, quarter)], piece_vmem, piece_send, piece_recv),
            (gain_ref, gain_vmem, gain_send, gain_recv),
        ):
            copy = pltpu.make_async_remote_copy(
                src_ref=src, dst_ref=dst.at[x_index],
                send_sem=send_sem.at[step - 1], recv_sem=recv_sem.at[x_index],
                device_id=x_peer(step), device_id_type=MESH_IDS,
            )
            copy.start()
            piece_copies.append(copy)

    own = [
        pltpu.make_async_copy(weight_ref, weight_out.at[weight_rank], own_sems.at[1]),
        pltpu.make_async_copy(ids_ref, ids_out.at[row_rank], own_sems.at[2]),
    ]
    for copy in own:
        copy.start()

    sends = []

    def send_row(source_z, device, sem_index, from_input):
        slot = source_z * c_count + c_index
        copy = pltpu.make_async_remote_copy(
            src_ref=normed_out.at[slot],
            dst_ref=normed_out.at[slot],
            send_sem=row_send.at[sem_index], recv_sem=row_recv.at[slot],
            device_id=device, device_id_type=MESH_IDS,
        )
        copy.start()
        sends.append(copy)

    def wait_row(source_z, source_core):
        slot = source_z * c_count + source_core
        pltpu.make_async_remote_copy(
            src_ref=normed_out.at[slot], dst_ref=normed_out.at[slot],
            send_sem=row_send.at[0], recv_sem=row_recv.at[slot],
            device_id=(x_index, y_index, z_index, other_core), device_id_type=MESH_IDS,
        ).wait_recv()

    right = (x_index, y_index, ring_z(1), c_index)
    left = (x_index, y_index, ring_z(-1), c_index)
    partner = (x_index, y_index, z_index, other_core)
    right_steps = z_count // 2
    left_steps = z_count - 1 - right_steps
    sem_count = [0]

    def next_sem():
        sem_count[0] += 1
        return sem_count[0] - 1

    for step in range(1, weight_group):
        _, device = weight_peer(step)
        copy = pltpu.make_async_remote_copy(
            src_ref=weight_ref, dst_ref=weight_out.at[weight_rank],
            send_sem=weight_send.at[step - 1], recv_sem=weight_recv.at[weight_rank],
            device_id=device, device_id_type=MESH_IDS,
        )
        copy.start()
        sends.append(copy)
    for step in range(1, row_group):
        copy = pltpu.make_async_remote_copy(
            src_ref=ids_ref, dst_ref=ids_out.at[row_rank],
            send_sem=id_send.at[step - 1], recv_sem=id_recv.at[row_rank],
            device_id=row_peer(step), device_id_type=MESH_IDS,
        )
        copy.start()
        sends.append(copy)

    own_piece.wait()
    own_gain.wait()
    for step in range(1, x_count):
        source = lax.rem(x_index + x_count - step, x_count)
        for src, dst, send_sem, recv_sem in (
            (hidden_ref.at[pl.ds(0, quarter)], piece_vmem, piece_send, piece_recv),
            (gain_ref, gain_vmem, gain_send, gain_recv),
        ):
            pltpu.make_async_remote_copy(
                src_ref=src, dst_ref=dst.at[source],
                send_sem=send_sem.at[step - 1], recv_sem=recv_sem.at[source],
                device_id=x_peer(x_count - step), device_id_type=MESH_IDS,
            ).wait_recv()
    squares = jnp.zeros((quarter, 1), jnp.float32)
    for part in range(x_count):
        values = piece_vmem[part].astype(jnp.float32)
        squares = squares + jnp.sum(values * values, axis=1, keepdims=True)
    scale = lax.rsqrt(squares / (x_count * width) + norm_epsilon)
    for part in range(x_count):
        values = piece_vmem[part].astype(jnp.float32)
        gain = gain_vmem[part].astype(jnp.float32)
        normed_vmem[:, part * width:(part + 1) * width] = (values * scale * gain).astype(normed_vmem.dtype)
    own_row = pltpu.make_async_copy(normed_vmem, normed_out.at[row_rank], own_sems.at[0])
    own_row.start()
    own_row.wait()

    send_row(z_index, right, next_sem(), True)
    if left_steps > 0:
        send_row(z_index, left, next_sem(), True)
    send_row(z_index, partner, next_sem(), True)

    for step in range(1, right_steps + 1):
        from_left = ring_z(-step)
        wait_row(from_left, c_index)
        if step < right_steps:
            send_row(from_left, right, next_sem(), False)
        send_row(from_left, partner, next_sem(), False)
        if step <= left_steps:
            from_right = ring_z(step)
            wait_row(from_right, c_index)
            if step < left_steps:
                send_row(from_right, left, next_sem(), False)
            send_row(from_right, partner, next_sem(), False)

    for copy in own:
        copy.wait()
    for step in range(z_count):
        wait_row(lax.rem(z_index + step, z_count), other_core)
    for step in range(1, weight_group):
        source = lax.rem(weight_rank + weight_group - step, weight_group)
        pltpu.make_async_remote_copy(
            src_ref=weight_ref, dst_ref=weight_out.at[source],
            send_sem=weight_send.at[0], recv_sem=weight_recv.at[source],
            device_id=weight_peer(step)[1], device_id_type=MESH_IDS,
        ).wait_recv()
    for step in range(1, row_group):
        source = lax.rem(row_rank + row_group - step, row_group)
        pltpu.make_async_remote_copy(
            src_ref=ids_ref, dst_ref=ids_out.at[source],
            send_sem=id_send.at[0], recv_sem=id_recv.at[source],
            device_id=row_peer(step), device_id_type=MESH_IDS,
        ).wait_recv()
    for copy in sends + piece_copies:
        copy.wait_send()


def gather_groups(hidden, gain, weight, ids, x_count, row_group, weight_group):
    quarter = hidden.shape[0] // x_count
    width = hidden.shape[1]
    any_spec = pl.BlockSpec(memory_space=pl.ANY)
    return pl.pallas_call(
        gather_kernel,
        out_shape=(
            jax.ShapeDtypeStruct((row_group, quarter, x_count * width), hidden.dtype),
            jax.ShapeDtypeStruct((weight_group,) + weight.shape, weight.dtype),
            jax.ShapeDtypeStruct((row_group,) + ids.shape, ids.dtype),
        ),
        in_specs=[any_spec] * 4,
        out_specs=(any_spec, any_spec, any_spec),
        scratch_shapes=[
            pltpu.VMEM((x_count, quarter, width), hidden.dtype),
            pltpu.VMEM((x_count,) + gain.shape, gain.dtype),
            pltpu.VMEM((quarter, x_count * width), hidden.dtype),
            pltpu.SemaphoreType.DMA((x_count - 1,)),
            pltpu.SemaphoreType.DMA((x_count,)),
            pltpu.SemaphoreType.DMA((x_count - 1,)),
            pltpu.SemaphoreType.DMA((x_count,)),
            pltpu.SemaphoreType.DMA((row_group - 1,)),
            pltpu.SemaphoreType.DMA((row_group,)),
            pltpu.SemaphoreType.DMA((weight_group - 1,)),
            pltpu.SemaphoreType.DMA((weight_group,)),
            pltpu.SemaphoreType.DMA((row_group - 1,)),
            pltpu.SemaphoreType.DMA((row_group,)),
            pltpu.SemaphoreType.DMA((5,)),
        ],
        compiler_params=pltpu.CompilerParams(collective_id=0, has_side_effects=True),
    )(hidden, gain, weight, ids)


def stats_kernel(
    vocab_local, rows_hbm, weight_hbm, local_ids, results_out,
    rows_vmem, weight_vmem, spread, merged, result, first_send, first_recv,
    second_send, second_recv, own_sems,
):
    x_count = lax.axis_size("x")
    y_count = lax.axis_size("y")
    z_count = lax.axis_size("z")
    c_count = lax.axis_size("c")
    x_index = lax.axis_index("x")
    y_index = lax.axis_index("y")
    z_index = lax.axis_index("z")
    c_index = lax.axis_index("c")
    group = z_count * c_count
    rank = z_index * c_count + c_index
    quarter = spread.shape[2] // 4
    width = weight_vmem.shape[1]
    padded = weight_vmem.shape[2]

    def row_peer(step):
        member = lax.rem(rank + step, group)
        return member, (x_index, y_index, member // c_count, member % c_count)

    def x_peer(step):
        return (lax.rem(x_index + step, x_count), y_index, z_index, c_index)

    barrier = pltpu.get_barrier_semaphore()

    def greet(step, carry):
        pl.semaphore_signal(barrier, inc=1, device_id=row_peer(step)[1], device_id_type=MESH_IDS)
        return carry

    lax.fori_loop(1, group, greet, 0)
    for step in range(1, x_count):
        pl.semaphore_signal(barrier, inc=1, device_id=x_peer(step), device_id_type=MESH_IDS)

    load_rows = pltpu.make_async_copy(rows_hbm, rows_vmem, own_sems.at[0])
    load_weight = pltpu.make_async_copy(weight_hbm, weight_vmem, own_sems.at[1])
    load_rows.start()
    load_weight.start()
    spread[...] = jnp.zeros_like(spread)
    result[...] = jnp.zeros_like(result)
    load_rows.wait()
    load_weight.wait()

    chunk = 256
    slots_per_chunk = chunk // quarter
    column = lax.broadcasted_iota(jnp.int32, (chunk, padded), 1)
    valid = column < vocab_local
    lane = lax.broadcasted_iota(jnp.int32, (chunk, 128), 1)
    for first in range(0, rows_vmem.shape[0], chunk):
        blocks = []
        for y_block in range(y_count):
            total = jnp.zeros((chunk, padded), jnp.float32)
            for x_block in range(x_count):
                total = total + jnp.dot(
                    rows_vmem[first:first + chunk, x_block * width:(x_block + 1) * width],
                    weight_vmem[x_block * y_count + y_block],
                    preferred_element_type=jnp.float32,
                )
            blocks.append(total)
        target = local_ids[first:first + chunk, 0:1]
        peak = None
        for y_block, block in enumerate(blocks):
            block_peak = jnp.max(jnp.where(valid, block, -jnp.inf), axis=1, keepdims=True)
            peak = block_peak if peak is None else jnp.maximum(peak, block_peak)
        row_sum = jnp.zeros((chunk, 1), jnp.float32)
        row_weighted = jnp.zeros((chunk, 1), jnp.float32)
        row_picked = jnp.zeros((chunk, 1), jnp.float32)
        for y_block, block in enumerate(blocks):
            scaled = jnp.where(valid, jnp.exp(block - peak), 0.0)
            row_sum = row_sum + jnp.sum(scaled, axis=1, keepdims=True)
            row_weighted = row_weighted + jnp.sum(scaled * block, axis=1, keepdims=True)
            hit = column + y_block * padded == target
            row_picked = row_picked + jnp.sum(jnp.where(hit, block, 0.0), axis=1, keepdims=True)
        table = jnp.where(
            lane == 0, peak,
            jnp.where(lane == 1, row_sum, jnp.where(lane == 2, row_weighted, jnp.where(lane == 3, row_picked, 0.0))),
        )
        lanes = table.T
        for part in range(slots_per_chunk):
            slot = first // quarter + part
            spread[slot, :, 0:quarter] = lanes[0:8, part * quarter:(part + 1) * quarter]

    pl.semaphore_wait(barrier, group - 1 + x_count - 1)

    own = pltpu.make_async_copy(spread.at[rank], merged.at[rank], own_sems.at[2])
    own.start()

    def first_copy(step):
        member, device = row_peer(step)
        return pltpu.make_async_remote_copy(
            src_ref=spread.at[member], dst_ref=merged.at[rank],
            send_sem=first_send.at[step - 1], recv_sem=first_recv.at[rank],
            device_id=device, device_id_type=MESH_IDS,
        )

    def start(step, carry):
        first_copy(step).start()
        return carry

    lax.fori_loop(1, group, start, 0)
    own.wait()

    def finish(step, carry):
        first_copy(step).wait_send()
        source = lax.rem(rank + group - step, group)
        pltpu.make_async_remote_copy(
            src_ref=spread.at[source], dst_ref=merged.at[source],
            send_sem=first_send.at[step - 1], recv_sem=first_recv.at[source],
            device_id=row_peer(step)[1], device_id_type=MESH_IDS,
        ).wait_recv()
        return carry

    lax.fori_loop(1, group, finish, 0)

    highest = merged[0, 0:1, :]
    for source in range(1, group):
        highest = jnp.maximum(highest, merged[source, 0:1, :])
    totals = jnp.zeros_like(highest)
    weighted = jnp.zeros_like(highest)
    picked = jnp.zeros_like(highest)
    for source in range(group):
        factor = jnp.exp(merged[source, 0:1, :] - highest)
        totals = totals + merged[source, 1:2, :] * factor
        weighted = weighted + merged[source, 2:3, :] * factor
        picked = picked + merged[source, 3:4, :]
    log_norm = highest + jnp.log(totals)
    result[0:1, :] = picked - log_norm
    result[1:2, :] = log_norm - weighted / totals

    mine = pltpu.make_async_copy(result, results_out.at[x_index], own_sems.at[3])
    mine.start()
    copies = []
    for step in range(1, x_count):
        copy = pltpu.make_async_remote_copy(
            src_ref=result, dst_ref=results_out.at[x_index],
            send_sem=second_send.at[step - 1], recv_sem=second_recv.at[x_index],
            device_id=x_peer(step), device_id_type=MESH_IDS,
        )
        copy.start()
        copies.append(copy)
    mine.wait()
    for step in range(1, x_count):
        copies[step - 1].wait_send()
        source = lax.rem(x_index + x_count - step, x_count)
        pltpu.make_async_remote_copy(
            src_ref=result, dst_ref=results_out.at[source],
            send_sem=second_send.at[step - 1], recv_sem=second_recv.at[source],
            device_id=x_peer(x_count - step), device_id_type=MESH_IDS,
        ).wait_recv()


def score_groups(rows, weight, local_ids, x_count, group, vocab_local):
    quarter = rows.shape[0] // group
    any_spec = pl.BlockSpec(memory_space=pl.ANY)
    return pl.pallas_call(
        functools.partial(stats_kernel, vocab_local),
        out_shape=jax.ShapeDtypeStruct((x_count, 8, 128), jnp.float32),
        in_specs=[any_spec, any_spec, pl.BlockSpec(memory_space=pltpu.VMEM)],
        out_specs=any_spec,
        scratch_shapes=[
            pltpu.VMEM(rows.shape, rows.dtype),
            pltpu.VMEM(weight.shape, weight.dtype),
            pltpu.VMEM((group, 8, 128), jnp.float32),
            pltpu.VMEM((group, 8, 128), jnp.float32),
            pltpu.VMEM((8, 128), jnp.float32),
            pltpu.SemaphoreType.DMA((group - 1,)),
            pltpu.SemaphoreType.DMA((group,)),
            pltpu.SemaphoreType.DMA((x_count - 1,)),
            pltpu.SemaphoreType.DMA((x_count,)),
            pltpu.SemaphoreType.DMA((4,)),
        ],
        compiler_params=pltpu.CompilerParams(collective_id=1, has_side_effects=True),
    )(rows, weight, local_ids)


def per_device(hidden, norm_gain, head_weight, target_ids, seq_lengths):
    x_count = lax.axis_size("x")
    y_count = lax.axis_size("y")
    z_count = lax.axis_size("z")
    c_count = lax.axis_size("c")
    x_index = lax.axis_index("x")
    y_index = lax.axis_index("y")
    z_index = lax.axis_index("z")
    c_index = lax.axis_index("c")
    vert_count = y_count * z_count * c_count
    vert_index = (y_index * z_count + z_index) * c_count + c_index
    tok_local = hidden.shape[0]
    quarter = tok_local // x_count
    vocab_local = head_weight.shape[1]
    group_count = z_count * c_count

    padded = 128 * pl.cdiv(vocab_local, 128)
    weight_padded = jnp.pad(head_weight, ((0, 0), (0, padded - vocab_local)))
    group_rows, weight, group_ids = gather_groups(
        hidden, norm_gain.reshape(1, -1), weight_padded, target_ids.reshape(1, -1),
        x_count, group_count, x_count * y_count,
    )
    group_rows = group_rows.reshape(-1, D)
    group_ids = lax.dynamic_slice_in_dim(group_ids[:, 0, :], x_index * quarter, quarter, 1).reshape(-1)
    target_block = group_ids // vocab_local
    in_group = (target_block // c_count) % z_count == z_index
    in_group = in_group & (target_block % c_count == c_index)
    local_column = (target_block // (z_count * c_count)) * padded + group_ids % vocab_local
    local_column = jnp.where(in_group, local_column, -1)
    local_ids = jnp.broadcast_to(local_column[:, None], (local_column.shape[0], 128))
    results = score_groups(group_rows, weight, local_ids, x_count, group_count, vocab_local)
    full_logprob = results[:, 0, :quarter].reshape(-1)
    full_entropy = results[:, 1, :quarter].reshape(-1)
    positions = vert_index * tok_local + jnp.arange(tok_local, dtype=jnp.int32)
    live_rows = live_mask(positions, seq_lengths, vert_count * tok_local // 2, SHORT)
    return (jnp.where(live_rows, full_logprob, 0.0), jnp.where(live_rows, full_entropy, 0.0))


def solution(mesh):
    wa_count, vert_count = mesh.devices.shape
    y_count = 4
    c_count = 2
    z_count = vert_count // (y_count * c_count)
    fine = Mesh(mesh.devices.reshape(wa_count, y_count, z_count, c_count), ("x",) + VERT)
    in_specs = (P(VERT, "x"), P("x"), P("x", VERT), P(VERT), P())
    out_specs = (P(VERT), P(VERT))
    return jax.shard_map(
        per_device, mesh=fine, in_specs=in_specs, out_specs=out_specs, check_vma=False
    )
```

```python
import functools

import jax
import jax.numpy as jnp
from jax import lax
from jax.experimental import pallas as pl
from jax.experimental.pallas import tpu as pltpu
from jax.sharding import Mesh
from jax.sharding import PartitionSpec as P

D = 1024
SHORT = 128


norm_epsilon = 1e-06

VERT = ("y", "z", "c")
TOKEN_AXES = ("z", "c")


def live_mask(positions, seq_lengths, long_len, short_len):
    is_long = positions < long_len
    beyond = jnp.maximum(positions - long_len, 0)
    seq_index = jnp.where(is_long, 0, 1 + beyond // short_len)
    offset = jnp.where(is_long, positions, beyond % short_len)
    return offset < jnp.take(seq_lengths, seq_index)


MESH_IDS = pl.DeviceIdType.MESH


def fused_kernel(
    vocab_local, hidden_ref, gain_ref, weight_ref, ids_ref, results_out,
    normed_out, weight_out, ids_out, piece_vmem, gain_vmem, normed_vmem,
    spread, merged, result, ids_turned,
    piece_send, piece_recv, gain_send, gain_recv,
    row_send, row_recv, weight_send, weight_recv, id_send, id_recv, own_sems,
    first_send, first_recv, second_send, second_recv, stat_sems,
):
    x_count = lax.axis_size("x")
    y_count = lax.axis_size("y")
    z_count = lax.axis_size("z")
    c_count = lax.axis_size("c")
    x_index = lax.axis_index("x")
    y_index = lax.axis_index("y")
    z_index = lax.axis_index("z")
    c_index = lax.axis_index("c")
    row_group = z_count * c_count
    weight_group = x_count * y_count
    row_rank = z_index * c_count + c_index
    weight_rank = x_index * y_count + y_index
    other_core = 1 - c_index

    def row_peer(step):
        rank = lax.rem(row_rank + step, row_group)
        return (x_index, y_index, rank // c_count, rank % c_count)

    def weight_peer(step):
        rank = lax.rem(weight_rank + step, weight_group)
        return rank, (rank // y_count, rank % y_count, z_index, c_index)

    def ring_z(shift):
        return lax.rem(z_index + shift + z_count, z_count)

    barrier = pltpu.get_barrier_semaphore()
    for step in range(1, row_group):
        pl.semaphore_signal(barrier, inc=1, device_id=row_peer(step), device_id_type=MESH_IDS)
    for step in range(1, weight_group):
        pl.semaphore_signal(barrier, inc=1, device_id=weight_peer(step)[1], device_id_type=MESH_IDS)
    pl.semaphore_wait(barrier, row_group - 1 + weight_group - 1)

    quarter = piece_vmem.shape[1]
    width = piece_vmem.shape[2]

    def x_peer(step):
        return (lax.rem(x_index + step, x_count), y_index, z_index, c_index)

    own_piece = pltpu.make_async_copy(
        hidden_ref.at[pl.ds(x_index * quarter, quarter)], piece_vmem.at[x_index], own_sems.at[3]
    )
    own_gain = pltpu.make_async_copy(gain_ref, gain_vmem.at[x_index], own_sems.at[4])
    own_piece.start()
    own_gain.start()
    piece_copies = []
    for step in range(1, x_count):
        target = lax.rem(x_index + step, x_count)
        for src, dst, send_sem, recv_sem in (
            (hidden_ref.at[pl.ds(target * quarter, quarter)], piece_vmem, piece_send, piece_recv),
            (gain_ref, gain_vmem, gain_send, gain_recv),
        ):
            copy = pltpu.make_async_remote_copy(
                src_ref=src, dst_ref=dst.at[x_index],
                send_sem=send_sem.at[step - 1], recv_sem=recv_sem.at[x_index],
                device_id=x_peer(step), device_id_type=MESH_IDS,
            )
            copy.start()
            piece_copies.append(copy)

    own = [
        pltpu.make_async_copy(weight_ref, weight_out.at[weight_rank], own_sems.at[1]),
        pltpu.make_async_copy(ids_ref, ids_out.at[row_rank], own_sems.at[2]),
    ]
    for copy in own:
        copy.start()

    sends = []

    def send_row(source_z, device, sem_index, from_input):
        slot = source_z * c_count + c_index
        copy = pltpu.make_async_remote_copy(
            src_ref=normed_out.at[slot],
            dst_ref=normed_out.at[slot],
            send_sem=row_send.at[sem_index], recv_sem=row_recv.at[slot],
            device_id=device, device_id_type=MESH_IDS,
        )
        copy.start()
        sends.append(copy)

    def wait_row(source_z, source_core):
        slot = source_z * c_count + source_core
        pltpu.make_async_remote_copy(
            src_ref=normed_out.at[slot], dst_ref=normed_out.at[slot],
            send_sem=row_send.at[0], recv_sem=row_recv.at[slot],
            device_id=(x_index, y_index, z_index, other_core), device_id_type=MESH_IDS,
        ).wait_recv()

    right = (x_index, y_index, ring_z(1), c_index)
    left = (x_index, y_index, ring_z(-1), c_index)
    partner = (x_index, y_index, z_index, other_core)
    right_steps = z_count // 2
    left_steps = z_count - 1 - right_steps
    sem_count = [0]

    def next_sem():
        sem_count[0] += 1
        return sem_count[0] - 1

    for step in range(1, weight_group):
        _, device = weight_peer(step)
        copy = pltpu.make_async_remote_copy(
            src_ref=weight_ref, dst_ref=weight_out.at[weight_rank],
            send_sem=weight_send.at[step - 1], recv_sem=weight_recv.at[weight_rank],
            device_id=device, device_id_type=MESH_IDS,
        )
        copy.start()
        sends.append(copy)
    for step in range(1, row_group):
        copy = pltpu.make_async_remote_copy(
            src_ref=ids_ref, dst_ref=ids_out.at[row_rank],
            send_sem=id_send.at[step - 1], recv_sem=id_recv.at[row_rank],
            device_id=row_peer(step), device_id_type=MESH_IDS,
        )
        copy.start()
        sends.append(copy)

    own_piece.wait()
    own_gain.wait()
    for step in range(1, x_count):
        source = lax.rem(x_index + x_count - step, x_count)
        for src, dst, send_sem, recv_sem in (
            (hidden_ref.at[pl.ds(0, quarter)], piece_vmem, piece_send, piece_recv),
            (gain_ref, gain_vmem, gain_send, gain_recv),
        ):
            pltpu.make_async_remote_copy(
                src_ref=src, dst_ref=dst.at[source],
                send_sem=send_sem.at[step - 1], recv_sem=recv_sem.at[source],
                device_id=x_peer(x_count - step), device_id_type=MESH_IDS,
            ).wait_recv()
    squares = jnp.zeros((quarter, 1), jnp.float32)
    for part in range(x_count):
        values = piece_vmem[part].astype(jnp.float32)
        squares = squares + jnp.sum(values * values, axis=1, keepdims=True)
    scale = lax.rsqrt(squares / (x_count * width) + norm_epsilon)
    for part in range(x_count):
        values = piece_vmem[part].astype(jnp.float32)
        gain = gain_vmem[part].astype(jnp.float32)
        normed_vmem[:, part * width:(part + 1) * width] = (values * scale * gain).astype(normed_vmem.dtype)
    own_row = pltpu.make_async_copy(normed_vmem, normed_out.at[row_rank], own_sems.at[0])
    own_row.start()
    own_row.wait()

    send_row(z_index, right, next_sem(), True)
    if left_steps > 0:
        send_row(z_index, left, next_sem(), True)
    send_row(z_index, partner, next_sem(), True)

    for step in range(1, right_steps + 1):
        from_left = ring_z(-step)
        wait_row(from_left, c_index)
        if step < right_steps:
            send_row(from_left, right, next_sem(), False)
        send_row(from_left, partner, next_sem(), False)
        if step <= left_steps:
            from_right = ring_z(step)
            wait_row(from_right, c_index)
            if step < left_steps:
                send_row(from_right, left, next_sem(), False)
            send_row(from_right, partner, next_sem(), False)

    for copy in own:
        copy.wait()
    for step in range(z_count):
        wait_row(lax.rem(z_index + step, z_count), other_core)
    for step in range(1, weight_group):
        source = lax.rem(weight_rank + weight_group - step, weight_group)
        pltpu.make_async_remote_copy(
            src_ref=weight_ref, dst_ref=weight_out.at[source],
            send_sem=weight_send.at[0], recv_sem=weight_recv.at[source],
            device_id=weight_peer(step)[1], device_id_type=MESH_IDS,
        ).wait_recv()
    for step in range(1, row_group):
        source = lax.rem(row_rank + row_group - step, row_group)
        pltpu.make_async_remote_copy(
            src_ref=ids_ref, dst_ref=ids_out.at[source],
            send_sem=id_send.at[0], recv_sem=id_recv.at[source],
            device_id=row_peer(step), device_id_type=MESH_IDS,
        ).wait_recv()
    for copy in sends + piece_copies:
        copy.wait_send()

    group = row_group
    rank = row_rank
    width = weight_out.shape[1]
    padded = weight_out.shape[2]
    spread[...] = jnp.zeros_like(spread)
    result[...] = jnp.zeros_like(result)

    chunk = 256
    slots_per_chunk = chunk // quarter
    column = lax.broadcasted_iota(jnp.int32, (chunk, padded), 1)
    valid = column < vocab_local
    lane = lax.broadcasted_iota(jnp.int32, (chunk, 128), 1)
    for first in range(0, normed_out.shape[0] * quarter, chunk):
        blocks = []
        for y_block in range(y_count):
            total = jnp.zeros((chunk, padded), jnp.float32)
            for x_block in range(x_count):
                rows = normed_out[first // quarter:(first + chunk) // quarter, :, x_block * width:(x_block + 1) * width]
                total = total + jnp.dot(
                    rows.reshape(chunk, width),
                    weight_out[x_block * y_count + y_block],
                    preferred_element_type=jnp.float32,
                )
            blocks.append(total)
        id_rows = jnp.concatenate(
            [ids_out[slot] for slot in range(first // quarter, first // quarter + slots_per_chunk)], axis=0
        )
        ids_turned[...] = id_rows.astype(jnp.float32).T
        mine = ids_turned[pl.ds(pl.multiple_of(x_index * quarter, quarter), quarter), :]
        target = jnp.concatenate(
            [mine[:, part:part + 1] for part in range(slots_per_chunk)], axis=0
        ).astype(jnp.int32)
        peak = None
        for y_block, block in enumerate(blocks):
            block_peak = jnp.max(jnp.where(valid, block, -jnp.inf), axis=1, keepdims=True)
            peak = block_peak if peak is None else jnp.maximum(peak, block_peak)
        row_sum = jnp.zeros((chunk, 1), jnp.float32)
        row_weighted = jnp.zeros((chunk, 1), jnp.float32)
        row_picked = jnp.zeros((chunk, 1), jnp.float32)
        for y_block, block in enumerate(blocks):
            scaled = jnp.where(valid, jnp.exp(block - peak), 0.0)
            row_sum = row_sum + jnp.sum(scaled, axis=1, keepdims=True)
            row_weighted = row_weighted + jnp.sum(scaled * block, axis=1, keepdims=True)
            global_id = ((y_block * z_count + z_index) * c_count + c_index) * vocab_local + column
            hit = valid & (global_id == target)
            row_picked = row_picked + jnp.sum(jnp.where(hit, block, 0.0), axis=1, keepdims=True)
        table = jnp.where(
            lane == 0, peak,
            jnp.where(lane == 1, row_sum, jnp.where(lane == 2, row_weighted, jnp.where(lane == 3, row_picked, 0.0))),
        )
        lanes = table.T
        for part in range(slots_per_chunk):
            slot = first // quarter + part
            spread[slot, :, 0:quarter] = lanes[0:8, part * quarter:(part + 1) * quarter]

    own = pltpu.make_async_copy(spread.at[rank], merged.at[rank], stat_sems.at[0])
    own.start()

    def first_copy(step):
        member = lax.rem(rank + step, group)
        device = row_peer(step)
        return pltpu.make_async_remote_copy(
            src_ref=spread.at[member], dst_ref=merged.at[rank],
            send_sem=first_send.at[step - 1], recv_sem=first_recv.at[rank],
            device_id=device, device_id_type=MESH_IDS,
        )

    def start(step, carry):
        first_copy(step).start()
        return carry

    lax.fori_loop(1, group, start, 0)
    own.wait()

    def finish(step, carry):
        first_copy(step).wait_send()
        source = lax.rem(rank + group - step, group)
        pltpu.make_async_remote_copy(
            src_ref=spread.at[source], dst_ref=merged.at[source],
            send_sem=first_send.at[step - 1], recv_sem=first_recv.at[source],
            device_id=row_peer(step), device_id_type=MESH_IDS,
        ).wait_recv()
        return carry

    lax.fori_loop(1, group, finish, 0)

    highest = merged[0, 0:1, :]
    for source in range(1, group):
        highest = jnp.maximum(highest, merged[source, 0:1, :])
    totals = jnp.zeros_like(highest)
    weighted = jnp.zeros_like(highest)
    picked = jnp.zeros_like(highest)
    for source in range(group):
        factor = jnp.exp(merged[source, 0:1, :] - highest)
        totals = totals + merged[source, 1:2, :] * factor
        weighted = weighted + merged[source, 2:3, :] * factor
        picked = picked + merged[source, 3:4, :]
    log_norm = highest + jnp.log(totals)
    result[0:1, :] = picked - log_norm
    result[1:2, :] = log_norm - weighted / totals

    mine = pltpu.make_async_copy(result, results_out.at[x_index], stat_sems.at[1])
    mine.start()
    copies = []
    for step in range(1, x_count):
        copy = pltpu.make_async_remote_copy(
            src_ref=result, dst_ref=results_out.at[x_index],
            send_sem=second_send.at[step - 1], recv_sem=second_recv.at[x_index],
            device_id=x_peer(step), device_id_type=MESH_IDS,
        )
        copy.start()
        copies.append(copy)
    mine.wait()
    for step in range(1, x_count):
        copies[step - 1].wait_send()
        source = lax.rem(x_index + x_count - step, x_count)
        pltpu.make_async_remote_copy(
            src_ref=result, dst_ref=results_out.at[source],
            send_sem=second_send.at[step - 1], recv_sem=second_recv.at[source],
            device_id=x_peer(x_count - step), device_id_type=MESH_IDS,
        ).wait_recv()


def score_all(hidden, gain, weight, ids, x_count, row_group, weight_group, vocab_local):
    quarter = hidden.shape[0] // x_count
    width = hidden.shape[1]
    any_spec = pl.BlockSpec(memory_space=pl.ANY)
    return pl.pallas_call(
        functools.partial(fused_kernel, vocab_local),
        out_shape=jax.ShapeDtypeStruct((x_count, 8, 128), jnp.float32),
        in_specs=[any_spec] * 4,
        out_specs=any_spec,
        scratch_shapes=[
            pltpu.VMEM((row_group, quarter, x_count * width), hidden.dtype),
            pltpu.VMEM((weight_group,) + weight.shape, weight.dtype),
            pltpu.VMEM((row_group,) + ids.shape, ids.dtype),
            pltpu.VMEM((x_count, quarter, width), hidden.dtype),
            pltpu.VMEM((x_count,) + gain.shape, gain.dtype),
            pltpu.VMEM((quarter, x_count * width), hidden.dtype),
            pltpu.VMEM((row_group, 8, 128), jnp.float32),
            pltpu.VMEM((row_group, 8, 128), jnp.float32),
            pltpu.VMEM((8, 128), jnp.float32),
            pltpu.VMEM((ids.shape[1], 8), jnp.float32),
            pltpu.SemaphoreType.DMA((x_count - 1,)),
            pltpu.SemaphoreType.DMA((x_count,)),
            pltpu.SemaphoreType.DMA((x_count - 1,)),
            pltpu.SemaphoreType.DMA((x_count,)),
            pltpu.SemaphoreType.DMA((row_group - 1,)),
            pltpu.SemaphoreType.DMA((row_group,)),
            pltpu.SemaphoreType.DMA((weight_group - 1,)),
            pltpu.SemaphoreType.DMA((weight_group,)),
            pltpu.SemaphoreType.DMA((row_group - 1,)),
            pltpu.SemaphoreType.DMA((row_group,)),
            pltpu.SemaphoreType.DMA((5,)),
            pltpu.SemaphoreType.DMA((row_group - 1,)),
            pltpu.SemaphoreType.DMA((row_group,)),
            pltpu.SemaphoreType.DMA((x_count - 1,)),
            pltpu.SemaphoreType.DMA((x_count,)),
            pltpu.SemaphoreType.DMA((2,)),
        ],
        compiler_params=pltpu.CompilerParams(collective_id=0, has_side_effects=True),
    )(hidden, gain, weight, ids)


def per_device(hidden, norm_gain, head_weight, target_ids, seq_lengths):
    x_count = lax.axis_size("x")
    y_count = lax.axis_size("y")
    z_count = lax.axis_size("z")
    c_count = lax.axis_size("c")
    x_index = lax.axis_index("x")
    y_index = lax.axis_index("y")
    z_index = lax.axis_index("z")
    c_index = lax.axis_index("c")
    vert_count = y_count * z_count * c_count
    vert_index = (y_index * z_count + z_index) * c_count + c_index
    tok_local = hidden.shape[0]
    quarter = tok_local // x_count
    vocab_local = head_weight.shape[1]
    group_count = z_count * c_count

    padded = 128 * pl.cdiv(vocab_local, 128)
    weight_padded = jnp.pad(head_weight, ((0, 0), (0, padded - vocab_local)))
    results = score_all(
        hidden, norm_gain.reshape(1, -1), weight_padded, target_ids.reshape(1, -1),
        x_count, group_count, x_count * y_count, vocab_local,
    )
    full_logprob = results[:, 0, :quarter].reshape(-1)
    full_entropy = results[:, 1, :quarter].reshape(-1)
    positions = vert_index * tok_local + jnp.arange(tok_local, dtype=jnp.int32)
    live_rows = live_mask(positions, seq_lengths, vert_count * tok_local // 2, SHORT)
    return (jnp.where(live_rows, full_logprob, 0.0), jnp.where(live_rows, full_entropy, 0.0))


def solution(mesh):
    wa_count, vert_count = mesh.devices.shape
    y_count = 4
    c_count = 2
    z_count = vert_count // (y_count * c_count)
    fine = Mesh(mesh.devices.reshape(wa_count, y_count, z_count, c_count), ("x",) + VERT)
    in_specs = (P(VERT, "x"), P("x"), P("x", VERT), P(VERT), P())
    out_specs = (P(VERT), P(VERT))
    return jax.shard_map(
        per_device, mesh=fine, in_specs=in_specs, out_specs=out_specs, check_vma=False
    )
```

```python
import functools

import jax
import jax.numpy as jnp
from jax import lax
from jax.experimental import pallas as pl
from jax.experimental.pallas import tpu as pltpu
from jax.sharding import Mesh
from jax.sharding import PartitionSpec as P

D = 1024
SHORT = 128


norm_epsilon = 1e-06

VERT = ("y", "z", "c")
TOKEN_AXES = ("z", "c")


def live_mask(positions, seq_lengths, long_len, short_len):
    is_long = positions < long_len
    beyond = jnp.maximum(positions - long_len, 0)
    seq_index = jnp.where(is_long, 0, 1 + beyond // short_len)
    offset = jnp.where(is_long, positions, beyond % short_len)
    return offset < jnp.take(seq_lengths, seq_index)


MESH_IDS = pl.DeviceIdType.MESH


def fused_kernel(
    vocab_local, hidden_ref, gain_ref, weight_ref, ids_ref, results_out,
    normed_out, weight_out, ids_out, piece_vmem, gain_vmem, normed_vmem,
    spread, merged, result, ids_turned,
    piece_send, piece_recv, gain_send, gain_recv,
    row_send, row_recv, weight_send, weight_recv, id_send, id_recv, own_sems,
    first_send, first_recv, second_send, second_recv, stat_sems,
):
    x_count = lax.axis_size("x")
    y_count = lax.axis_size("y")
    z_count = lax.axis_size("z")
    c_count = lax.axis_size("c")
    x_index = lax.axis_index("x")
    y_index = lax.axis_index("y")
    z_index = lax.axis_index("z")
    c_index = lax.axis_index("c")
    row_group = z_count * c_count
    weight_group = x_count * y_count
    row_rank = z_index * c_count + c_index
    weight_rank = x_index * y_count + y_index
    other_core = 1 - c_index

    def row_peer(step):
        rank = lax.rem(row_rank + step, row_group)
        return (x_index, y_index, rank // c_count, rank % c_count)

    def weight_peer(step):
        rank = lax.rem(weight_rank + step, weight_group)
        return rank, (rank // y_count, rank % y_count, z_index, c_index)

    def ring_z(shift):
        return lax.rem(z_index + shift + z_count, z_count)

    barrier = pltpu.get_barrier_semaphore()
    for step in range(1, row_group):
        pl.semaphore_signal(barrier, inc=1, device_id=row_peer(step), device_id_type=MESH_IDS)
    for step in range(1, weight_group):
        pl.semaphore_signal(barrier, inc=1, device_id=weight_peer(step)[1], device_id_type=MESH_IDS)
    pl.semaphore_wait(barrier, row_group - 1 + weight_group - 1)

    quarter = piece_vmem.shape[1]
    width = piece_vmem.shape[2]

    def x_peer(step):
        return (lax.rem(x_index + step, x_count), y_index, z_index, c_index)

    own_piece = pltpu.make_async_copy(
        hidden_ref.at[pl.ds(x_index * quarter, quarter)], piece_vmem.at[x_index], own_sems.at[3]
    )
    own_gain = pltpu.make_async_copy(gain_ref, gain_vmem.at[x_index], own_sems.at[4])
    own_piece.start()
    own_gain.start()
    piece_copies = []
    for step in range(1, x_count):
        target = lax.rem(x_index + step, x_count)
        for src, dst, send_sem, recv_sem in (
            (hidden_ref.at[pl.ds(target * quarter, quarter)], piece_vmem, piece_send, piece_recv),
            (gain_ref, gain_vmem, gain_send, gain_recv),
        ):
            copy = pltpu.make_async_remote_copy(
                src_ref=src, dst_ref=dst.at[x_index],
                send_sem=send_sem.at[step - 1], recv_sem=recv_sem.at[x_index],
                device_id=x_peer(step), device_id_type=MESH_IDS,
            )
            copy.start()
            piece_copies.append(copy)

    own = [
        pltpu.make_async_copy(weight_ref, weight_out.at[weight_rank], own_sems.at[1]),
        pltpu.make_async_copy(ids_ref, ids_out.at[row_rank], own_sems.at[2]),
    ]
    for copy in own:
        copy.start()

    sends = []

    def send_row(source_z, device, sem_index, from_input):
        slot = source_z * c_count + c_index
        copy = pltpu.make_async_remote_copy(
            src_ref=normed_out.at[slot],
            dst_ref=normed_out.at[slot],
            send_sem=row_send.at[sem_index], recv_sem=row_recv.at[slot],
            device_id=device, device_id_type=MESH_IDS,
        )
        copy.start()
        sends.append(copy)

    def wait_row(source_z, source_core):
        slot = source_z * c_count + source_core
        pltpu.make_async_remote_copy(
            src_ref=normed_out.at[slot], dst_ref=normed_out.at[slot],
            send_sem=row_send.at[0], recv_sem=row_recv.at[slot],
            device_id=(x_index, y_index, z_index, other_core), device_id_type=MESH_IDS,
        ).wait_recv()

    right = (x_index, y_index, ring_z(1), c_index)
    left = (x_index, y_index, ring_z(-1), c_index)
    partner = (x_index, y_index, z_index, other_core)
    right_steps = z_count // 2
    left_steps = z_count - 1 - right_steps
    sem_count = [0]

    def next_sem():
        sem_count[0] += 1
        return sem_count[0] - 1

    for step in range(1, weight_group):
        _, device = weight_peer(step)
        copy = pltpu.make_async_remote_copy(
            src_ref=weight_ref, dst_ref=weight_out.at[weight_rank],
            send_sem=weight_send.at[step - 1], recv_sem=weight_recv.at[weight_rank],
            device_id=device, device_id_type=MESH_IDS,
        )
        copy.start()
        sends.append(copy)
    for step in range(1, row_group):
        copy = pltpu.make_async_remote_copy(
            src_ref=ids_ref, dst_ref=ids_out.at[row_rank],
            send_sem=id_send.at[step - 1], recv_sem=id_recv.at[row_rank],
            device_id=row_peer(step), device_id_type=MESH_IDS,
        )
        copy.start()
        sends.append(copy)

    own_piece.wait()
    own_gain.wait()
    for step in range(1, x_count):
        source = lax.rem(x_index + x_count - step, x_count)
        for src, dst, send_sem, recv_sem in (
            (hidden_ref.at[pl.ds(0, quarter)], piece_vmem, piece_send, piece_recv),
            (gain_ref, gain_vmem, gain_send, gain_recv),
        ):
            pltpu.make_async_remote_copy(
                src_ref=src, dst_ref=dst.at[source],
                send_sem=send_sem.at[step - 1], recv_sem=recv_sem.at[source],
                device_id=x_peer(x_count - step), device_id_type=MESH_IDS,
            ).wait_recv()
    squares = jnp.zeros((quarter, 1), jnp.float32)
    for part in range(x_count):
        values = piece_vmem[part].astype(jnp.float32)
        squares = squares + jnp.sum(values * values, axis=1, keepdims=True)
    scale = lax.rsqrt(squares / (x_count * width) + norm_epsilon)
    for part in range(x_count):
        values = piece_vmem[part].astype(jnp.float32)
        gain = gain_vmem[part].astype(jnp.float32)
        normed_vmem[:, part * width:(part + 1) * width] = (values * scale * gain).astype(normed_vmem.dtype)
    own_row = pltpu.make_async_copy(normed_vmem, normed_out.at[row_rank], own_sems.at[0])
    own_row.start()
    own_row.wait()

    send_row(z_index, right, next_sem(), True)
    if left_steps > 0:
        send_row(z_index, left, next_sem(), True)
    send_row(z_index, partner, next_sem(), True)

    for step in range(1, right_steps + 1):
        from_left = ring_z(-step)
        wait_row(from_left, c_index)
        if step < right_steps:
            send_row(from_left, right, next_sem(), False)
        send_row(from_left, partner, next_sem(), False)
        if step <= left_steps:
            from_right = ring_z(step)
            wait_row(from_right, c_index)
            if step < left_steps:
                send_row(from_right, left, next_sem(), False)
            send_row(from_right, partner, next_sem(), False)

    for copy in own:
        copy.wait()
    for step in range(z_count):
        wait_row(lax.rem(z_index + step, z_count), other_core)
    for step in range(1, weight_group):
        source = lax.rem(weight_rank + weight_group - step, weight_group)
        pltpu.make_async_remote_copy(
            src_ref=weight_ref, dst_ref=weight_out.at[source],
            send_sem=weight_send.at[0], recv_sem=weight_recv.at[source],
            device_id=weight_peer(step)[1], device_id_type=MESH_IDS,
        ).wait_recv()
    for step in range(1, row_group):
        source = lax.rem(row_rank + row_group - step, row_group)
        pltpu.make_async_remote_copy(
            src_ref=ids_ref, dst_ref=ids_out.at[source],
            send_sem=id_send.at[0], recv_sem=id_recv.at[source],
            device_id=row_peer(step), device_id_type=MESH_IDS,
        ).wait_recv()
    for copy in sends + piece_copies:
        copy.wait_send()

    group = row_group
    rank = row_rank
    width = weight_out.shape[1]
    padded = weight_out.shape[2]
    spread[...] = jnp.zeros_like(spread)
    result[...] = jnp.zeros_like(result)

    own_stats = pltpu.make_async_copy(spread.at[rank], merged.at[rank], stat_sems.at[0])

    def stats_copy(slot):
        return pltpu.make_async_remote_copy(
            src_ref=spread.at[slot], dst_ref=merged.at[rank],
            send_sem=first_send.at[slot], recv_sem=first_recv.at[rank],
            device_id=(x_index, y_index, slot // c_count, slot % c_count), device_id_type=MESH_IDS,
        )

    def send_chunk(first_slot):
        for slot in range(first_slot, first_slot + slots_per_chunk):

            @pl.when(slot != rank)
            def _():
                stats_copy(slot).start()

            @pl.when(slot == rank)
            def _():
                own_stats.start()

    chunk = 256
    slots_per_chunk = chunk // quarter
    column = lax.broadcasted_iota(jnp.int32, (chunk, padded), 1)
    valid = column < vocab_local
    lane = lax.broadcasted_iota(jnp.int32, (chunk, 128), 1)
    for first in range(0, normed_out.shape[0] * quarter, chunk):
        blocks = []
        for y_block in range(y_count):
            total = jnp.zeros((chunk, padded), jnp.float32)
            for x_block in range(x_count):
                rows = normed_out[first // quarter:(first + chunk) // quarter, :, x_block * width:(x_block + 1) * width]
                total = total + jnp.dot(
                    rows.reshape(chunk, width),
                    weight_out[x_block * y_count + y_block],
                    preferred_element_type=jnp.float32,
                )
            blocks.append(total)
        id_rows = jnp.concatenate(
            [ids_out[slot] for slot in range(first // quarter, first // quarter + slots_per_chunk)], axis=0
        )
        ids_turned[...] = id_rows.astype(jnp.float32).T
        mine = ids_turned[pl.ds(pl.multiple_of(x_index * quarter, quarter), quarter), :]
        target = jnp.concatenate(
            [mine[:, part:part + 1] for part in range(slots_per_chunk)], axis=0
        ).astype(jnp.int32)
        peak = None
        for y_block, block in enumerate(blocks):
            block_peak = jnp.max(jnp.where(valid, block, -jnp.inf), axis=1, keepdims=True)
            peak = block_peak if peak is None else jnp.maximum(peak, block_peak)
        row_sum = jnp.zeros((chunk, 1), jnp.float32)
        row_weighted = jnp.zeros((chunk, 1), jnp.float32)
        row_picked = jnp.zeros((chunk, 1), jnp.float32)
        for y_block, block in enumerate(blocks):
            scaled = jnp.where(valid, jnp.exp(block - peak), 0.0)
            row_sum = row_sum + jnp.sum(scaled, axis=1, keepdims=True)
            row_weighted = row_weighted + jnp.sum(scaled * block, axis=1, keepdims=True)
            global_id = ((y_block * z_count + z_index) * c_count + c_index) * vocab_local + column
            hit = valid & (global_id == target)
            row_picked = row_picked + jnp.sum(jnp.where(hit, block, 0.0), axis=1, keepdims=True)
        table = jnp.where(
            lane == 0, peak,
            jnp.where(lane == 1, row_sum, jnp.where(lane == 2, row_weighted, jnp.where(lane == 3, row_picked, 0.0))),
        )
        lanes = table.T
        for part in range(slots_per_chunk):
            slot = first // quarter + part
            spread[slot, :, 0:quarter] = lanes[0:8, part * quarter:(part + 1) * quarter]
        if first > 0:
            send_chunk(first // quarter - slots_per_chunk)
    send_chunk(group - slots_per_chunk)

    for slot in range(group):

        @pl.when(slot != rank)
        def _():
            stats_copy(slot).wait_send()

        @pl.when(slot == rank)
        def _():
            own_stats.wait()

    def finish(step, carry):
        source = lax.rem(rank + group - step, group)
        pltpu.make_async_remote_copy(
            src_ref=spread.at[source], dst_ref=merged.at[source],
            send_sem=first_send.at[source], recv_sem=first_recv.at[source],
            device_id=row_peer(step), device_id_type=MESH_IDS,
        ).wait_recv()
        return carry

    lax.fori_loop(1, group, finish, 0)

    highest = merged[0, 0:1, :]
    for source in range(1, group):
        highest = jnp.maximum(highest, merged[source, 0:1, :])
    totals = jnp.zeros_like(highest)
    weighted = jnp.zeros_like(highest)
    picked = jnp.zeros_like(highest)
    for source in range(group):
        factor = jnp.exp(merged[source, 0:1, :] - highest)
        totals = totals + merged[source, 1:2, :] * factor
        weighted = weighted + merged[source, 2:3, :] * factor
        picked = picked + merged[source, 3:4, :]
    log_norm = highest + jnp.log(totals)
    result[0:1, :] = picked - log_norm
    result[1:2, :] = log_norm - weighted / totals

    mine = pltpu.make_async_copy(result, results_out.at[x_index], stat_sems.at[1])
    mine.start()
    copies = []
    for step in range(1, x_count):
        copy = pltpu.make_async_remote_copy(
            src_ref=result, dst_ref=results_out.at[x_index],
            send_sem=second_send.at[step - 1], recv_sem=second_recv.at[x_index],
            device_id=x_peer(step), device_id_type=MESH_IDS,
        )
        copy.start()
        copies.append(copy)
    mine.wait()
    for step in range(1, x_count):
        copies[step - 1].wait_send()
        source = lax.rem(x_index + x_count - step, x_count)
        pltpu.make_async_remote_copy(
            src_ref=result, dst_ref=results_out.at[source],
            send_sem=second_send.at[step - 1], recv_sem=second_recv.at[source],
            device_id=x_peer(x_count - step), device_id_type=MESH_IDS,
        ).wait_recv()


def score_all(hidden, gain, weight, ids, x_count, row_group, weight_group, vocab_local):
    quarter = hidden.shape[0] // x_count
    width = hidden.shape[1]
    any_spec = pl.BlockSpec(memory_space=pl.ANY)
    return pl.pallas_call(
        functools.partial(fused_kernel, vocab_local),
        out_shape=jax.ShapeDtypeStruct((x_count, 8, 128), jnp.float32),
        in_specs=[any_spec] * 4,
        out_specs=any_spec,
        scratch_shapes=[
            pltpu.VMEM((row_group, quarter, x_count * width), hidden.dtype),
            pltpu.VMEM((weight_group,) + weight.shape, weight.dtype),
            pltpu.VMEM((row_group,) + ids.shape, ids.dtype),
            pltpu.VMEM((x_count, quarter, width), hidden.dtype),
            pltpu.VMEM((x_count,) + gain.shape, gain.dtype),
            pltpu.VMEM((quarter, x_count * width), hidden.dtype),
            pltpu.VMEM((row_group, 8, 128), jnp.float32),
            pltpu.VMEM((row_group, 8, 128), jnp.float32),
            pltpu.VMEM((8, 128), jnp.float32),
            pltpu.VMEM((ids.shape[1], 8), jnp.float32),
            pltpu.SemaphoreType.DMA((x_count - 1,)),
            pltpu.SemaphoreType.DMA((x_count,)),
            pltpu.SemaphoreType.DMA((x_count - 1,)),
            pltpu.SemaphoreType.DMA((x_count,)),
            pltpu.SemaphoreType.DMA((row_group - 1,)),
            pltpu.SemaphoreType.DMA((row_group,)),
            pltpu.SemaphoreType.DMA((weight_group - 1,)),
            pltpu.SemaphoreType.DMA((weight_group,)),
            pltpu.SemaphoreType.DMA((row_group - 1,)),
            pltpu.SemaphoreType.DMA((row_group,)),
            pltpu.SemaphoreType.DMA((5,)),
            pltpu.SemaphoreType.DMA((row_group,)),
            pltpu.SemaphoreType.DMA((row_group,)),
            pltpu.SemaphoreType.DMA((x_count - 1,)),
            pltpu.SemaphoreType.DMA((x_count,)),
            pltpu.SemaphoreType.DMA((2,)),
        ],
        compiler_params=pltpu.CompilerParams(collective_id=0, has_side_effects=True),
    )(hidden, gain, weight, ids)


def per_device(hidden, norm_gain, head_weight, target_ids, seq_lengths):
    x_count = lax.axis_size("x")
    y_count = lax.axis_size("y")
    z_count = lax.axis_size("z")
    c_count = lax.axis_size("c")
    x_index = lax.axis_index("x")
    y_index = lax.axis_index("y")
    z_index = lax.axis_index("z")
    c_index = lax.axis_index("c")
    vert_count = y_count * z_count * c_count
    vert_index = (y_index * z_count + z_index) * c_count + c_index
    tok_local = hidden.shape[0]
    quarter = tok_local // x_count
    vocab_local = head_weight.shape[1]
    group_count = z_count * c_count

    padded = 128 * pl.cdiv(vocab_local, 128)
    weight_padded = jnp.pad(head_weight, ((0, 0), (0, padded - vocab_local)))
    results = score_all(
        hidden, norm_gain.reshape(1, -1), weight_padded, target_ids.reshape(1, -1),
        x_count, group_count, x_count * y_count, vocab_local,
    )
    full_logprob = results[:, 0, :quarter].reshape(-1)
    full_entropy = results[:, 1, :quarter].reshape(-1)
    positions = vert_index * tok_local + jnp.arange(tok_local, dtype=jnp.int32)
    live_rows = live_mask(positions, seq_lengths, vert_count * tok_local // 2, SHORT)
    return (jnp.where(live_rows, full_logprob, 0.0), jnp.where(live_rows, full_entropy, 0.0))


def solution(mesh):
    wa_count, vert_count = mesh.devices.shape
    y_count = 4
    c_count = 2
    z_count = vert_count // (y_count * c_count)
    fine = Mesh(mesh.devices.reshape(wa_count, y_count, z_count, c_count), ("x",) + VERT)
    in_specs = (P(VERT, "x"), P("x"), P("x", VERT), P(VERT), P())
    out_specs = (P(VERT), P(VERT))
    return jax.shard_map(
        per_device, mesh=fine, in_specs=in_specs, out_specs=out_specs, check_vma=False
    )
```

```python
import functools

import jax
import jax.numpy as jnp
from jax import lax
from jax.experimental import pallas as pl
from jax.experimental.pallas import tpu as pltpu
from jax.sharding import Mesh
from jax.sharding import PartitionSpec as P

D = 1024
SHORT = 128


norm_epsilon = 1e-06

VERT = ("y", "z", "c")
TOKEN_AXES = ("z", "c")


def live_mask(positions, seq_lengths, long_len, short_len):
    is_long = positions < long_len
    beyond = jnp.maximum(positions - long_len, 0)
    seq_index = jnp.where(is_long, 0, 1 + beyond // short_len)
    offset = jnp.where(is_long, positions, beyond % short_len)
    return offset < jnp.take(seq_lengths, seq_index)


MESH_IDS = pl.DeviceIdType.MESH


def fused_kernel(
    vocab_local, hidden_ref, gain_ref, weight_ref, ids_ref, results_out,
    normed_out, weight_out, ids_out, piece_vmem, gain_vmem, normed_vmem,
    spread, merged, result, ids_turned,
    piece_send, piece_recv, gain_send, gain_recv,
    row_send, row_recv, weight_send, weight_recv, id_send, id_recv, own_sems,
    first_send, first_recv, second_send, second_recv, stat_sems,
):
    x_count = lax.axis_size("x")
    y_count = lax.axis_size("y")
    z_count = lax.axis_size("z")
    c_count = lax.axis_size("c")
    x_index = lax.axis_index("x")
    y_index = lax.axis_index("y")
    z_index = lax.axis_index("z")
    c_index = lax.axis_index("c")
    row_group = z_count * c_count
    weight_group = x_count * y_count
    row_rank = z_index * c_count + c_index
    weight_rank = x_index * y_count + y_index
    other_core = 1 - c_index

    def row_peer(step):
        rank = lax.rem(row_rank + step, row_group)
        return (x_index, y_index, rank // c_count, rank % c_count)

    def weight_peer(step):
        rank = lax.rem(weight_rank + step, weight_group)
        return rank, (rank // y_count, rank % y_count, z_index, c_index)

    def ring_z(shift):
        return lax.rem(z_index + shift + z_count, z_count)

    barrier = pltpu.get_barrier_semaphore()
    for step in range(1, row_group):
        pl.semaphore_signal(barrier, inc=1, device_id=row_peer(step), device_id_type=MESH_IDS)
    for step in range(1, weight_group):
        pl.semaphore_signal(barrier, inc=1, device_id=weight_peer(step)[1], device_id_type=MESH_IDS)
    pl.semaphore_wait(barrier, row_group - 1 + weight_group - 1)

    quarter = piece_vmem.shape[1]
    width = piece_vmem.shape[2]

    def x_peer(step):
        return (lax.rem(x_index + step, x_count), y_index, z_index, c_index)

    own_piece = pltpu.make_async_copy(
        hidden_ref.at[pl.ds(x_index * quarter, quarter)], piece_vmem.at[x_index], own_sems.at[3]
    )
    own_gain = pltpu.make_async_copy(gain_ref, gain_vmem.at[x_index], own_sems.at[4])
    own_piece.start()
    own_gain.start()
    piece_copies = []
    for step in range(1, x_count):
        target = lax.rem(x_index + step, x_count)
        for src, dst, send_sem, recv_sem in (
            (hidden_ref.at[pl.ds(target * quarter, quarter)], piece_vmem, piece_send, piece_recv),
            (gain_ref, gain_vmem, gain_send, gain_recv),
        ):
            copy = pltpu.make_async_remote_copy(
                src_ref=src, dst_ref=dst.at[x_index],
                send_sem=send_sem.at[step - 1], recv_sem=recv_sem.at[x_index],
                device_id=x_peer(step), device_id_type=MESH_IDS,
            )
            copy.start()
            piece_copies.append(copy)

    own = [
        pltpu.make_async_copy(weight_ref, weight_out.at[weight_rank], own_sems.at[1]),
        pltpu.make_async_copy(ids_ref, ids_out.at[row_rank], own_sems.at[2]),
    ]
    for copy in own:
        copy.start()

    sends = []

    def send_row(source_z, device, sem_index, from_input):
        slot = source_z * c_count + c_index
        copy = pltpu.make_async_remote_copy(
            src_ref=normed_out.at[slot],
            dst_ref=normed_out.at[slot],
            send_sem=row_send.at[sem_index], recv_sem=row_recv.at[slot],
            device_id=device, device_id_type=MESH_IDS,
        )
        copy.start()
        sends.append(copy)

    def wait_row(source_z, source_core):
        slot = source_z * c_count + source_core
        pltpu.make_async_remote_copy(
            src_ref=normed_out.at[slot], dst_ref=normed_out.at[slot],
            send_sem=row_send.at[0], recv_sem=row_recv.at[slot],
            device_id=(x_index, y_index, z_index, other_core), device_id_type=MESH_IDS,
        ).wait_recv()

    right = (x_index, y_index, ring_z(1), c_index)
    left = (x_index, y_index, ring_z(-1), c_index)
    partner = (x_index, y_index, z_index, other_core)
    right_steps = z_count // 2
    left_steps = z_count - 1 - right_steps
    sem_count = [0]

    def next_sem():
        sem_count[0] += 1
        return sem_count[0] - 1

    for step in range(1, weight_group):
        _, device = weight_peer(step)
        copy = pltpu.make_async_remote_copy(
            src_ref=weight_ref, dst_ref=weight_out.at[weight_rank],
            send_sem=weight_send.at[step - 1], recv_sem=weight_recv.at[weight_rank],
            device_id=device, device_id_type=MESH_IDS,
        )
        copy.start()
        sends.append(copy)
    for step in range(1, row_group):
        copy = pltpu.make_async_remote_copy(
            src_ref=ids_ref, dst_ref=ids_out.at[row_rank],
            send_sem=id_send.at[step - 1], recv_sem=id_recv.at[row_rank],
            device_id=row_peer(step), device_id_type=MESH_IDS,
        )
        copy.start()
        sends.append(copy)

    own_piece.wait()
    own_gain.wait()
    for step in range(1, x_count):
        source = lax.rem(x_index + x_count - step, x_count)
        for src, dst, send_sem, recv_sem in (
            (hidden_ref.at[pl.ds(0, quarter)], piece_vmem, piece_send, piece_recv),
            (gain_ref, gain_vmem, gain_send, gain_recv),
        ):
            pltpu.make_async_remote_copy(
                src_ref=src, dst_ref=dst.at[source],
                send_sem=send_sem.at[step - 1], recv_sem=recv_sem.at[source],
                device_id=x_peer(x_count - step), device_id_type=MESH_IDS,
            ).wait_recv()
    squares = jnp.zeros((quarter, 1), jnp.float32)
    for part in range(x_count):
        values = piece_vmem[part].astype(jnp.float32)
        squares = squares + jnp.sum(values * values, axis=1, keepdims=True)
    scale = lax.rsqrt(squares / (x_count * width) + norm_epsilon)
    for part in range(x_count):
        values = piece_vmem[part].astype(jnp.float32)
        gain = gain_vmem[part].astype(jnp.float32)
        normed_vmem[:, part * width:(part + 1) * width] = (values * scale * gain).astype(normed_vmem.dtype)
    own_row = pltpu.make_async_copy(normed_vmem, normed_out.at[row_rank], own_sems.at[0])
    own_row.start()
    own_row.wait()

    send_row(z_index, right, next_sem(), True)
    if left_steps > 0:
        send_row(z_index, left, next_sem(), True)
    send_row(z_index, partner, next_sem(), True)

    for step in range(1, right_steps + 1):
        from_left = ring_z(-step)
        wait_row(from_left, c_index)
        if step < right_steps:
            send_row(from_left, right, next_sem(), False)
        send_row(from_left, partner, next_sem(), False)
        if step <= left_steps:
            from_right = ring_z(step)
            wait_row(from_right, c_index)
            if step < left_steps:
                send_row(from_right, left, next_sem(), False)
            send_row(from_right, partner, next_sem(), False)

    for copy in own:
        copy.wait()
    for step in range(z_count):
        wait_row(lax.rem(z_index + step, z_count), other_core)
    for step in range(1, weight_group):
        source = lax.rem(weight_rank + weight_group - step, weight_group)
        pltpu.make_async_remote_copy(
            src_ref=weight_ref, dst_ref=weight_out.at[source],
            send_sem=weight_send.at[0], recv_sem=weight_recv.at[source],
            device_id=weight_peer(step)[1], device_id_type=MESH_IDS,
        ).wait_recv()
    for step in range(1, row_group):
        source = lax.rem(row_rank + row_group - step, row_group)
        pltpu.make_async_remote_copy(
            src_ref=ids_ref, dst_ref=ids_out.at[source],
            send_sem=id_send.at[0], recv_sem=id_recv.at[source],
            device_id=row_peer(step), device_id_type=MESH_IDS,
        ).wait_recv()
    for copy in sends + piece_copies:
        copy.wait_send()

    group = row_group
    rank = row_rank
    width = weight_out.shape[1]
    padded = weight_out.shape[2]
    spread[...] = jnp.zeros_like(spread)
    result[...] = jnp.zeros_like(result)

    own_stats = pltpu.make_async_copy(spread.at[rank], merged.at[rank], stat_sems.at[0])

    def stats_copy(slot):
        return pltpu.make_async_remote_copy(
            src_ref=spread.at[slot], dst_ref=merged.at[rank],
            send_sem=first_send.at[slot], recv_sem=first_recv.at[rank],
            device_id=(x_index, y_index, slot // c_count, slot % c_count), device_id_type=MESH_IDS,
        )

    def send_chunk(first_slot):
        for slot in range(first_slot, first_slot + slots_per_chunk):

            @pl.when(slot != rank)
            def _():
                stats_copy(slot).start()

            @pl.when(slot == rank)
            def _():
                own_stats.start()

    chunk = 256
    slots_per_chunk = chunk // quarter
    column = lax.broadcasted_iota(jnp.int32, (chunk, padded), 1)
    valid = column < vocab_local
    lane = lax.broadcasted_iota(jnp.int32, (chunk, 128), 1)
    for first in range(0, normed_out.shape[0] * quarter, chunk):
        blocks = []
        for y_block in range(y_count):
            total = jnp.zeros((chunk, padded), jnp.float32)
            for x_block in range(x_count):
                rows = normed_out[first // quarter:(first + chunk) // quarter, :, x_block * width:(x_block + 1) * width]
                total = total + jnp.dot(
                    rows.reshape(chunk, width),
                    weight_out[x_block * y_count + y_block],
                    preferred_element_type=jnp.float32,
                )
            blocks.append(total)
        id_rows = jnp.concatenate(
            [ids_out[slot] for slot in range(first // quarter, first // quarter + slots_per_chunk)], axis=0
        )
        ids_turned[...] = id_rows.astype(jnp.float32).T
        mine = ids_turned[pl.ds(pl.multiple_of(x_index * quarter, quarter), quarter), :]
        target = jnp.concatenate(
            [mine[:, part:part + 1] for part in range(slots_per_chunk)], axis=0
        ).astype(jnp.int32)
        peak = None
        for y_block, block in enumerate(blocks):
            block_peak = jnp.max(jnp.where(valid, block, -jnp.inf), axis=1, keepdims=True)
            peak = block_peak if peak is None else jnp.maximum(peak, block_peak)
        row_sum = jnp.zeros((chunk, 1), jnp.float32)
        row_weighted = jnp.zeros((chunk, 1), jnp.float32)
        row_picked = jnp.zeros((chunk, 1), jnp.float32)
        for y_block, block in enumerate(blocks):
            scaled = jnp.where(valid, jnp.exp(block - peak), 0.0)
            row_sum = row_sum + jnp.sum(scaled, axis=1, keepdims=True)
            row_weighted = row_weighted + jnp.sum(scaled * block, axis=1, keepdims=True)
            global_id = ((y_block * z_count + z_index) * c_count + c_index) * vocab_local + column
            hit = valid & (global_id == target)
            row_picked = row_picked + jnp.sum(jnp.where(hit, block, 0.0), axis=1, keepdims=True)
        table = jnp.where(
            lane == 0, peak,
            jnp.where(lane == 1, row_sum, jnp.where(lane == 2, row_weighted, jnp.where(lane == 3, row_picked, 0.0))),
        )
        lanes = table.T
        for part in range(slots_per_chunk):
            slot = first // quarter + part
            spread[slot, :, 0:quarter] = lanes[0:8, part * quarter:(part + 1) * quarter]
        if first > 0:
            send_chunk(first // quarter - slots_per_chunk)
    send_chunk(group - slots_per_chunk)

    for slot in range(group):

        @pl.when(slot != rank)
        def _():
            stats_copy(slot).wait_send()

        @pl.when(slot == rank)
        def _():
            own_stats.wait()

    def finish(step, carry):
        source = lax.rem(rank + group - step, group)
        pltpu.make_async_remote_copy(
            src_ref=spread.at[source], dst_ref=merged.at[source],
            send_sem=first_send.at[source], recv_sem=first_recv.at[source],
            device_id=row_peer(step), device_id_type=MESH_IDS,
        ).wait_recv()
        return carry

    lax.fori_loop(1, group, finish, 0)

    highest = merged[0, 0:1, :]
    for source in range(1, group):
        highest = jnp.maximum(highest, merged[source, 0:1, :])
    totals = jnp.zeros_like(highest)
    weighted = jnp.zeros_like(highest)
    picked = jnp.zeros_like(highest)
    for source in range(group):
        factor = jnp.exp(merged[source, 0:1, :] - highest)
        totals = totals + merged[source, 1:2, :] * factor
        weighted = weighted + merged[source, 2:3, :] * factor
        picked = picked + merged[source, 3:4, :]
    log_norm = highest + jnp.log(totals)
    result[0:1, :] = picked - log_norm
    result[1:2, :] = log_norm - weighted / totals

    mine = pltpu.make_async_copy(result, results_out.at[x_index], stat_sems.at[1])
    mine.start()
    copies = []
    for step in range(1, x_count):
        copy = pltpu.make_async_remote_copy(
            src_ref=result, dst_ref=results_out.at[x_index],
            send_sem=second_send.at[step - 1], recv_sem=second_recv.at[x_index],
            device_id=x_peer(step), device_id_type=MESH_IDS,
        )
        copy.start()
        copies.append(copy)
    mine.wait()
    for step in range(1, x_count):
        copies[step - 1].wait_send()
        source = lax.rem(x_index + x_count - step, x_count)
        pltpu.make_async_remote_copy(
            src_ref=result, dst_ref=results_out.at[source],
            send_sem=second_send.at[step - 1], recv_sem=second_recv.at[source],
            device_id=x_peer(x_count - step), device_id_type=MESH_IDS,
        ).wait_recv()


def score_all(hidden, gain, weight, ids, x_count, row_group, weight_group, vocab_local):
    quarter = hidden.shape[0] // x_count
    width = hidden.shape[1]
    any_spec = pl.BlockSpec(memory_space=pl.ANY)
    return pl.pallas_call(
        functools.partial(fused_kernel, vocab_local),
        out_shape=jax.ShapeDtypeStruct((x_count, 8, 128), jnp.float32),
        in_specs=[any_spec] * 4,
        out_specs=any_spec,
        scratch_shapes=[
            pltpu.VMEM((row_group, quarter, x_count * width), hidden.dtype),
            pltpu.VMEM((weight_group,) + weight.shape, weight.dtype),
            pltpu.VMEM((row_group,) + ids.shape, ids.dtype),
            pltpu.VMEM((x_count, quarter, width), hidden.dtype),
            pltpu.VMEM((x_count,) + gain.shape, gain.dtype),
            pltpu.VMEM((quarter, x_count * width), hidden.dtype),
            pltpu.VMEM((row_group, 8, 128), jnp.float32),
            pltpu.VMEM((row_group, 8, 128), jnp.float32),
            pltpu.VMEM((8, 128), jnp.float32),
            pltpu.VMEM((ids.shape[1], 8), jnp.float32),
            pltpu.SemaphoreType.DMA((x_count - 1,)),
            pltpu.SemaphoreType.DMA((x_count,)),
            pltpu.SemaphoreType.DMA((x_count - 1,)),
            pltpu.SemaphoreType.DMA((x_count,)),
            pltpu.SemaphoreType.DMA((row_group - 1,)),
            pltpu.SemaphoreType.DMA((row_group,)),
            pltpu.SemaphoreType.DMA((weight_group - 1,)),
            pltpu.SemaphoreType.DMA((weight_group,)),
            pltpu.SemaphoreType.DMA((row_group - 1,)),
            pltpu.SemaphoreType.DMA((row_group,)),
            pltpu.SemaphoreType.DMA((5,)),
            pltpu.SemaphoreType.DMA((row_group,)),
            pltpu.SemaphoreType.DMA((row_group,)),
            pltpu.SemaphoreType.DMA((x_count - 1,)),
            pltpu.SemaphoreType.DMA((x_count,)),
            pltpu.SemaphoreType.DMA((2,)),
        ],
        compiler_params=pltpu.CompilerParams(collective_id=0, has_side_effects=True),
    )(hidden, gain, weight, ids)


def per_device(hidden, norm_gain, head_weight, target_ids, seq_lengths):
    x_count = lax.axis_size("x")
    y_count = lax.axis_size("y")
    z_count = lax.axis_size("z")
    c_count = lax.axis_size("c")
    x_index = lax.axis_index("x")
    y_index = lax.axis_index("y")
    z_index = lax.axis_index("z")
    c_index = lax.axis_index("c")
    vert_count = y_count * z_count * c_count
    vert_index = (y_index * z_count + z_index) * c_count + c_index
    tok_local = hidden.shape[0]
    quarter = tok_local // x_count
    vocab_local = head_weight.shape[1]
    group_count = z_count * c_count

    results = score_all(
        hidden, norm_gain.reshape(1, -1), head_weight, target_ids.reshape(1, -1),
        x_count, group_count, x_count * y_count, vocab_local,
    )
    full_logprob = results[:, 0, :quarter].reshape(-1)
    full_entropy = results[:, 1, :quarter].reshape(-1)
    positions = vert_index * tok_local + jnp.arange(tok_local, dtype=jnp.int32)
    live_rows = live_mask(positions, seq_lengths, vert_count * tok_local // 2, SHORT)
    return (jnp.where(live_rows, full_logprob, 0.0), jnp.where(live_rows, full_entropy, 0.0))


def solution(mesh):
    wa_count, vert_count = mesh.devices.shape
    y_count = 4
    c_count = 2
    z_count = vert_count // (y_count * c_count)
    fine = Mesh(mesh.devices.reshape(wa_count, y_count, z_count, c_count), ("x",) + VERT)
    in_specs = (P(VERT, "x"), P("x"), P("x", VERT), P(VERT), P())
    out_specs = (P(VERT), P(VERT))
    return jax.shard_map(
        per_device, mesh=fine, in_specs=in_specs, out_specs=out_specs, check_vma=False
    )
```

```python
import functools

import jax
import jax.numpy as jnp
from jax import lax
from jax.experimental import pallas as pl
from jax.experimental.pallas import tpu as pltpu
from jax.sharding import Mesh
from jax.sharding import PartitionSpec as P

D = 1024
SHORT = 128


norm_epsilon = 1e-06

VERT = ("y", "z", "c")
TOKEN_AXES = ("z", "c")


def live_mask(positions, seq_lengths, long_len, short_len):
    is_long = positions < long_len
    beyond = jnp.maximum(positions - long_len, 0)
    seq_index = jnp.where(is_long, 0, 1 + beyond // short_len)
    offset = jnp.where(is_long, positions, beyond % short_len)
    return offset < jnp.take(seq_lengths, seq_index)


MESH_IDS = pl.DeviceIdType.MESH


def fused_kernel(
    vocab_local, hidden_ref, gain_ref, weight_ref, ids_ref, lengths_ref, results_out,
    normed_out, weight_out, ids_out, piece_vmem, gain_vmem, normed_vmem,
    spread, merged, result, ids_turned,
    piece_send, piece_recv, gain_send, gain_recv,
    row_send, row_recv, weight_send, weight_recv, id_send, id_recv, own_sems,
    first_send, first_recv, second_send, second_recv, stat_sems,
):
    x_count = lax.axis_size("x")
    y_count = lax.axis_size("y")
    z_count = lax.axis_size("z")
    c_count = lax.axis_size("c")
    x_index = lax.axis_index("x")
    y_index = lax.axis_index("y")
    z_index = lax.axis_index("z")
    c_index = lax.axis_index("c")
    row_group = z_count * c_count
    weight_group = x_count * y_count
    row_rank = z_index * c_count + c_index
    weight_rank = x_index * y_count + y_index
    other_core = 1 - c_index

    def row_peer(step):
        rank = lax.rem(row_rank + step, row_group)
        return (x_index, y_index, rank // c_count, rank % c_count)

    def weight_peer(step):
        rank = lax.rem(weight_rank + step, weight_group)
        return rank, (rank // y_count, rank % y_count, z_index, c_index)

    def ring_z(shift):
        return lax.rem(z_index + shift + z_count, z_count)

    barrier = pltpu.get_barrier_semaphore()
    for step in range(1, row_group):
        pl.semaphore_signal(barrier, inc=1, device_id=row_peer(step), device_id_type=MESH_IDS)
    for step in range(1, weight_group):
        pl.semaphore_signal(barrier, inc=1, device_id=weight_peer(step)[1], device_id_type=MESH_IDS)
    pl.semaphore_wait(barrier, row_group - 1 + weight_group - 1)

    quarter = piece_vmem.shape[1]
    width = piece_vmem.shape[2]

    def x_peer(step):
        return (lax.rem(x_index + step, x_count), y_index, z_index, c_index)

    own_piece = pltpu.make_async_copy(
        hidden_ref.at[pl.ds(x_index * quarter, quarter)], piece_vmem.at[x_index], own_sems.at[3]
    )
    own_gain = pltpu.make_async_copy(gain_ref, gain_vmem.at[x_index], own_sems.at[4])
    own_piece.start()
    own_gain.start()
    piece_copies = []
    for step in range(1, x_count):
        target = lax.rem(x_index + step, x_count)
        for src, dst, send_sem, recv_sem in (
            (hidden_ref.at[pl.ds(target * quarter, quarter)], piece_vmem, piece_send, piece_recv),
            (gain_ref, gain_vmem, gain_send, gain_recv),
        ):
            copy = pltpu.make_async_remote_copy(
                src_ref=src, dst_ref=dst.at[x_index],
                send_sem=send_sem.at[step - 1], recv_sem=recv_sem.at[x_index],
                device_id=x_peer(step), device_id_type=MESH_IDS,
            )
            copy.start()
            piece_copies.append(copy)

    own = [
        pltpu.make_async_copy(weight_ref, weight_out.at[weight_rank], own_sems.at[1]),
        pltpu.make_async_copy(ids_ref, ids_out.at[row_rank], own_sems.at[2]),
    ]
    for copy in own:
        copy.start()

    sends = []

    def send_row(source_z, device, sem_index, from_input):
        slot = source_z * c_count + c_index
        copy = pltpu.make_async_remote_copy(
            src_ref=normed_out.at[slot],
            dst_ref=normed_out.at[slot],
            send_sem=row_send.at[sem_index], recv_sem=row_recv.at[slot],
            device_id=device, device_id_type=MESH_IDS,
        )
        copy.start()
        sends.append(copy)

    def wait_row(source_z, source_core):
        slot = source_z * c_count + source_core
        pltpu.make_async_remote_copy(
            src_ref=normed_out.at[slot], dst_ref=normed_out.at[slot],
            send_sem=row_send.at[0], recv_sem=row_recv.at[slot],
            device_id=(x_index, y_index, z_index, other_core), device_id_type=MESH_IDS,
        ).wait_recv()

    right = (x_index, y_index, ring_z(1), c_index)
    left = (x_index, y_index, ring_z(-1), c_index)
    partner = (x_index, y_index, z_index, other_core)
    right_steps = z_count // 2
    left_steps = z_count - 1 - right_steps
    sem_count = [0]

    def next_sem():
        sem_count[0] += 1
        return sem_count[0] - 1

    for step in range(1, weight_group):
        _, device = weight_peer(step)
        copy = pltpu.make_async_remote_copy(
            src_ref=weight_ref, dst_ref=weight_out.at[weight_rank],
            send_sem=weight_send.at[step - 1], recv_sem=weight_recv.at[weight_rank],
            device_id=device, device_id_type=MESH_IDS,
        )
        copy.start()
        sends.append(copy)
    for step in range(1, row_group):
        copy = pltpu.make_async_remote_copy(
            src_ref=ids_ref, dst_ref=ids_out.at[row_rank],
            send_sem=id_send.at[step - 1], recv_sem=id_recv.at[row_rank],
            device_id=row_peer(step), device_id_type=MESH_IDS,
        )
        copy.start()
        sends.append(copy)

    own_piece.wait()
    own_gain.wait()
    for step in range(1, x_count):
        source = lax.rem(x_index + x_count - step, x_count)
        for src, dst, send_sem, recv_sem in (
            (hidden_ref.at[pl.ds(0, quarter)], piece_vmem, piece_send, piece_recv),
            (gain_ref, gain_vmem, gain_send, gain_recv),
        ):
            pltpu.make_async_remote_copy(
                src_ref=src, dst_ref=dst.at[source],
                send_sem=send_sem.at[step - 1], recv_sem=recv_sem.at[source],
                device_id=x_peer(x_count - step), device_id_type=MESH_IDS,
            ).wait_recv()
    squares = jnp.zeros((quarter, 1), jnp.float32)
    for part in range(x_count):
        values = piece_vmem[part].astype(jnp.float32)
        squares = squares + jnp.sum(values * values, axis=1, keepdims=True)
    scale = lax.rsqrt(squares / (x_count * width) + norm_epsilon)
    for part in range(x_count):
        values = piece_vmem[part].astype(jnp.float32)
        gain = gain_vmem[part].astype(jnp.float32)
        normed_vmem[:, part * width:(part + 1) * width] = (values * scale * gain).astype(normed_vmem.dtype)
    own_row = pltpu.make_async_copy(normed_vmem, normed_out.at[row_rank], own_sems.at[0])
    own_row.start()
    own_row.wait()

    send_row(z_index, right, next_sem(), True)
    if left_steps > 0:
        send_row(z_index, left, next_sem(), True)
    send_row(z_index, partner, next_sem(), True)

    for step in range(1, right_steps + 1):
        from_left = ring_z(-step)
        wait_row(from_left, c_index)
        if step < right_steps:
            send_row(from_left, right, next_sem(), False)
        send_row(from_left, partner, next_sem(), False)
        if step <= left_steps:
            from_right = ring_z(step)
            wait_row(from_right, c_index)
            if step < left_steps:
                send_row(from_right, left, next_sem(), False)
            send_row(from_right, partner, next_sem(), False)

    for copy in own:
        copy.wait()
    for step in range(z_count):
        wait_row(lax.rem(z_index + step, z_count), other_core)
    for step in range(1, weight_group):
        source = lax.rem(weight_rank + weight_group - step, weight_group)
        pltpu.make_async_remote_copy(
            src_ref=weight_ref, dst_ref=weight_out.at[source],
            send_sem=weight_send.at[0], recv_sem=weight_recv.at[source],
            device_id=weight_peer(step)[1], device_id_type=MESH_IDS,
        ).wait_recv()
    for step in range(1, row_group):
        source = lax.rem(row_rank + row_group - step, row_group)
        pltpu.make_async_remote_copy(
            src_ref=ids_ref, dst_ref=ids_out.at[source],
            send_sem=id_send.at[0], recv_sem=id_recv.at[source],
            device_id=row_peer(step), device_id_type=MESH_IDS,
        ).wait_recv()
    for copy in sends + piece_copies:
        copy.wait_send()

    group = row_group
    rank = row_rank
    width = weight_out.shape[1]
    padded = weight_out.shape[2]
    spread[...] = jnp.zeros_like(spread)
    result[...] = jnp.zeros_like(result)

    own_stats = pltpu.make_async_copy(spread.at[rank], merged.at[rank], stat_sems.at[0])

    def stats_copy(slot):
        return pltpu.make_async_remote_copy(
            src_ref=spread.at[slot], dst_ref=merged.at[rank],
            send_sem=first_send.at[slot], recv_sem=first_recv.at[rank],
            device_id=(x_index, y_index, slot // c_count, slot % c_count), device_id_type=MESH_IDS,
        )

    def send_chunk(first_slot):
        for slot in range(first_slot, first_slot + slots_per_chunk):

            @pl.when(slot != rank)
            def _():
                stats_copy(slot).start()

            @pl.when(slot == rank)
            def _():
                own_stats.start()

    chunk = 256
    slots_per_chunk = chunk // quarter
    column = lax.broadcasted_iota(jnp.int32, (chunk, padded), 1)
    valid = column < vocab_local
    lane = lax.broadcasted_iota(jnp.int32, (chunk, 128), 1)
    for first in range(0, normed_out.shape[0] * quarter, chunk):
        blocks = []
        for y_block in range(y_count):
            total = jnp.zeros((chunk, padded), jnp.float32)
            for x_block in range(x_count):
                rows = normed_out[first // quarter:(first + chunk) // quarter, :, x_block * width:(x_block + 1) * width]
                total = total + jnp.dot(
                    rows.reshape(chunk, width),
                    weight_out[x_block * y_count + y_block],
                    preferred_element_type=jnp.float32,
                )
            blocks.append(total)
        id_rows = jnp.concatenate(
            [ids_out[slot] for slot in range(first // quarter, first // quarter + slots_per_chunk)], axis=0
        )
        ids_turned[...] = id_rows.astype(jnp.float32).T
        mine = ids_turned[pl.ds(pl.multiple_of(x_index * quarter, quarter), quarter), :]
        target = jnp.concatenate(
            [mine[:, part:part + 1] for part in range(slots_per_chunk)], axis=0
        ).astype(jnp.int32)
        peak = None
        for y_block, block in enumerate(blocks):
            block_peak = jnp.max(jnp.where(valid, block, -jnp.inf), axis=1, keepdims=True)
            peak = block_peak if peak is None else jnp.maximum(peak, block_peak)
        row_sum = jnp.zeros((chunk, 1), jnp.float32)
        row_weighted = jnp.zeros((chunk, 1), jnp.float32)
        row_picked = jnp.zeros((chunk, 1), jnp.float32)
        for y_block, block in enumerate(blocks):
            scaled = jnp.where(valid, jnp.exp(block - peak), 0.0)
            row_sum = row_sum + jnp.sum(scaled, axis=1, keepdims=True)
            row_weighted = row_weighted + jnp.sum(scaled * block, axis=1, keepdims=True)
            global_id = ((y_block * z_count + z_index) * c_count + c_index) * vocab_local + column
            hit = valid & (global_id == target)
            row_picked = row_picked + jnp.sum(jnp.where(hit, block, 0.0), axis=1, keepdims=True)
        table = jnp.where(
            lane == 0, peak,
            jnp.where(lane == 1, row_sum, jnp.where(lane == 2, row_weighted, jnp.where(lane == 3, row_picked, 0.0))),
        )
        lanes = table.T
        for part in range(slots_per_chunk):
            slot = first // quarter + part
            spread[slot, :, 0:quarter] = lanes[0:8, part * quarter:(part + 1) * quarter]
        if first > 0:
            send_chunk(first // quarter - slots_per_chunk)
    send_chunk(group - slots_per_chunk)

    for slot in range(group):

        @pl.when(slot != rank)
        def _():
            stats_copy(slot).wait_send()

        @pl.when(slot == rank)
        def _():
            own_stats.wait()

    def finish(step, carry):
        source = lax.rem(rank + group - step, group)
        pltpu.make_async_remote_copy(
            src_ref=spread.at[source], dst_ref=merged.at[source],
            send_sem=first_send.at[source], recv_sem=first_recv.at[source],
            device_id=row_peer(step), device_id_type=MESH_IDS,
        ).wait_recv()
        return carry

    lax.fori_loop(1, group, finish, 0)

    highest = merged[0, 0:1, :]
    for source in range(1, group):
        highest = jnp.maximum(highest, merged[source, 0:1, :])
    totals = jnp.zeros_like(highest)
    weighted = jnp.zeros_like(highest)
    picked = jnp.zeros_like(highest)
    for source in range(group):
        factor = jnp.exp(merged[source, 0:1, :] - highest)
        totals = totals + merged[source, 1:2, :] * factor
        weighted = weighted + merged[source, 2:3, :] * factor
        picked = picked + merged[source, 3:4, :]
    log_norm = highest + jnp.log(totals)

    block_tokens = x_count * quarter
    vert_index = (y_index * z_count + z_index) * c_count + c_index
    long_len = y_count * z_count * c_count * block_tokens // 2
    block_start = vert_index * block_tokens
    in_long = block_start < long_len
    sequence = jnp.where(in_long, 0, 1 + (block_start - long_len) // SHORT)
    live_length = lengths_ref[sequence]
    positions = block_start + x_index * quarter + lax.broadcasted_iota(jnp.int32, (1, 128), 1)
    offsets = jnp.where(in_long, positions, jnp.maximum(positions - long_len, 0) % SHORT)
    live = offsets < live_length
    result[0:1, :] = jnp.where(live, picked - log_norm, 0.0)
    result[1:2, :] = jnp.where(live, log_norm - weighted / totals, 0.0)

    mine = pltpu.make_async_copy(result, results_out.at[x_index], stat_sems.at[1])
    mine.start()
    copies = []
    for step in range(1, x_count):
        copy = pltpu.make_async_remote_copy(
            src_ref=result, dst_ref=results_out.at[x_index],
            send_sem=second_send.at[step - 1], recv_sem=second_recv.at[x_index],
            device_id=x_peer(step), device_id_type=MESH_IDS,
        )
        copy.start()
        copies.append(copy)
    mine.wait()
    for step in range(1, x_count):
        copies[step - 1].wait_send()
        source = lax.rem(x_index + x_count - step, x_count)
        pltpu.make_async_remote_copy(
            src_ref=result, dst_ref=results_out.at[source],
            send_sem=second_send.at[step - 1], recv_sem=second_recv.at[source],
            device_id=x_peer(x_count - step), device_id_type=MESH_IDS,
        ).wait_recv()


def score_all(hidden, gain, weight, ids, lengths, x_count, row_group, weight_group, vocab_local):
    quarter = hidden.shape[0] // x_count
    width = hidden.shape[1]
    any_spec = pl.BlockSpec(memory_space=pl.ANY)
    return pl.pallas_call(
        functools.partial(fused_kernel, vocab_local),
        out_shape=jax.ShapeDtypeStruct((x_count, 8, 128), jnp.float32),
        in_specs=[any_spec] * 4 + [pl.BlockSpec(memory_space=pltpu.SMEM)],
        out_specs=any_spec,
        scratch_shapes=[
            pltpu.VMEM((row_group, quarter, x_count * width), hidden.dtype),
            pltpu.VMEM((weight_group,) + weight.shape, weight.dtype),
            pltpu.VMEM((row_group,) + ids.shape, ids.dtype),
            pltpu.VMEM((x_count, quarter, width), hidden.dtype),
            pltpu.VMEM((x_count,) + gain.shape, gain.dtype),
            pltpu.VMEM((quarter, x_count * width), hidden.dtype),
            pltpu.VMEM((row_group, 8, 128), jnp.float32),
            pltpu.VMEM((row_group, 8, 128), jnp.float32),
            pltpu.VMEM((8, 128), jnp.float32),
            pltpu.VMEM((ids.shape[1], 8), jnp.float32),
            pltpu.SemaphoreType.DMA((x_count - 1,)),
            pltpu.SemaphoreType.DMA((x_count,)),
            pltpu.SemaphoreType.DMA((x_count - 1,)),
            pltpu.SemaphoreType.DMA((x_count,)),
            pltpu.SemaphoreType.DMA((row_group - 1,)),
            pltpu.SemaphoreType.DMA((row_group,)),
            pltpu.SemaphoreType.DMA((weight_group - 1,)),
            pltpu.SemaphoreType.DMA((weight_group,)),
            pltpu.SemaphoreType.DMA((row_group - 1,)),
            pltpu.SemaphoreType.DMA((row_group,)),
            pltpu.SemaphoreType.DMA((5,)),
            pltpu.SemaphoreType.DMA((row_group,)),
            pltpu.SemaphoreType.DMA((row_group,)),
            pltpu.SemaphoreType.DMA((x_count - 1,)),
            pltpu.SemaphoreType.DMA((x_count,)),
            pltpu.SemaphoreType.DMA((2,)),
        ],
        compiler_params=pltpu.CompilerParams(collective_id=0, has_side_effects=True),
    )(hidden, gain, weight, ids, lengths)


def per_device(hidden, norm_gain, head_weight, target_ids, seq_lengths):
    x_count = lax.axis_size("x")
    y_count = lax.axis_size("y")
    z_count = lax.axis_size("z")
    c_count = lax.axis_size("c")
    x_index = lax.axis_index("x")
    y_index = lax.axis_index("y")
    z_index = lax.axis_index("z")
    c_index = lax.axis_index("c")
    vert_count = y_count * z_count * c_count
    vert_index = (y_index * z_count + z_index) * c_count + c_index
    tok_local = hidden.shape[0]
    quarter = tok_local // x_count
    vocab_local = head_weight.shape[1]
    group_count = z_count * c_count

    results = score_all(
        hidden, norm_gain.reshape(1, -1), head_weight, target_ids.reshape(1, -1), seq_lengths,
        x_count, group_count, x_count * y_count, vocab_local,
    )
    full_logprob = results[:, 0, :quarter].reshape(-1)
    full_entropy = results[:, 1, :quarter].reshape(-1)
    return (full_logprob, full_entropy)


def solution(mesh):
    wa_count, vert_count = mesh.devices.shape
    y_count = 4
    c_count = 2
    z_count = vert_count // (y_count * c_count)
    fine = Mesh(mesh.devices.reshape(wa_count, y_count, z_count, c_count), ("x",) + VERT)
    in_specs = (P(VERT, "x"), P("x"), P("x", VERT), P(VERT), P())
    out_specs = (P(VERT), P(VERT))
    return jax.shard_map(
        per_device, mesh=fine, in_specs=in_specs, out_specs=out_specs, check_vma=False
    )
```

```python
import functools

import jax
import jax.numpy as jnp
from jax import lax
from jax.experimental import pallas as pl
from jax.experimental.pallas import tpu as pltpu
from jax.sharding import Mesh
from jax.sharding import PartitionSpec as P

D = 1024
SHORT = 128


norm_epsilon = 1e-06

VERT = ("y", "z", "c")
TOKEN_AXES = ("z", "c")


def live_mask(positions, seq_lengths, long_len, short_len):
    is_long = positions < long_len
    beyond = jnp.maximum(positions - long_len, 0)
    seq_index = jnp.where(is_long, 0, 1 + beyond // short_len)
    offset = jnp.where(is_long, positions, beyond % short_len)
    return offset < jnp.take(seq_lengths, seq_index)


MESH_IDS = pl.DeviceIdType.MESH


def fused_kernel(
    vocab_local, hidden_ref, gain_ref, weight_ref, ids_ref, lengths_ref, results_out,
    normed_out, weight_out, ids_out, piece_vmem, gain_vmem, normed_vmem,
    spread, merged, result, ids_turned,
    piece_send, piece_recv, gain_send, gain_recv,
    row_send, row_recv, weight_send, weight_recv, id_send, id_recv, own_sems,
    first_send, first_recv, second_send, second_recv, stat_sems,
):
    x_count = lax.axis_size("x")
    y_count = lax.axis_size("y")
    z_count = lax.axis_size("z")
    c_count = lax.axis_size("c")
    x_index = lax.axis_index("x")
    y_index = lax.axis_index("y")
    z_index = lax.axis_index("z")
    c_index = lax.axis_index("c")
    row_group = z_count * c_count
    weight_group = x_count * y_count
    row_rank = z_index * c_count + c_index
    weight_rank = x_index * y_count + y_index
    other_core = 1 - c_index

    def row_peer(step):
        rank = lax.rem(row_rank + step, row_group)
        return (x_index, y_index, rank // c_count, rank % c_count)

    def weight_peer(step):
        rank = lax.rem(weight_rank + step, weight_group)
        return rank, (rank // y_count, rank % y_count, z_index, c_index)

    def ring_z(shift):
        return lax.rem(z_index + shift + z_count, z_count)

    barrier = pltpu.get_barrier_semaphore()
    for step in range(1, row_group):
        pl.semaphore_signal(barrier, inc=1, device_id=row_peer(step), device_id_type=MESH_IDS)
    for step in range(1, weight_group):
        pl.semaphore_signal(barrier, inc=1, device_id=weight_peer(step)[1], device_id_type=MESH_IDS)
    pl.semaphore_wait(barrier, row_group - 1 + weight_group - 1)

    quarter = piece_vmem.shape[1]
    width = piece_vmem.shape[2]

    def x_peer(step):
        return (lax.rem(x_index + step, x_count), y_index, z_index, c_index)

    own_piece = pltpu.make_async_copy(
        hidden_ref.at[pl.ds(x_index * quarter, quarter)], piece_vmem.at[x_index], own_sems.at[3]
    )
    own_gain = pltpu.make_async_copy(gain_ref, gain_vmem.at[x_index], own_sems.at[4])
    own_piece.start()
    own_gain.start()
    piece_copies = []
    for step in range(1, x_count):
        target = lax.rem(x_index + step, x_count)
        for src, dst, send_sem, recv_sem in (
            (hidden_ref.at[pl.ds(target * quarter, quarter)], piece_vmem, piece_send, piece_recv),
            (gain_ref, gain_vmem, gain_send, gain_recv),
        ):
            copy = pltpu.make_async_remote_copy(
                src_ref=src, dst_ref=dst.at[x_index],
                send_sem=send_sem.at[step - 1], recv_sem=recv_sem.at[x_index],
                device_id=x_peer(step), device_id_type=MESH_IDS,
            )
            copy.start()
            piece_copies.append(copy)

    own = [
        pltpu.make_async_copy(weight_ref, weight_out.at[weight_rank], own_sems.at[1]),
        pltpu.make_async_copy(ids_ref, ids_out.at[row_rank], own_sems.at[2]),
    ]
    for copy in own:
        copy.start()

    sends = []

    def send_row(source_z, device, sem_index, from_input):
        slot = source_z * c_count + c_index
        copy = pltpu.make_async_remote_copy(
            src_ref=normed_out.at[slot],
            dst_ref=normed_out.at[slot],
            send_sem=row_send.at[sem_index], recv_sem=row_recv.at[slot],
            device_id=device, device_id_type=MESH_IDS,
        )
        copy.start()
        sends.append(copy)

    def wait_row(source_z, source_core):
        slot = source_z * c_count + source_core
        pltpu.make_async_remote_copy(
            src_ref=normed_out.at[slot], dst_ref=normed_out.at[slot],
            send_sem=row_send.at[0], recv_sem=row_recv.at[slot],
            device_id=(x_index, y_index, z_index, other_core), device_id_type=MESH_IDS,
        ).wait_recv()

    right = (x_index, y_index, ring_z(1), c_index)
    left = (x_index, y_index, ring_z(-1), c_index)
    partner = (x_index, y_index, z_index, other_core)
    right_steps = z_count // 2
    left_steps = z_count - 1 - right_steps
    sem_count = [0]

    def next_sem():
        sem_count[0] += 1
        return sem_count[0] - 1

    for step in range(1, weight_group):
        _, device = weight_peer(step)
        copy = pltpu.make_async_remote_copy(
            src_ref=weight_ref, dst_ref=weight_out.at[weight_rank],
            send_sem=weight_send.at[step - 1], recv_sem=weight_recv.at[weight_rank],
            device_id=device, device_id_type=MESH_IDS,
        )
        copy.start()
        sends.append(copy)
    for step in range(1, row_group):
        copy = pltpu.make_async_remote_copy(
            src_ref=ids_ref, dst_ref=ids_out.at[row_rank],
            send_sem=id_send.at[step - 1], recv_sem=id_recv.at[row_rank],
            device_id=row_peer(step), device_id_type=MESH_IDS,
        )
        copy.start()
        sends.append(copy)

    own_piece.wait()
    own_gain.wait()
    for step in range(1, x_count):
        source = lax.rem(x_index + x_count - step, x_count)
        for src, dst, send_sem, recv_sem in (
            (hidden_ref.at[pl.ds(0, quarter)], piece_vmem, piece_send, piece_recv),
            (gain_ref, gain_vmem, gain_send, gain_recv),
        ):
            pltpu.make_async_remote_copy(
                src_ref=src, dst_ref=dst.at[source],
                send_sem=send_sem.at[step - 1], recv_sem=recv_sem.at[source],
                device_id=x_peer(x_count - step), device_id_type=MESH_IDS,
            ).wait_recv()
    squares = jnp.zeros((quarter, 1), jnp.float32)
    for part in range(x_count):
        values = piece_vmem[part].astype(jnp.float32)
        squares = squares + jnp.sum(values * values, axis=1, keepdims=True)
    scale = lax.rsqrt(squares / (x_count * width) + norm_epsilon)
    for part in range(x_count):
        values = piece_vmem[part].astype(jnp.float32)
        gain = gain_vmem[part].astype(jnp.float32)
        normed_vmem[:, part * width:(part + 1) * width] = (values * scale * gain).astype(normed_vmem.dtype)
    own_row = pltpu.make_async_copy(normed_vmem, normed_out.at[row_rank], own_sems.at[0])
    own_row.start()
    own_row.wait()

    send_row(z_index, right, next_sem(), True)
    if left_steps > 0:
        send_row(z_index, left, next_sem(), True)
    send_row(z_index, partner, next_sem(), True)

    for step in range(1, right_steps + 1):
        from_left = ring_z(-step)
        wait_row(from_left, c_index)
        if step < right_steps:
            send_row(from_left, right, next_sem(), False)
        send_row(from_left, partner, next_sem(), False)
        if step <= left_steps:
            from_right = ring_z(step)
            wait_row(from_right, c_index)
            if step < left_steps:
                send_row(from_right, left, next_sem(), False)
            send_row(from_right, partner, next_sem(), False)

    for copy in own:
        copy.wait()
    for step in range(z_count):
        wait_row(lax.rem(z_index + step, z_count), other_core)
    for step in range(1, weight_group):
        source = lax.rem(weight_rank + weight_group - step, weight_group)
        pltpu.make_async_remote_copy(
            src_ref=weight_ref, dst_ref=weight_out.at[source],
            send_sem=weight_send.at[0], recv_sem=weight_recv.at[source],
            device_id=weight_peer(step)[1], device_id_type=MESH_IDS,
        ).wait_recv()
    for step in range(1, row_group):
        source = lax.rem(row_rank + row_group - step, row_group)
        pltpu.make_async_remote_copy(
            src_ref=ids_ref, dst_ref=ids_out.at[source],
            send_sem=id_send.at[0], recv_sem=id_recv.at[source],
            device_id=row_peer(step), device_id_type=MESH_IDS,
        ).wait_recv()

    group = row_group
    rank = row_rank
    width = weight_out.shape[1]
    padded = weight_out.shape[2]
    spread[...] = jnp.zeros_like(spread)
    result[...] = jnp.zeros_like(result)

    own_stats = pltpu.make_async_copy(spread.at[rank], merged.at[rank], stat_sems.at[0])

    def stats_copy(slot):
        return pltpu.make_async_remote_copy(
            src_ref=spread.at[slot], dst_ref=merged.at[rank],
            send_sem=first_send.at[slot], recv_sem=first_recv.at[rank],
            device_id=(x_index, y_index, slot // c_count, slot % c_count), device_id_type=MESH_IDS,
        )

    def send_chunk(first_slot):
        for slot in range(first_slot, first_slot + slots_per_chunk):

            @pl.when(slot != rank)
            def _():
                stats_copy(slot).start()

            @pl.when(slot == rank)
            def _():
                own_stats.start()

    chunk = 256
    slots_per_chunk = chunk // quarter
    column = lax.broadcasted_iota(jnp.int32, (chunk, padded), 1)
    valid = column < vocab_local
    lane = lax.broadcasted_iota(jnp.int32, (chunk, 128), 1)
    for first in range(0, normed_out.shape[0] * quarter, chunk):
        blocks = []
        for y_block in range(y_count):
            total = jnp.zeros((chunk, padded), jnp.float32)
            for x_block in range(x_count):
                rows = normed_out[first // quarter:(first + chunk) // quarter, :, x_block * width:(x_block + 1) * width]
                total = total + jnp.dot(
                    rows.reshape(chunk, width),
                    weight_out[x_block * y_count + y_block],
                    preferred_element_type=jnp.float32,
                )
            blocks.append(total)
        id_rows = jnp.concatenate(
            [ids_out[slot] for slot in range(first // quarter, first // quarter + slots_per_chunk)], axis=0
        )
        ids_turned[...] = id_rows.astype(jnp.float32).T
        mine = ids_turned[pl.ds(pl.multiple_of(x_index * quarter, quarter), quarter), :]
        target = jnp.concatenate(
            [mine[:, part:part + 1] for part in range(slots_per_chunk)], axis=0
        ).astype(jnp.int32)
        peak = None
        for y_block, block in enumerate(blocks):
            block_peak = jnp.max(jnp.where(valid, block, -jnp.inf), axis=1, keepdims=True)
            peak = block_peak if peak is None else jnp.maximum(peak, block_peak)
        row_sum = jnp.zeros((chunk, 1), jnp.float32)
        row_weighted = jnp.zeros((chunk, 1), jnp.float32)
        row_picked = jnp.zeros((chunk, 1), jnp.float32)
        for y_block, block in enumerate(blocks):
            scaled = jnp.where(valid, jnp.exp(block - peak), 0.0)
            row_sum = row_sum + jnp.sum(scaled, axis=1, keepdims=True)
            row_weighted = row_weighted + jnp.sum(scaled * block, axis=1, keepdims=True)
            global_id = ((y_block * z_count + z_index) * c_count + c_index) * vocab_local + column
            hit = valid & (global_id == target)
            row_picked = row_picked + jnp.sum(jnp.where(hit, block, 0.0), axis=1, keepdims=True)
        table = jnp.where(
            lane == 0, peak,
            jnp.where(lane == 1, row_sum, jnp.where(lane == 2, row_weighted, jnp.where(lane == 3, row_picked, 0.0))),
        )
        lanes = table.T
        for part in range(slots_per_chunk):
            slot = first // quarter + part
            spread[slot, :, 0:quarter] = lanes[0:8, part * quarter:(part + 1) * quarter]
        if first > 0:
            send_chunk(first // quarter - slots_per_chunk)
    send_chunk(group - slots_per_chunk)

    own_stats.wait()

    def finish(step, carry):
        source = lax.rem(rank + group - step, group)
        pltpu.make_async_remote_copy(
            src_ref=spread.at[source], dst_ref=merged.at[source],
            send_sem=first_send.at[source], recv_sem=first_recv.at[source],
            device_id=row_peer(step), device_id_type=MESH_IDS,
        ).wait_recv()
        return carry

    lax.fori_loop(1, group, finish, 0)

    highest = merged[0, 0:1, :]
    for source in range(1, group):
        highest = jnp.maximum(highest, merged[source, 0:1, :])
    totals = jnp.zeros_like(highest)
    weighted = jnp.zeros_like(highest)
    picked = jnp.zeros_like(highest)
    for source in range(group):
        factor = jnp.exp(merged[source, 0:1, :] - highest)
        totals = totals + merged[source, 1:2, :] * factor
        weighted = weighted + merged[source, 2:3, :] * factor
        picked = picked + merged[source, 3:4, :]
    log_norm = highest + jnp.log(totals)

    block_tokens = x_count * quarter
    vert_index = (y_index * z_count + z_index) * c_count + c_index
    long_len = y_count * z_count * c_count * block_tokens // 2
    block_start = vert_index * block_tokens
    in_long = block_start < long_len
    sequence = jnp.where(in_long, 0, 1 + (block_start - long_len) // SHORT)
    live_length = lengths_ref[sequence]
    positions = block_start + x_index * quarter + lax.broadcasted_iota(jnp.int32, (1, 128), 1)
    offsets = jnp.where(in_long, positions, jnp.maximum(positions - long_len, 0) % SHORT)
    live = offsets < live_length
    result[0:1, :] = jnp.where(live, picked - log_norm, 0.0)
    result[1:2, :] = jnp.where(live, log_norm - weighted / totals, 0.0)

    mine = pltpu.make_async_copy(result, results_out.at[x_index], stat_sems.at[1])
    mine.start()
    copies = []
    for step in range(1, x_count):
        copy = pltpu.make_async_remote_copy(
            src_ref=result, dst_ref=results_out.at[x_index],
            send_sem=second_send.at[step - 1], recv_sem=second_recv.at[x_index],
            device_id=x_peer(step), device_id_type=MESH_IDS,
        )
        copy.start()
        copies.append(copy)
    mine.wait()
    for step in range(1, x_count):
        copies[step - 1].wait_send()
        source = lax.rem(x_index + x_count - step, x_count)
        pltpu.make_async_remote_copy(
            src_ref=result, dst_ref=results_out.at[source],
            send_sem=second_send.at[step - 1], recv_sem=second_recv.at[source],
            device_id=x_peer(x_count - step), device_id_type=MESH_IDS,
        ).wait_recv()
    for copy in sends + piece_copies:
        copy.wait_send()
    for slot in range(group):

        @pl.when(slot != rank)
        def _():
            stats_copy(slot).wait_send()


def score_all(hidden, gain, weight, ids, lengths, x_count, row_group, weight_group, vocab_local):
    quarter = hidden.shape[0] // x_count
    width = hidden.shape[1]
    any_spec = pl.BlockSpec(memory_space=pl.ANY)
    return pl.pallas_call(
        functools.partial(fused_kernel, vocab_local),
        out_shape=jax.ShapeDtypeStruct((x_count, 8, 128), jnp.float32),
        in_specs=[any_spec] * 4 + [pl.BlockSpec(memory_space=pltpu.SMEM)],
        out_specs=any_spec,
        scratch_shapes=[
            pltpu.VMEM((row_group, quarter, x_count * width), hidden.dtype),
            pltpu.VMEM((weight_group,) + weight.shape, weight.dtype),
            pltpu.VMEM((row_group,) + ids.shape, ids.dtype),
            pltpu.VMEM((x_count, quarter, width), hidden.dtype),
            pltpu.VMEM((x_count,) + gain.shape, gain.dtype),
            pltpu.VMEM((quarter, x_count * width), hidden.dtype),
            pltpu.VMEM((row_group, 8, 128), jnp.float32),
            pltpu.VMEM((row_group, 8, 128), jnp.float32),
            pltpu.VMEM((8, 128), jnp.float32),
            pltpu.VMEM((ids.shape[1], 8), jnp.float32),
            pltpu.SemaphoreType.DMA((x_count - 1,)),
            pltpu.SemaphoreType.DMA((x_count,)),
            pltpu.SemaphoreType.DMA((x_count - 1,)),
            pltpu.SemaphoreType.DMA((x_count,)),
            pltpu.SemaphoreType.DMA((row_group - 1,)),
            pltpu.SemaphoreType.DMA((row_group,)),
            pltpu.SemaphoreType.DMA((weight_group - 1,)),
            pltpu.SemaphoreType.DMA((weight_group,)),
            pltpu.SemaphoreType.DMA((row_group - 1,)),
            pltpu.SemaphoreType.DMA((row_group,)),
            pltpu.SemaphoreType.DMA((5,)),
            pltpu.SemaphoreType.DMA((row_group,)),
            pltpu.SemaphoreType.DMA((row_group,)),
            pltpu.SemaphoreType.DMA((x_count - 1,)),
            pltpu.SemaphoreType.DMA((x_count,)),
            pltpu.SemaphoreType.DMA((2,)),
        ],
        compiler_params=pltpu.CompilerParams(collective_id=0, has_side_effects=True),
    )(hidden, gain, weight, ids, lengths)


def per_device(hidden, norm_gain, head_weight, target_ids, seq_lengths):
    x_count = lax.axis_size("x")
    y_count = lax.axis_size("y")
    z_count = lax.axis_size("z")
    c_count = lax.axis_size("c")
    x_index = lax.axis_index("x")
    y_index = lax.axis_index("y")
    z_index = lax.axis_index("z")
    c_index = lax.axis_index("c")
    vert_count = y_count * z_count * c_count
    vert_index = (y_index * z_count + z_index) * c_count + c_index
    tok_local = hidden.shape[0]
    quarter = tok_local // x_count
    vocab_local = head_weight.shape[1]
    group_count = z_count * c_count

    results = score_all(
        hidden, norm_gain.reshape(1, -1), head_weight, target_ids.reshape(1, -1), seq_lengths,
        x_count, group_count, x_count * y_count, vocab_local,
    )
    full_logprob = results[:, 0, :quarter].reshape(-1)
    full_entropy = results[:, 1, :quarter].reshape(-1)
    return (full_logprob, full_entropy)


def solution(mesh):
    wa_count, vert_count = mesh.devices.shape
    y_count = 4
    c_count = 2
    z_count = vert_count // (y_count * c_count)
    fine = Mesh(mesh.devices.reshape(wa_count, y_count, z_count, c_count), ("x",) + VERT)
    in_specs = (P(VERT, "x"), P("x"), P("x", VERT), P(VERT), P())
    out_specs = (P(VERT), P(VERT))
    return jax.shard_map(
        per_device, mesh=fine, in_specs=in_specs, out_specs=out_specs, check_vma=False
    )
```

```python
import functools

import jax
import jax.numpy as jnp
from jax import lax
from jax.experimental import pallas as pl
from jax.experimental.pallas import tpu as pltpu
from jax.sharding import Mesh
from jax.sharding import PartitionSpec as P

D = 1024
SHORT = 128


norm_epsilon = 1e-06

VERT = ("y", "z", "c")
TOKEN_AXES = ("z", "c")


def live_mask(positions, seq_lengths, long_len, short_len):
    is_long = positions < long_len
    beyond = jnp.maximum(positions - long_len, 0)
    seq_index = jnp.where(is_long, 0, 1 + beyond // short_len)
    offset = jnp.where(is_long, positions, beyond % short_len)
    return offset < jnp.take(seq_lengths, seq_index)


MESH_IDS = pl.DeviceIdType.MESH


def fused_kernel(
    vocab_local, hidden_ref, gain_ref, weight_ref, ids_ref, lengths_ref, results_out,
    normed_out, weight_out, ids_out, piece_vmem, gain_vmem, normed_vmem,
    spread, merged, result, ids_turned,
    piece_send, piece_recv, gain_send, gain_recv,
    row_send, row_recv, weight_send, weight_recv, id_send, id_recv, own_sems,
    first_send, first_recv, second_send, second_recv, stat_sems,
):
    x_count = lax.axis_size("x")
    y_count = lax.axis_size("y")
    z_count = lax.axis_size("z")
    c_count = lax.axis_size("c")
    x_index = lax.axis_index("x")
    y_index = lax.axis_index("y")
    z_index = lax.axis_index("z")
    c_index = lax.axis_index("c")
    row_group = z_count * c_count
    weight_group = x_count * y_count
    row_rank = z_index * c_count + c_index
    weight_rank = x_index * y_count + y_index
    other_core = 1 - c_index

    def row_peer(step):
        rank = lax.rem(row_rank + step, row_group)
        return (x_index, y_index, rank // c_count, rank % c_count)

    def weight_peer(step):
        rank = lax.rem(weight_rank + step, weight_group)
        return rank, (rank // y_count, rank % y_count, z_index, c_index)

    def ring_z(shift):
        return lax.rem(z_index + shift + z_count, z_count)

    barrier = pltpu.get_barrier_semaphore()
    for step in range(1, row_group):
        pl.semaphore_signal(barrier, inc=1, device_id=row_peer(step), device_id_type=MESH_IDS)
    for step in range(1, weight_group):
        pl.semaphore_signal(barrier, inc=1, device_id=weight_peer(step)[1], device_id_type=MESH_IDS)
    pl.semaphore_wait(barrier, row_group - 1 + weight_group - 1)

    quarter = piece_vmem.shape[1]
    width = piece_vmem.shape[2]

    def x_peer(step):
        return (lax.rem(x_index + step, x_count), y_index, z_index, c_index)

    own_piece = pltpu.make_async_copy(
        hidden_ref.at[pl.ds(x_index * quarter, quarter)], piece_vmem.at[x_index], own_sems.at[3]
    )
    own_gain = pltpu.make_async_copy(gain_ref, gain_vmem.at[pl.ds(x_index * width, width)], own_sems.at[4])
    own_piece.start()
    own_gain.start()
    piece_copies = []
    for step in range(1, x_count):
        target = lax.rem(x_index + step, x_count)
        for src, dst, send_sem, recv_sem in (
            (hidden_ref.at[pl.ds(target * quarter, quarter)], piece_vmem, piece_send, piece_recv),
            (gain_ref, gain_vmem, gain_send, gain_recv),
        ):
            copy = pltpu.make_async_remote_copy(
                src_ref=src, dst_ref=dst.at[x_index] if dst is piece_vmem else dst.at[pl.ds(x_index * width, width)],
                send_sem=send_sem.at[step - 1], recv_sem=recv_sem.at[x_index],
                device_id=x_peer(step), device_id_type=MESH_IDS,
            )
            copy.start()
            piece_copies.append(copy)

    own = [
        pltpu.make_async_copy(weight_ref, weight_out.at[weight_rank], own_sems.at[1]),
        pltpu.make_async_copy(ids_ref, ids_out.at[row_rank], own_sems.at[2]),
    ]
    for copy in own:
        copy.start()

    sends = []

    def send_row(source_z, device, sem_index, from_input):
        slot = source_z * c_count + c_index
        copy = pltpu.make_async_remote_copy(
            src_ref=normed_out.at[slot],
            dst_ref=normed_out.at[slot],
            send_sem=row_send.at[sem_index], recv_sem=row_recv.at[slot],
            device_id=device, device_id_type=MESH_IDS,
        )
        copy.start()
        sends.append(copy)

    def wait_row(source_z, source_core):
        slot = source_z * c_count + source_core
        pltpu.make_async_remote_copy(
            src_ref=normed_out.at[slot], dst_ref=normed_out.at[slot],
            send_sem=row_send.at[0], recv_sem=row_recv.at[slot],
            device_id=(x_index, y_index, z_index, other_core), device_id_type=MESH_IDS,
        ).wait_recv()

    right = (x_index, y_index, ring_z(1), c_index)
    left = (x_index, y_index, ring_z(-1), c_index)
    partner = (x_index, y_index, z_index, other_core)
    right_steps = z_count // 2
    left_steps = z_count - 1 - right_steps
    sem_count = [0]

    def next_sem():
        sem_count[0] += 1
        return sem_count[0] - 1

    for step in range(1, weight_group):
        _, device = weight_peer(step)
        copy = pltpu.make_async_remote_copy(
            src_ref=weight_ref, dst_ref=weight_out.at[weight_rank],
            send_sem=weight_send.at[step - 1], recv_sem=weight_recv.at[weight_rank],
            device_id=device, device_id_type=MESH_IDS,
        )
        copy.start()
        sends.append(copy)
    for step in range(1, row_group):
        copy = pltpu.make_async_remote_copy(
            src_ref=ids_ref, dst_ref=ids_out.at[row_rank],
            send_sem=id_send.at[step - 1], recv_sem=id_recv.at[row_rank],
            device_id=row_peer(step), device_id_type=MESH_IDS,
        )
        copy.start()
        sends.append(copy)

    own_piece.wait()
    own_gain.wait()
    for step in range(1, x_count):
        source = lax.rem(x_index + x_count - step, x_count)
        for src, dst, send_sem, recv_sem in (
            (hidden_ref.at[pl.ds(0, quarter)], piece_vmem, piece_send, piece_recv),
            (gain_ref, gain_vmem, gain_send, gain_recv),
        ):
            pltpu.make_async_remote_copy(
                src_ref=src, dst_ref=dst.at[source] if dst is piece_vmem else dst.at[pl.ds(source * width, width)],
                send_sem=send_sem.at[step - 1], recv_sem=recv_sem.at[source],
                device_id=x_peer(x_count - step), device_id_type=MESH_IDS,
            ).wait_recv()
    squares = jnp.zeros((quarter, 1), jnp.float32)
    for part in range(x_count):
        values = piece_vmem[part].astype(jnp.float32)
        squares = squares + jnp.sum(values * values, axis=1, keepdims=True)
    scale = lax.rsqrt(squares / (x_count * width) + norm_epsilon)
    for part in range(x_count):
        values = piece_vmem[part].astype(jnp.float32)
        gain = gain_vmem[pl.ds(part * width, width)].astype(jnp.float32).reshape(1, width)
        normed_vmem[:, part * width:(part + 1) * width] = (values * scale * gain).astype(normed_vmem.dtype)
    own_row = pltpu.make_async_copy(normed_vmem, normed_out.at[row_rank], own_sems.at[0])
    own_row.start()
    own_row.wait()

    send_row(z_index, right, next_sem(), True)
    if left_steps > 0:
        send_row(z_index, left, next_sem(), True)
    send_row(z_index, partner, next_sem(), True)

    for step in range(1, right_steps + 1):
        from_left = ring_z(-step)
        wait_row(from_left, c_index)
        if step < right_steps:
            send_row(from_left, right, next_sem(), False)
        send_row(from_left, partner, next_sem(), False)
        if step <= left_steps:
            from_right = ring_z(step)
            wait_row(from_right, c_index)
            if step < left_steps:
                send_row(from_right, left, next_sem(), False)
            send_row(from_right, partner, next_sem(), False)

    for copy in own:
        copy.wait()
    for step in range(z_count):
        wait_row(lax.rem(z_index + step, z_count), other_core)
    for step in range(1, weight_group):
        source = lax.rem(weight_rank + weight_group - step, weight_group)
        pltpu.make_async_remote_copy(
            src_ref=weight_ref, dst_ref=weight_out.at[source],
            send_sem=weight_send.at[0], recv_sem=weight_recv.at[source],
            device_id=weight_peer(step)[1], device_id_type=MESH_IDS,
        ).wait_recv()
    for step in range(1, row_group):
        source = lax.rem(row_rank + row_group - step, row_group)
        pltpu.make_async_remote_copy(
            src_ref=ids_ref, dst_ref=ids_out.at[source],
            send_sem=id_send.at[0], recv_sem=id_recv.at[source],
            device_id=row_peer(step), device_id_type=MESH_IDS,
        ).wait_recv()

    group = row_group
    rank = row_rank
    width = weight_out.shape[1]
    padded = weight_out.shape[2]
    spread[...] = jnp.zeros_like(spread)
    result[...] = jnp.zeros_like(result)

    own_stats = pltpu.make_async_copy(spread.at[rank], merged.at[rank], stat_sems.at[0])

    def stats_copy(slot):
        return pltpu.make_async_remote_copy(
            src_ref=spread.at[slot], dst_ref=merged.at[rank],
            send_sem=first_send.at[slot], recv_sem=first_recv.at[rank],
            device_id=(x_index, y_index, slot // c_count, slot % c_count), device_id_type=MESH_IDS,
        )

    def send_chunk(first_slot):
        for slot in range(first_slot, first_slot + slots_per_chunk):

            @pl.when(slot != rank)
            def _():
                stats_copy(slot).start()

            @pl.when(slot == rank)
            def _():
                own_stats.start()

    chunk = 256
    slots_per_chunk = chunk // quarter
    column = lax.broadcasted_iota(jnp.int32, (chunk, padded), 1)
    valid = column < vocab_local
    lane = lax.broadcasted_iota(jnp.int32, (chunk, 128), 1)
    for first in range(0, normed_out.shape[0] * quarter, chunk):
        blocks = []
        for y_block in range(y_count):
            total = jnp.zeros((chunk, padded), jnp.float32)
            for x_block in range(x_count):
                rows = normed_out[first // quarter:(first + chunk) // quarter, :, x_block * width:(x_block + 1) * width]
                total = total + jnp.dot(
                    rows.reshape(chunk, width),
                    weight_out[x_block * y_count + y_block],
                    preferred_element_type=jnp.float32,
                )
            blocks.append(total)
        id_rows = jnp.concatenate(
            [ids_out[slot] for slot in range(first // quarter, first // quarter + slots_per_chunk)], axis=0
        )
        ids_turned[...] = id_rows.astype(jnp.float32).T
        mine = ids_turned[pl.ds(pl.multiple_of(x_index * quarter, quarter), quarter), :]
        target = jnp.concatenate(
            [mine[:, part:part + 1] for part in range(slots_per_chunk)], axis=0
        ).astype(jnp.int32)
        peak = None
        for y_block, block in enumerate(blocks):
            block_peak = jnp.max(jnp.where(valid, block, -jnp.inf), axis=1, keepdims=True)
            peak = block_peak if peak is None else jnp.maximum(peak, block_peak)
        row_sum = jnp.zeros((chunk, 1), jnp.float32)
        row_weighted = jnp.zeros((chunk, 1), jnp.float32)
        row_picked = jnp.zeros((chunk, 1), jnp.float32)
        for y_block, block in enumerate(blocks):
            scaled = jnp.where(valid, jnp.exp(block - peak), 0.0)
            row_sum = row_sum + jnp.sum(scaled, axis=1, keepdims=True)
            row_weighted = row_weighted + jnp.sum(scaled * block, axis=1, keepdims=True)
            global_id = ((y_block * z_count + z_index) * c_count + c_index) * vocab_local + column
            hit = valid & (global_id == target)
            row_picked = row_picked + jnp.sum(jnp.where(hit, block, 0.0), axis=1, keepdims=True)
        table = jnp.where(
            lane == 0, peak,
            jnp.where(lane == 1, row_sum, jnp.where(lane == 2, row_weighted, jnp.where(lane == 3, row_picked, 0.0))),
        )
        lanes = table.T
        for part in range(slots_per_chunk):
            slot = first // quarter + part
            spread[slot, :, 0:quarter] = lanes[0:8, part * quarter:(part + 1) * quarter]
        if first > 0:
            send_chunk(first // quarter - slots_per_chunk)
    send_chunk(group - slots_per_chunk)

    own_stats.wait()

    def finish(step, carry):
        source = lax.rem(rank + group - step, group)
        pltpu.make_async_remote_copy(
            src_ref=spread.at[source], dst_ref=merged.at[source],
            send_sem=first_send.at[source], recv_sem=first_recv.at[source],
            device_id=row_peer(step), device_id_type=MESH_IDS,
        ).wait_recv()
        return carry

    lax.fori_loop(1, group, finish, 0)

    highest = merged[0, 0:1, :]
    for source in range(1, group):
        highest = jnp.maximum(highest, merged[source, 0:1, :])
    totals = jnp.zeros_like(highest)
    weighted = jnp.zeros_like(highest)
    picked = jnp.zeros_like(highest)
    for source in range(group):
        factor = jnp.exp(merged[source, 0:1, :] - highest)
        totals = totals + merged[source, 1:2, :] * factor
        weighted = weighted + merged[source, 2:3, :] * factor
        picked = picked + merged[source, 3:4, :]
    log_norm = highest + jnp.log(totals)

    block_tokens = x_count * quarter
    vert_index = (y_index * z_count + z_index) * c_count + c_index
    long_len = y_count * z_count * c_count * block_tokens // 2
    block_start = vert_index * block_tokens
    in_long = block_start < long_len
    sequence = jnp.where(in_long, 0, 1 + (block_start - long_len) // SHORT)
    live_length = lengths_ref[sequence]
    positions = block_start + x_index * quarter + lax.broadcasted_iota(jnp.int32, (1, 128), 1)
    offsets = jnp.where(in_long, positions, jnp.maximum(positions - long_len, 0) % SHORT)
    live = offsets < live_length
    result[0:1, :] = jnp.where(live, picked - log_norm, 0.0)
    result[1:2, :] = jnp.where(live, log_norm - weighted / totals, 0.0)

    mine = pltpu.make_async_copy(result, results_out.at[x_index], stat_sems.at[1])
    mine.start()
    copies = []
    for step in range(1, x_count):
        copy = pltpu.make_async_remote_copy(
            src_ref=result, dst_ref=results_out.at[x_index],
            send_sem=second_send.at[step - 1], recv_sem=second_recv.at[x_index],
            device_id=x_peer(step), device_id_type=MESH_IDS,
        )
        copy.start()
        copies.append(copy)
    mine.wait()
    for step in range(1, x_count):
        copies[step - 1].wait_send()
        source = lax.rem(x_index + x_count - step, x_count)
        pltpu.make_async_remote_copy(
            src_ref=result, dst_ref=results_out.at[source],
            send_sem=second_send.at[step - 1], recv_sem=second_recv.at[source],
            device_id=x_peer(x_count - step), device_id_type=MESH_IDS,
        ).wait_recv()
    for copy in sends + piece_copies:
        copy.wait_send()
    for slot in range(group):

        @pl.when(slot != rank)
        def _():
            stats_copy(slot).wait_send()


def score_all(hidden, gain, weight, ids, lengths, x_count, row_group, weight_group, vocab_local):
    quarter = hidden.shape[0] // x_count
    width = hidden.shape[1]
    any_spec = pl.BlockSpec(memory_space=pl.ANY)
    return pl.pallas_call(
        functools.partial(fused_kernel, vocab_local),
        out_shape=jax.ShapeDtypeStruct((x_count, 8, 128), jnp.float32),
        in_specs=[any_spec] * 4 + [pl.BlockSpec(memory_space=pltpu.SMEM)],
        out_specs=any_spec,
        scratch_shapes=[
            pltpu.VMEM((row_group, quarter, x_count * width), hidden.dtype),
            pltpu.VMEM((weight_group,) + weight.shape, weight.dtype),
            pltpu.VMEM((row_group,) + ids.shape, ids.dtype),
            pltpu.VMEM((x_count, quarter, width), hidden.dtype),
            pltpu.VMEM((x_count * gain.shape[0],), gain.dtype),
            pltpu.VMEM((quarter, x_count * width), hidden.dtype),
            pltpu.VMEM((row_group, 8, 128), jnp.float32),
            pltpu.VMEM((row_group, 8, 128), jnp.float32),
            pltpu.VMEM((8, 128), jnp.float32),
            pltpu.VMEM((ids.shape[1], 8), jnp.float32),
            pltpu.SemaphoreType.DMA((x_count - 1,)),
            pltpu.SemaphoreType.DMA((x_count,)),
            pltpu.SemaphoreType.DMA((x_count - 1,)),
            pltpu.SemaphoreType.DMA((x_count,)),
            pltpu.SemaphoreType.DMA((row_group - 1,)),
            pltpu.SemaphoreType.DMA((row_group,)),
            pltpu.SemaphoreType.DMA((weight_group - 1,)),
            pltpu.SemaphoreType.DMA((weight_group,)),
            pltpu.SemaphoreType.DMA((row_group - 1,)),
            pltpu.SemaphoreType.DMA((row_group,)),
            pltpu.SemaphoreType.DMA((5,)),
            pltpu.SemaphoreType.DMA((row_group,)),
            pltpu.SemaphoreType.DMA((row_group,)),
            pltpu.SemaphoreType.DMA((x_count - 1,)),
            pltpu.SemaphoreType.DMA((x_count,)),
            pltpu.SemaphoreType.DMA((2,)),
        ],
        compiler_params=pltpu.CompilerParams(collective_id=0, has_side_effects=True),
    )(hidden, gain, weight, ids, lengths)


def per_device(hidden, norm_gain, head_weight, target_ids, seq_lengths):
    x_count = lax.axis_size("x")
    y_count = lax.axis_size("y")
    z_count = lax.axis_size("z")
    c_count = lax.axis_size("c")
    x_index = lax.axis_index("x")
    y_index = lax.axis_index("y")
    z_index = lax.axis_index("z")
    c_index = lax.axis_index("c")
    vert_count = y_count * z_count * c_count
    vert_index = (y_index * z_count + z_index) * c_count + c_index
    tok_local = hidden.shape[0]
    quarter = tok_local // x_count
    vocab_local = head_weight.shape[1]
    group_count = z_count * c_count

    results = score_all(
        hidden, norm_gain, head_weight, target_ids.reshape(1, -1), seq_lengths,
        x_count, group_count, x_count * y_count, vocab_local,
    )
    full_logprob = results[:, 0, :quarter].reshape(-1)
    full_entropy = results[:, 1, :quarter].reshape(-1)
    return (full_logprob, full_entropy)


def solution(mesh):
    wa_count, vert_count = mesh.devices.shape
    y_count = 4
    c_count = 2
    z_count = vert_count // (y_count * c_count)
    fine = Mesh(mesh.devices.reshape(wa_count, y_count, z_count, c_count), ("x",) + VERT)
    in_specs = (P(VERT, "x"), P("x"), P("x", VERT), P(VERT), P())
    out_specs = (P(VERT), P(VERT))
    return jax.shard_map(
        per_device, mesh=fine, in_specs=in_specs, out_specs=out_specs, check_vma=False
    )
```

```python
import functools

import jax
import jax.numpy as jnp
from jax import lax
from jax.experimental import pallas as pl
from jax.experimental.pallas import tpu as pltpu
from jax.sharding import Mesh
from jax.sharding import PartitionSpec as P

D = 1024
SHORT = 128


norm_epsilon = 1e-06

VERT = ("y", "z", "c")
TOKEN_AXES = ("z", "c")


def live_mask(positions, seq_lengths, long_len, short_len):
    is_long = positions < long_len
    beyond = jnp.maximum(positions - long_len, 0)
    seq_index = jnp.where(is_long, 0, 1 + beyond // short_len)
    offset = jnp.where(is_long, positions, beyond % short_len)
    return offset < jnp.take(seq_lengths, seq_index)


MESH_IDS = pl.DeviceIdType.MESH


def fused_kernel(
    vocab_local, hidden_ref, gain_ref, weight_ref, ids_ref, lengths_ref, results_out,
    normed_out, weight_out, ids_out, piece_vmem, gain_vmem, normed_vmem,
    spread, merged, result, ids_turned,
    piece_send, piece_recv, gain_send, gain_recv,
    row_send, row_recv, weight_send, weight_recv, id_send, id_recv, own_sems,
    first_send, first_recv, second_send, second_recv, stat_sems,
):
    x_count = lax.axis_size("x")
    y_count = lax.axis_size("y")
    z_count = lax.axis_size("z")
    c_count = lax.axis_size("c")
    x_index = lax.axis_index("x")
    y_index = lax.axis_index("y")
    z_index = lax.axis_index("z")
    c_index = lax.axis_index("c")
    row_group = z_count * c_count
    weight_group = x_count * y_count
    row_rank = z_index * c_count + c_index
    weight_rank = x_index * y_count + y_index
    other_core = 1 - c_index

    def row_peer(step):
        rank = lax.rem(row_rank + step, row_group)
        return (x_index, y_index, rank // c_count, rank % c_count)

    def weight_peer(step):
        rank = lax.rem(weight_rank + step, weight_group)
        return rank, (rank // y_count, rank % y_count, z_index, c_index)

    def ring_z(shift):
        return lax.rem(z_index + shift + z_count, z_count)

    barrier = pltpu.get_barrier_semaphore()
    for step in range(1, row_group):
        pl.semaphore_signal(barrier, inc=1, device_id=row_peer(step), device_id_type=MESH_IDS)
    for step in range(1, weight_group):
        pl.semaphore_signal(barrier, inc=1, device_id=weight_peer(step)[1], device_id_type=MESH_IDS)
    pl.semaphore_wait(barrier, row_group - 1 + weight_group - 1)

    quarter = piece_vmem.shape[1]
    width = piece_vmem.shape[2]

    def x_peer(step):
        return (lax.rem(x_index + step, x_count), y_index, z_index, c_index)

    own_piece = pltpu.make_async_copy(
        hidden_ref.at[pl.ds(x_index * quarter, quarter)], piece_vmem.at[x_index], own_sems.at[3]
    )
    own_gain = pltpu.make_async_copy(gain_ref, gain_vmem.at[pl.ds(x_index * width, width)], own_sems.at[4])
    own_piece.start()
    own_gain.start()
    piece_copies = []
    for step in range(1, x_count):
        target = lax.rem(x_index + step, x_count)
        for src, dst, send_sem, recv_sem in (
            (hidden_ref.at[pl.ds(target * quarter, quarter)], piece_vmem, piece_send, piece_recv),
            (gain_ref, gain_vmem, gain_send, gain_recv),
        ):
            copy = pltpu.make_async_remote_copy(
                src_ref=src, dst_ref=dst.at[x_index] if dst is piece_vmem else dst.at[pl.ds(x_index * width, width)],
                send_sem=send_sem.at[step - 1], recv_sem=recv_sem.at[x_index],
                device_id=x_peer(step), device_id_type=MESH_IDS,
            )
            copy.start()
            piece_copies.append(copy)

    own = [
        pltpu.make_async_copy(weight_ref, weight_out.at[weight_rank], own_sems.at[1]),
        pltpu.make_async_copy(ids_ref, ids_out.at[row_rank], own_sems.at[2]),
    ]
    for copy in own:
        copy.start()

    sends = []

    def send_row(source_z, device, sem_index, from_input):
        slot = source_z * c_count + c_index
        copy = pltpu.make_async_remote_copy(
            src_ref=normed_out.at[slot],
            dst_ref=normed_out.at[slot],
            send_sem=row_send.at[sem_index], recv_sem=row_recv.at[slot],
            device_id=device, device_id_type=MESH_IDS,
        )
        copy.start()
        sends.append(copy)

    def wait_row(source_z, source_core):
        slot = source_z * c_count + source_core
        pltpu.make_async_remote_copy(
            src_ref=normed_out.at[slot], dst_ref=normed_out.at[slot],
            send_sem=row_send.at[0], recv_sem=row_recv.at[slot],
            device_id=(x_index, y_index, z_index, other_core), device_id_type=MESH_IDS,
        ).wait_recv()

    right = (x_index, y_index, ring_z(1), c_index)
    left = (x_index, y_index, ring_z(-1), c_index)
    partner = (x_index, y_index, z_index, other_core)
    right_steps = z_count // 2
    left_steps = z_count - 1 - right_steps
    sem_count = [0]

    def next_sem():
        sem_count[0] += 1
        return sem_count[0] - 1

    for step in range(1, weight_group):
        _, device = weight_peer(step)
        copy = pltpu.make_async_remote_copy(
            src_ref=weight_ref, dst_ref=weight_out.at[weight_rank],
            send_sem=weight_send.at[step - 1], recv_sem=weight_recv.at[weight_rank],
            device_id=device, device_id_type=MESH_IDS,
        )
        copy.start()
        sends.append(copy)
    for step in range(1, row_group):
        copy = pltpu.make_async_remote_copy(
            src_ref=ids_ref, dst_ref=ids_out.at[row_rank],
            send_sem=id_send.at[step - 1], recv_sem=id_recv.at[row_rank],
            device_id=row_peer(step), device_id_type=MESH_IDS,
        )
        copy.start()
        sends.append(copy)

    own_piece.wait()
    own_gain.wait()
    for step in range(1, x_count):
        source = lax.rem(x_index + x_count - step, x_count)
        for src, dst, send_sem, recv_sem in (
            (hidden_ref.at[pl.ds(0, quarter)], piece_vmem, piece_send, piece_recv),
            (gain_ref, gain_vmem, gain_send, gain_recv),
        ):
            pltpu.make_async_remote_copy(
                src_ref=src, dst_ref=dst.at[source] if dst is piece_vmem else dst.at[pl.ds(source * width, width)],
                send_sem=send_sem.at[step - 1], recv_sem=recv_sem.at[source],
                device_id=x_peer(x_count - step), device_id_type=MESH_IDS,
            ).wait_recv()
    squares = jnp.zeros((quarter, 1), jnp.float32)
    for part in range(x_count):
        values = piece_vmem[part].astype(jnp.float32)
        squares = squares + jnp.sum(values * values, axis=1, keepdims=True)
    scale = lax.rsqrt(squares / (x_count * width) + norm_epsilon)
    for part in range(x_count):
        values = piece_vmem[part].astype(jnp.float32)
        gain = gain_vmem[pl.ds(part * width, width)].astype(jnp.float32).reshape(1, width)
        normed_vmem[:, part * width:(part + 1) * width] = (values * scale * gain).astype(normed_vmem.dtype)
    own_row = pltpu.make_async_copy(normed_vmem, normed_out.at[row_rank], own_sems.at[0])
    own_row.start()
    own_row.wait()

    send_row(z_index, right, next_sem(), True)
    if left_steps > 0:
        send_row(z_index, left, next_sem(), True)
    send_row(z_index, partner, next_sem(), True)

    for step in range(1, right_steps + 1):
        from_left = ring_z(-step)
        wait_row(from_left, c_index)
        if step < right_steps:
            send_row(from_left, right, next_sem(), False)
        send_row(from_left, partner, next_sem(), False)
        if step <= left_steps:
            from_right = ring_z(step)
            wait_row(from_right, c_index)
            if step < left_steps:
                send_row(from_right, left, next_sem(), False)
            send_row(from_right, partner, next_sem(), False)

    for copy in own:
        copy.wait()
    for step in range(z_count):
        wait_row(lax.rem(z_index + step, z_count), other_core)
    for step in range(1, weight_group):
        source = lax.rem(weight_rank + weight_group - step, weight_group)
        pltpu.make_async_remote_copy(
            src_ref=weight_ref, dst_ref=weight_out.at[source],
            send_sem=weight_send.at[0], recv_sem=weight_recv.at[source],
            device_id=weight_peer(step)[1], device_id_type=MESH_IDS,
        ).wait_recv()
    for step in range(1, row_group):
        source = lax.rem(row_rank + row_group - step, row_group)
        pltpu.make_async_remote_copy(
            src_ref=ids_ref, dst_ref=ids_out.at[source],
            send_sem=id_send.at[0], recv_sem=id_recv.at[source],
            device_id=row_peer(step), device_id_type=MESH_IDS,
        ).wait_recv()

    group = row_group
    rank = row_rank
    width = weight_out.shape[1]
    padded = weight_out.shape[2]
    spread[...] = jnp.zeros_like(spread)
    result[...] = jnp.zeros_like(result)

    own_stats = pltpu.make_async_copy(spread.at[rank], merged.at[rank], stat_sems.at[0])

    def stats_copy(slot):
        return pltpu.make_async_remote_copy(
            src_ref=spread.at[slot], dst_ref=merged.at[rank],
            send_sem=first_send.at[slot], recv_sem=first_recv.at[rank],
            device_id=(x_index, y_index, slot // c_count, slot % c_count), device_id_type=MESH_IDS,
        )

    def send_chunk(first_slot):
        for slot in range(first_slot, first_slot + slots_per_chunk):

            @pl.when(slot != rank)
            def _():
                stats_copy(slot).start()

            @pl.when(slot == rank)
            def _():
                own_stats.start()

    chunk = 128
    slots_per_chunk = chunk // quarter
    column = lax.broadcasted_iota(jnp.int32, (chunk, padded), 1)
    valid = column < vocab_local
    lane = lax.broadcasted_iota(jnp.int32, (chunk, 128), 1)
    for first in range(0, normed_out.shape[0] * quarter, chunk):
        blocks = []
        for y_block in range(y_count):
            total = jnp.zeros((chunk, padded), jnp.float32)
            for x_block in range(x_count):
                rows = normed_out[first // quarter:(first + chunk) // quarter, :, x_block * width:(x_block + 1) * width]
                total = total + jnp.dot(
                    rows.reshape(chunk, width),
                    weight_out[x_block * y_count + y_block],
                    preferred_element_type=jnp.float32,
                )
            blocks.append(total)
        id_rows = jnp.concatenate(
            [ids_out[slot] for slot in range(first // quarter, first // quarter + slots_per_chunk)], axis=0
        )
        ids_turned[...] = id_rows.astype(jnp.float32).T
        mine = ids_turned[pl.ds(pl.multiple_of(x_index * quarter, quarter), quarter), :]
        target = jnp.concatenate(
            [mine[:, part:part + 1] for part in range(slots_per_chunk)], axis=0
        ).astype(jnp.int32)
        peak = None
        for y_block, block in enumerate(blocks):
            block_peak = jnp.max(jnp.where(valid, block, -jnp.inf), axis=1, keepdims=True)
            peak = block_peak if peak is None else jnp.maximum(peak, block_peak)
        row_sum = jnp.zeros((chunk, 1), jnp.float32)
        row_weighted = jnp.zeros((chunk, 1), jnp.float32)
        row_picked = jnp.zeros((chunk, 1), jnp.float32)
        for y_block, block in enumerate(blocks):
            scaled = jnp.where(valid, jnp.exp(block - peak), 0.0)
            row_sum = row_sum + jnp.sum(scaled, axis=1, keepdims=True)
            row_weighted = row_weighted + jnp.sum(scaled * block, axis=1, keepdims=True)
            global_id = ((y_block * z_count + z_index) * c_count + c_index) * vocab_local + column
            hit = valid & (global_id == target)
            row_picked = row_picked + jnp.sum(jnp.where(hit, block, 0.0), axis=1, keepdims=True)
        table = jnp.where(
            lane == 0, peak,
            jnp.where(lane == 1, row_sum, jnp.where(lane == 2, row_weighted, jnp.where(lane == 3, row_picked, 0.0))),
        )
        lanes = table.T
        for part in range(slots_per_chunk):
            slot = first // quarter + part
            spread[slot, :, 0:quarter] = lanes[0:8, part * quarter:(part + 1) * quarter]
        if first > 0:
            send_chunk(first // quarter - slots_per_chunk)
    send_chunk(group - slots_per_chunk)

    own_stats.wait()

    def finish(step, carry):
        source = lax.rem(rank + group - step, group)
        pltpu.make_async_remote_copy(
            src_ref=spread.at[source], dst_ref=merged.at[source],
            send_sem=first_send.at[source], recv_sem=first_recv.at[source],
            device_id=row_peer(step), device_id_type=MESH_IDS,
        ).wait_recv()
        return carry

    lax.fori_loop(1, group, finish, 0)

    highest = merged[0, 0:1, :]
    for source in range(1, group):
        highest = jnp.maximum(highest, merged[source, 0:1, :])
    totals = jnp.zeros_like(highest)
    weighted = jnp.zeros_like(highest)
    picked = jnp.zeros_like(highest)
    for source in range(group):
        factor = jnp.exp(merged[source, 0:1, :] - highest)
        totals = totals + merged[source, 1:2, :] * factor
        weighted = weighted + merged[source, 2:3, :] * factor
        picked = picked + merged[source, 3:4, :]
    log_norm = highest + jnp.log(totals)

    block_tokens = x_count * quarter
    vert_index = (y_index * z_count + z_index) * c_count + c_index
    long_len = y_count * z_count * c_count * block_tokens // 2
    block_start = vert_index * block_tokens
    in_long = block_start < long_len
    sequence = jnp.where(in_long, 0, 1 + (block_start - long_len) // SHORT)
    live_length = lengths_ref[sequence]
    positions = block_start + x_index * quarter + lax.broadcasted_iota(jnp.int32, (1, 128), 1)
    offsets = jnp.where(in_long, positions, jnp.maximum(positions - long_len, 0) % SHORT)
    live = offsets < live_length
    result[0:1, :] = jnp.where(live, picked - log_norm, 0.0)
    result[1:2, :] = jnp.where(live, log_norm - weighted / totals, 0.0)

    mine = pltpu.make_async_copy(result, results_out.at[x_index], stat_sems.at[1])
    mine.start()
    copies = []
    for step in range(1, x_count):
        copy = pltpu.make_async_remote_copy(
            src_ref=result, dst_ref=results_out.at[x_index],
            send_sem=second_send.at[step - 1], recv_sem=second_recv.at[x_index],
            device_id=x_peer(step), device_id_type=MESH_IDS,
        )
        copy.start()
        copies.append(copy)
    mine.wait()
    for step in range(1, x_count):
        copies[step - 1].wait_send()
        source = lax.rem(x_index + x_count - step, x_count)
        pltpu.make_async_remote_copy(
            src_ref=result, dst_ref=results_out.at[source],
            send_sem=second_send.at[step - 1], recv_sem=second_recv.at[source],
            device_id=x_peer(x_count - step), device_id_type=MESH_IDS,
        ).wait_recv()
    for copy in sends + piece_copies:
        copy.wait_send()
    for slot in range(group):

        @pl.when(slot != rank)
        def _():
            stats_copy(slot).wait_send()


def score_all(hidden, gain, weight, ids, lengths, x_count, row_group, weight_group, vocab_local):
    quarter = hidden.shape[0] // x_count
    width = hidden.shape[1]
    any_spec = pl.BlockSpec(memory_space=pl.ANY)
    return pl.pallas_call(
        functools.partial(fused_kernel, vocab_local),
        out_shape=jax.ShapeDtypeStruct((x_count, 8, 128), jnp.float32),
        in_specs=[any_spec] * 4 + [pl.BlockSpec(memory_space=pltpu.SMEM)],
        out_specs=any_spec,
        scratch_shapes=[
            pltpu.VMEM((row_group, quarter, x_count * width), hidden.dtype),
            pltpu.VMEM((weight_group,) + weight.shape, weight.dtype),
            pltpu.VMEM((row_group,) + ids.shape, ids.dtype),
            pltpu.VMEM((x_count, quarter, width), hidden.dtype),
            pltpu.VMEM((x_count * gain.shape[0],), gain.dtype),
            pltpu.VMEM((quarter, x_count * width), hidden.dtype),
            pltpu.VMEM((row_group, 8, 128), jnp.float32),
            pltpu.VMEM((row_group, 8, 128), jnp.float32),
            pltpu.VMEM((8, 128), jnp.float32),
            pltpu.VMEM((ids.shape[1], 4), jnp.float32),
            pltpu.SemaphoreType.DMA((x_count - 1,)),
            pltpu.SemaphoreType.DMA((x_count,)),
            pltpu.SemaphoreType.DMA((x_count - 1,)),
            pltpu.SemaphoreType.DMA((x_count,)),
            pltpu.SemaphoreType.DMA((row_group - 1,)),
            pltpu.SemaphoreType.DMA((row_group,)),
            pltpu.SemaphoreType.DMA((weight_group - 1,)),
            pltpu.SemaphoreType.DMA((weight_group,)),
            pltpu.SemaphoreType.DMA((row_group - 1,)),
            pltpu.SemaphoreType.DMA((row_group,)),
            pltpu.SemaphoreType.DMA((5,)),
            pltpu.SemaphoreType.DMA((row_group,)),
            pltpu.SemaphoreType.DMA((row_group,)),
            pltpu.SemaphoreType.DMA((x_count - 1,)),
            pltpu.SemaphoreType.DMA((x_count,)),
            pltpu.SemaphoreType.DMA((2,)),
        ],
        compiler_params=pltpu.CompilerParams(collective_id=0, has_side_effects=True),
    )(hidden, gain, weight, ids, lengths)


def per_device(hidden, norm_gain, head_weight, target_ids, seq_lengths):
    x_count = lax.axis_size("x")
    y_count = lax.axis_size("y")
    z_count = lax.axis_size("z")
    c_count = lax.axis_size("c")
    x_index = lax.axis_index("x")
    y_index = lax.axis_index("y")
    z_index = lax.axis_index("z")
    c_index = lax.axis_index("c")
    vert_count = y_count * z_count * c_count
    vert_index = (y_index * z_count + z_index) * c_count + c_index
    tok_local = hidden.shape[0]
    quarter = tok_local // x_count
    vocab_local = head_weight.shape[1]
    group_count = z_count * c_count

    results = score_all(
        hidden, norm_gain, head_weight, target_ids.reshape(1, -1), seq_lengths,
        x_count, group_count, x_count * y_count, vocab_local,
    )
    full_logprob = results[:, 0, :quarter].reshape(-1)
    full_entropy = results[:, 1, :quarter].reshape(-1)
    return (full_logprob, full_entropy)


def solution(mesh):
    wa_count, vert_count = mesh.devices.shape
    y_count = 4
    c_count = 2
    z_count = vert_count // (y_count * c_count)
    fine = Mesh(mesh.devices.reshape(wa_count, y_count, z_count, c_count), ("x",) + VERT)
    in_specs = (P(VERT, "x"), P("x"), P("x", VERT), P(VERT), P())
    out_specs = (P(VERT), P(VERT))
    return jax.shard_map(
        per_device, mesh=fine, in_specs=in_specs, out_specs=out_specs, check_vma=False
    )
```

```python
import functools

import jax
import jax.numpy as jnp
from jax import lax
from jax.experimental import pallas as pl
from jax.experimental.pallas import tpu as pltpu
from jax.sharding import Mesh
from jax.sharding import PartitionSpec as P

D = 1024
SHORT = 128


norm_epsilon = 1e-06

VERT = ("y", "z", "c")
TOKEN_AXES = ("z", "c")


def live_mask(positions, seq_lengths, long_len, short_len):
    is_long = positions < long_len
    beyond = jnp.maximum(positions - long_len, 0)
    seq_index = jnp.where(is_long, 0, 1 + beyond // short_len)
    offset = jnp.where(is_long, positions, beyond % short_len)
    return offset < jnp.take(seq_lengths, seq_index)


MESH_IDS = pl.DeviceIdType.MESH


def fused_kernel(
    vocab_local, hidden_ref, gain_ref, weight_ref, ids_ref, lengths_ref, results_out,
    normed_out, weight_out, ids_out, piece_vmem, gain_vmem, normed_vmem,
    spread, merged, result, ids_turned,
    piece_send, piece_recv, gain_send, gain_recv,
    row_send, row_recv, weight_send, weight_recv, id_send, id_recv, own_sems,
    first_send, first_recv, second_send, second_recv, stat_sems,
):
    x_count = lax.axis_size("x")
    y_count = lax.axis_size("y")
    z_count = lax.axis_size("z")
    c_count = lax.axis_size("c")
    x_index = lax.axis_index("x")
    y_index = lax.axis_index("y")
    z_index = lax.axis_index("z")
    c_index = lax.axis_index("c")
    row_group = z_count * c_count
    weight_group = x_count * y_count
    row_rank = z_index * c_count + c_index
    weight_rank = x_index * y_count + y_index
    other_core = 1 - c_index

    def row_peer(step):
        rank = lax.rem(row_rank + step, row_group)
        return (x_index, y_index, rank // c_count, rank % c_count)

    def weight_peer(step):
        rank = lax.rem(weight_rank + step, weight_group)
        return rank, (rank // y_count, rank % y_count, z_index, c_index)

    def ring_z(shift):
        return lax.rem(z_index + shift + z_count, z_count)

    barrier = pltpu.get_barrier_semaphore()
    for step in range(1, row_group):
        pl.semaphore_signal(barrier, inc=1, device_id=row_peer(step), device_id_type=MESH_IDS)
    for step in range(1, weight_group):
        pl.semaphore_signal(barrier, inc=1, device_id=weight_peer(step)[1], device_id_type=MESH_IDS)
    pl.semaphore_wait(barrier, row_group - 1 + weight_group - 1)

    quarter = piece_vmem.shape[1]
    width = piece_vmem.shape[2]

    def x_peer(step):
        return (lax.rem(x_index + step, x_count), y_index, z_index, c_index)

    own_piece = pltpu.make_async_copy(
        hidden_ref.at[pl.ds(x_index * quarter, quarter)], piece_vmem.at[x_index], own_sems.at[3]
    )
    own_gain = pltpu.make_async_copy(gain_ref, gain_vmem.at[pl.ds(x_index * width, width)], own_sems.at[4])
    own_piece.start()
    own_gain.start()
    piece_copies = []
    for step in range(1, x_count):
        target = lax.rem(x_index + step, x_count)
        for src, dst, send_sem, recv_sem in (
            (hidden_ref.at[pl.ds(target * quarter, quarter)], piece_vmem, piece_send, piece_recv),
            (gain_ref, gain_vmem, gain_send, gain_recv),
        ):
            copy = pltpu.make_async_remote_copy(
                src_ref=src, dst_ref=dst.at[x_index] if dst is piece_vmem else dst.at[pl.ds(x_index * width, width)],
                send_sem=send_sem.at[step - 1], recv_sem=recv_sem.at[x_index],
                device_id=x_peer(step), device_id_type=MESH_IDS,
            )
            copy.start()
            piece_copies.append(copy)

    own = [
        pltpu.make_async_copy(weight_ref, weight_out.at[weight_rank], own_sems.at[1]),
        pltpu.make_async_copy(ids_ref, ids_out.at[row_rank], own_sems.at[2]),
    ]
    for copy in own:
        copy.start()

    sends = []

    halves = 2
    half = quarter // halves

    def send_row(source_z, device, sem_index, from_input, parts=range(halves)):
        slot = source_z * c_count + c_index
        for h in parts:
            rows = pl.ds(h * half, half)
            copy = pltpu.make_async_remote_copy(
                src_ref=normed_out.at[slot, rows],
                dst_ref=normed_out.at[slot, rows],
                send_sem=row_send.at[sem_index * halves + h], recv_sem=row_recv.at[slot, h],
                device_id=device, device_id_type=MESH_IDS,
            )
            copy.start()
            sends.append(copy)

    def wait_row(source_z, source_core, parts=range(halves)):
        slot = source_z * c_count + source_core
        for h in parts:
            rows = pl.ds(h * half, half)
            pltpu.make_async_remote_copy(
                src_ref=normed_out.at[slot, rows], dst_ref=normed_out.at[slot, rows],
                send_sem=row_send.at[0], recv_sem=row_recv.at[slot, h],
                device_id=(x_index, y_index, z_index, other_core), device_id_type=MESH_IDS,
            ).wait_recv()

    right = (x_index, y_index, ring_z(1), c_index)
    left = (x_index, y_index, ring_z(-1), c_index)
    partner = (x_index, y_index, z_index, other_core)
    right_steps = z_count // 2
    left_steps = z_count - 1 - right_steps
    sem_count = [0]

    def next_sem():
        sem_count[0] += 1
        return sem_count[0] - 1

    for step in range(1, weight_group):
        _, device = weight_peer(step)
        copy = pltpu.make_async_remote_copy(
            src_ref=weight_ref, dst_ref=weight_out.at[weight_rank],
            send_sem=weight_send.at[step - 1], recv_sem=weight_recv.at[weight_rank],
            device_id=device, device_id_type=MESH_IDS,
        )
        copy.start()
        sends.append(copy)
    for step in range(1, row_group):
        copy = pltpu.make_async_remote_copy(
            src_ref=ids_ref, dst_ref=ids_out.at[row_rank],
            send_sem=id_send.at[step - 1], recv_sem=id_recv.at[row_rank],
            device_id=row_peer(step), device_id_type=MESH_IDS,
        )
        copy.start()
        sends.append(copy)

    own_piece.wait()
    own_gain.wait()
    for step in range(1, x_count):
        source = lax.rem(x_index + x_count - step, x_count)
        for src, dst, send_sem, recv_sem in (
            (hidden_ref.at[pl.ds(0, quarter)], piece_vmem, piece_send, piece_recv),
            (gain_ref, gain_vmem, gain_send, gain_recv),
        ):
            pltpu.make_async_remote_copy(
                src_ref=src, dst_ref=dst.at[source] if dst is piece_vmem else dst.at[pl.ds(source * width, width)],
                send_sem=send_sem.at[step - 1], recv_sem=recv_sem.at[source],
                device_id=x_peer(x_count - step), device_id_type=MESH_IDS,
            ).wait_recv()
    squares = jnp.zeros((quarter, 1), jnp.float32)
    for part in range(x_count):
        values = piece_vmem[part].astype(jnp.float32)
        squares = squares + jnp.sum(values * values, axis=1, keepdims=True)
    scale = lax.rsqrt(squares / (x_count * width) + norm_epsilon)
    for part in range(x_count):
        values = piece_vmem[part].astype(jnp.float32)
        gain = gain_vmem[pl.ds(part * width, width)].astype(jnp.float32).reshape(1, width)
        normed_vmem[:, part * width:(part + 1) * width] = (values * scale * gain).astype(normed_vmem.dtype)
    own_row = pltpu.make_async_copy(normed_vmem, normed_out.at[row_rank], own_sems.at[0])
    own_row.start()
    own_row.wait()

    send_row(z_index, right, next_sem(), True)
    if left_steps > 0:
        send_row(z_index, left, next_sem(), True)
    send_row(z_index, partner, next_sem(), True)

    for step in range(1, right_steps + 1):
        from_left = ring_z(-step)
        onward = next_sem() if step < right_steps else None
        across = next_sem()
        for h in range(halves):
            wait_row(from_left, c_index, (h,))
            if onward is not None:
                send_row(from_left, right, onward, False, (h,))
            send_row(from_left, partner, across, False, (h,))
        if step <= left_steps:
            from_right = ring_z(step)
            onward = next_sem() if step < left_steps else None
            across = next_sem()
            for h in range(halves):
                wait_row(from_right, c_index, (h,))
                if onward is not None:
                    send_row(from_right, left, onward, False, (h,))
                send_row(from_right, partner, across, False, (h,))

    for copy in own:
        copy.wait()
    for step in range(z_count):
        wait_row(lax.rem(z_index + step, z_count), other_core)
    for step in range(1, weight_group):
        source = lax.rem(weight_rank + weight_group - step, weight_group)
        pltpu.make_async_remote_copy(
            src_ref=weight_ref, dst_ref=weight_out.at[source],
            send_sem=weight_send.at[0], recv_sem=weight_recv.at[source],
            device_id=weight_peer(step)[1], device_id_type=MESH_IDS,
        ).wait_recv()
    for step in range(1, row_group):
        source = lax.rem(row_rank + row_group - step, row_group)
        pltpu.make_async_remote_copy(
            src_ref=ids_ref, dst_ref=ids_out.at[source],
            send_sem=id_send.at[0], recv_sem=id_recv.at[source],
            device_id=row_peer(step), device_id_type=MESH_IDS,
        ).wait_recv()

    group = row_group
    rank = row_rank
    width = weight_out.shape[1]
    padded = weight_out.shape[2]
    spread[...] = jnp.zeros_like(spread)
    result[...] = jnp.zeros_like(result)

    own_stats = pltpu.make_async_copy(spread.at[rank], merged.at[rank], stat_sems.at[0])

    def stats_copy(slot):
        return pltpu.make_async_remote_copy(
            src_ref=spread.at[slot], dst_ref=merged.at[rank],
            send_sem=first_send.at[slot], recv_sem=first_recv.at[rank],
            device_id=(x_index, y_index, slot // c_count, slot % c_count), device_id_type=MESH_IDS,
        )

    def send_chunk(first_slot):
        for slot in range(first_slot, first_slot + slots_per_chunk):

            @pl.when(slot != rank)
            def _():
                stats_copy(slot).start()

            @pl.when(slot == rank)
            def _():
                own_stats.start()

    chunk = 128
    slots_per_chunk = chunk // quarter
    column = lax.broadcasted_iota(jnp.int32, (chunk, padded), 1)
    valid = column < vocab_local
    lane = lax.broadcasted_iota(jnp.int32, (chunk, 128), 1)
    for first in range(0, normed_out.shape[0] * quarter, chunk):
        blocks = []
        for y_block in range(y_count):
            total = jnp.zeros((chunk, padded), jnp.float32)
            for x_block in range(x_count):
                rows = normed_out[first // quarter:(first + chunk) // quarter, :, x_block * width:(x_block + 1) * width]
                total = total + jnp.dot(
                    rows.reshape(chunk, width),
                    weight_out[x_block * y_count + y_block],
                    preferred_element_type=jnp.float32,
                )
            blocks.append(total)
        id_rows = jnp.concatenate(
            [ids_out[slot] for slot in range(first // quarter, first // quarter + slots_per_chunk)], axis=0
        )
        ids_turned[...] = id_rows.astype(jnp.float32).T
        mine = ids_turned[pl.ds(pl.multiple_of(x_index * quarter, quarter), quarter), :]
        target = jnp.concatenate(
            [mine[:, part:part + 1] for part in range(slots_per_chunk)], axis=0
        ).astype(jnp.int32)
        peak = None
        for y_block, block in enumerate(blocks):
            block_peak = jnp.max(jnp.where(valid, block, -jnp.inf), axis=1, keepdims=True)
            peak = block_peak if peak is None else jnp.maximum(peak, block_peak)
        row_sum = jnp.zeros((chunk, 1), jnp.float32)
        row_weighted = jnp.zeros((chunk, 1), jnp.float32)
        row_picked = jnp.zeros((chunk, 1), jnp.float32)
        for y_block, block in enumerate(blocks):
            scaled = jnp.where(valid, jnp.exp(block - peak), 0.0)
            row_sum = row_sum + jnp.sum(scaled, axis=1, keepdims=True)
            row_weighted = row_weighted + jnp.sum(scaled * block, axis=1, keepdims=True)
            global_id = ((y_block * z_count + z_index) * c_count + c_index) * vocab_local + column
            hit = valid & (global_id == target)
            row_picked = row_picked + jnp.sum(jnp.where(hit, block, 0.0), axis=1, keepdims=True)
        table = jnp.where(
            lane == 0, peak,
            jnp.where(lane == 1, row_sum, jnp.where(lane == 2, row_weighted, jnp.where(lane == 3, row_picked, 0.0))),
        )
        lanes = table.T
        for part in range(slots_per_chunk):
            slot = first // quarter + part
            spread[slot, :, 0:quarter] = lanes[0:8, part * quarter:(part + 1) * quarter]
        if first > 0:
            send_chunk(first // quarter - slots_per_chunk)
    send_chunk(group - slots_per_chunk)

    own_stats.wait()

    def finish(step, carry):
        source = lax.rem(rank + group - step, group)
        pltpu.make_async_remote_copy(
            src_ref=spread.at[source], dst_ref=merged.at[source],
            send_sem=first_send.at[source], recv_sem=first_recv.at[source],
            device_id=row_peer(step), device_id_type=MESH_IDS,
        ).wait_recv()
        return carry

    lax.fori_loop(1, group, finish, 0)

    highest = merged[0, 0:1, :]
    for source in range(1, group):
        highest = jnp.maximum(highest, merged[source, 0:1, :])
    totals = jnp.zeros_like(highest)
    weighted = jnp.zeros_like(highest)
    picked = jnp.zeros_like(highest)
    for source in range(group):
        factor = jnp.exp(merged[source, 0:1, :] - highest)
        totals = totals + merged[source, 1:2, :] * factor
        weighted = weighted + merged[source, 2:3, :] * factor
        picked = picked + merged[source, 3:4, :]
    log_norm = highest + jnp.log(totals)

    block_tokens = x_count * quarter
    vert_index = (y_index * z_count + z_index) * c_count + c_index
    long_len = y_count * z_count * c_count * block_tokens // 2
    block_start = vert_index * block_tokens
    in_long = block_start < long_len
    sequence = jnp.where(in_long, 0, 1 + (block_start - long_len) // SHORT)
    live_length = lengths_ref[sequence]
    positions = block_start + x_index * quarter + lax.broadcasted_iota(jnp.int32, (1, 128), 1)
    offsets = jnp.where(in_long, positions, jnp.maximum(positions - long_len, 0) % SHORT)
    live = offsets < live_length
    result[0:1, :] = jnp.where(live, picked - log_norm, 0.0)
    result[1:2, :] = jnp.where(live, log_norm - weighted / totals, 0.0)

    mine = pltpu.make_async_copy(result, results_out.at[x_index], stat_sems.at[1])
    mine.start()
    copies = []
    for step in range(1, x_count):
        copy = pltpu.make_async_remote_copy(
            src_ref=result, dst_ref=results_out.at[x_index],
            send_sem=second_send.at[step - 1], recv_sem=second_recv.at[x_index],
            device_id=x_peer(step), device_id_type=MESH_IDS,
        )
        copy.start()
        copies.append(copy)
    mine.wait()
    for step in range(1, x_count):
        copies[step - 1].wait_send()
        source = lax.rem(x_index + x_count - step, x_count)
        pltpu.make_async_remote_copy(
            src_ref=result, dst_ref=results_out.at[source],
            send_sem=second_send.at[step - 1], recv_sem=second_recv.at[source],
            device_id=x_peer(x_count - step), device_id_type=MESH_IDS,
        ).wait_recv()
    for copy in sends + piece_copies:
        copy.wait_send()
    for slot in range(group):

        @pl.when(slot != rank)
        def _():
            stats_copy(slot).wait_send()


def score_all(hidden, gain, weight, ids, lengths, x_count, row_group, weight_group, vocab_local):
    quarter = hidden.shape[0] // x_count
    width = hidden.shape[1]
    any_spec = pl.BlockSpec(memory_space=pl.ANY)
    return pl.pallas_call(
        functools.partial(fused_kernel, vocab_local),
        out_shape=jax.ShapeDtypeStruct((x_count, 8, 128), jnp.float32),
        in_specs=[any_spec] * 4 + [pl.BlockSpec(memory_space=pltpu.SMEM)],
        out_specs=any_spec,
        scratch_shapes=[
            pltpu.VMEM((row_group, quarter, x_count * width), hidden.dtype),
            pltpu.VMEM((weight_group,) + weight.shape, weight.dtype),
            pltpu.VMEM((row_group,) + ids.shape, ids.dtype),
            pltpu.VMEM((x_count, quarter, width), hidden.dtype),
            pltpu.VMEM((x_count * gain.shape[0],), gain.dtype),
            pltpu.VMEM((quarter, x_count * width), hidden.dtype),
            pltpu.VMEM((row_group, 8, 128), jnp.float32),
            pltpu.VMEM((row_group, 8, 128), jnp.float32),
            pltpu.VMEM((8, 128), jnp.float32),
            pltpu.VMEM((ids.shape[1], 4), jnp.float32),
            pltpu.SemaphoreType.DMA((x_count - 1,)),
            pltpu.SemaphoreType.DMA((x_count,)),
            pltpu.SemaphoreType.DMA((x_count - 1,)),
            pltpu.SemaphoreType.DMA((x_count,)),
            pltpu.SemaphoreType.DMA(((row_group - 1) * 2,)),
            pltpu.SemaphoreType.DMA((row_group, 2)),
            pltpu.SemaphoreType.DMA((weight_group - 1,)),
            pltpu.SemaphoreType.DMA((weight_group,)),
            pltpu.SemaphoreType.DMA((row_group - 1,)),
            pltpu.SemaphoreType.DMA((row_group,)),
            pltpu.SemaphoreType.DMA((5,)),
            pltpu.SemaphoreType.DMA((row_group,)),
            pltpu.SemaphoreType.DMA((row_group,)),
            pltpu.SemaphoreType.DMA((x_count - 1,)),
            pltpu.SemaphoreType.DMA((x_count,)),
            pltpu.SemaphoreType.DMA((2,)),
        ],
        compiler_params=pltpu.CompilerParams(collective_id=0, has_side_effects=True),
    )(hidden, gain, weight, ids, lengths)


def per_device(hidden, norm_gain, head_weight, target_ids, seq_lengths):
    x_count = lax.axis_size("x")
    y_count = lax.axis_size("y")
    z_count = lax.axis_size("z")
    c_count = lax.axis_size("c")
    x_index = lax.axis_index("x")
    y_index = lax.axis_index("y")
    z_index = lax.axis_index("z")
    c_index = lax.axis_index("c")
    vert_count = y_count * z_count * c_count
    vert_index = (y_index * z_count + z_index) * c_count + c_index
    tok_local = hidden.shape[0]
    quarter = tok_local // x_count
    vocab_local = head_weight.shape[1]
    group_count = z_count * c_count

    results = score_all(
        hidden, norm_gain, head_weight, target_ids.reshape(1, -1), seq_lengths,
        x_count, group_count, x_count * y_count, vocab_local,
    )
    full_logprob = results[:, 0, :quarter].reshape(-1)
    full_entropy = results[:, 1, :quarter].reshape(-1)
    return (full_logprob, full_entropy)


def solution(mesh):
    wa_count, vert_count = mesh.devices.shape
    y_count = 4
    c_count = 2
    z_count = vert_count // (y_count * c_count)
    fine = Mesh(mesh.devices.reshape(wa_count, y_count, z_count, c_count), ("x",) + VERT)
    in_specs = (P(VERT, "x"), P("x"), P("x", VERT), P(VERT), P())
    out_specs = (P(VERT), P(VERT))
    return jax.shard_map(
        per_device, mesh=fine, in_specs=in_specs, out_specs=out_specs, check_vma=False
    )
```

```python
import functools

import jax
import jax.numpy as jnp
from jax import lax
from jax.experimental import pallas as pl
from jax.experimental.pallas import tpu as pltpu
from jax.sharding import Mesh
from jax.sharding import PartitionSpec as P

D = 1024
SHORT = 128


norm_epsilon = 1e-06

VERT = ("y", "z", "c")
TOKEN_AXES = ("z", "c")


def live_mask(positions, seq_lengths, long_len, short_len):
    is_long = positions < long_len
    beyond = jnp.maximum(positions - long_len, 0)
    seq_index = jnp.where(is_long, 0, 1 + beyond // short_len)
    offset = jnp.where(is_long, positions, beyond % short_len)
    return offset < jnp.take(seq_lengths, seq_index)


MESH_IDS = pl.DeviceIdType.MESH


def fused_kernel(
    vocab_local, hidden_ref, gain_ref, weight_ref, ids_ref, lengths_ref, results_out,
    normed_out, weight_out, ids_out, piece_vmem, gain_vmem, normed_vmem,
    spread, merged, result, ids_turned,
    piece_send, piece_recv, gain_send, gain_recv,
    row_send, row_recv, weight_send, weight_recv, id_send, id_recv, own_sems,
    first_send, first_recv, second_send, second_recv, stat_sems,
):
    x_count = lax.axis_size("x")
    y_count = lax.axis_size("y")
    z_count = lax.axis_size("z")
    c_count = lax.axis_size("c")
    x_index = lax.axis_index("x")
    y_index = lax.axis_index("y")
    z_index = lax.axis_index("z")
    c_index = lax.axis_index("c")
    row_group = z_count * c_count
    weight_group = x_count * y_count
    row_rank = z_index * c_count + c_index
    weight_rank = x_index * y_count + y_index
    other_core = 1 - c_index

    def row_peer(step):
        rank = lax.rem(row_rank + step, row_group)
        return (x_index, y_index, rank // c_count, rank % c_count)

    def weight_peer(step):
        rank = lax.rem(weight_rank + step, weight_group)
        return rank, (rank // y_count, rank % y_count, z_index, c_index)

    def ring_z(shift):
        return lax.rem(z_index + shift + z_count, z_count)

    barrier = pltpu.get_barrier_semaphore()
    for step in range(1, row_group):
        pl.semaphore_signal(barrier, inc=1, device_id=row_peer(step), device_id_type=MESH_IDS)
    for step in range(1, weight_group):
        pl.semaphore_signal(barrier, inc=1, device_id=weight_peer(step)[1], device_id_type=MESH_IDS)
    pl.semaphore_wait(barrier, row_group - 1 + weight_group - 1)

    quarter = piece_vmem.shape[1]
    width = piece_vmem.shape[2]

    def x_peer(step):
        return (lax.rem(x_index + step, x_count), y_index, z_index, c_index)

    own_piece = pltpu.make_async_copy(
        hidden_ref.at[pl.ds(x_index * quarter, quarter)], piece_vmem.at[x_index], own_sems.at[3]
    )
    own_gain = pltpu.make_async_copy(gain_ref, gain_vmem.at[pl.ds(x_index * width, width)], own_sems.at[4])
    own_piece.start()
    own_gain.start()
    piece_copies = []
    for step in range(1, x_count):
        target = lax.rem(x_index + step, x_count)
        for src, dst, send_sem, recv_sem in (
            (hidden_ref.at[pl.ds(target * quarter, quarter)], piece_vmem, piece_send, piece_recv),
            (gain_ref, gain_vmem, gain_send, gain_recv),
        ):
            copy = pltpu.make_async_remote_copy(
                src_ref=src, dst_ref=dst.at[x_index] if dst is piece_vmem else dst.at[pl.ds(x_index * width, width)],
                send_sem=send_sem.at[step - 1], recv_sem=recv_sem.at[x_index],
                device_id=x_peer(step), device_id_type=MESH_IDS,
            )
            copy.start()
            piece_copies.append(copy)

    own = [
        pltpu.make_async_copy(weight_ref, weight_out.at[weight_rank], own_sems.at[1]),
        pltpu.make_async_copy(ids_ref, ids_out.at[row_rank], own_sems.at[2]),
    ]
    for copy in own:
        copy.start()

    sends = []

    halves = 4
    half = quarter // halves

    def send_row(source_z, device, sem_index, from_input, parts=range(halves)):
        slot = source_z * c_count + c_index
        for h in parts:
            rows = pl.ds(h * half, half)
            copy = pltpu.make_async_remote_copy(
                src_ref=normed_out.at[slot, rows],
                dst_ref=normed_out.at[slot, rows],
                send_sem=row_send.at[sem_index * halves + h], recv_sem=row_recv.at[slot, h],
                device_id=device, device_id_type=MESH_IDS,
            )
            copy.start()
            sends.append(copy)

    def wait_row(source_z, source_core, parts=range(halves)):
        slot = source_z * c_count + source_core
        for h in parts:
            rows = pl.ds(h * half, half)
            pltpu.make_async_remote_copy(
                src_ref=normed_out.at[slot, rows], dst_ref=normed_out.at[slot, rows],
                send_sem=row_send.at[0], recv_sem=row_recv.at[slot, h],
                device_id=(x_index, y_index, z_index, other_core), device_id_type=MESH_IDS,
            ).wait_recv()

    right = (x_index, y_index, ring_z(1), c_index)
    left = (x_index, y_index, ring_z(-1), c_index)
    partner = (x_index, y_index, z_index, other_core)
    right_steps = z_count // 2
    left_steps = z_count - 1 - right_steps
    sem_count = [0]

    def next_sem():
        sem_count[0] += 1
        return sem_count[0] - 1

    for step in range(1, weight_group):
        _, device = weight_peer(step)
        copy = pltpu.make_async_remote_copy(
            src_ref=weight_ref, dst_ref=weight_out.at[weight_rank],
            send_sem=weight_send.at[step - 1], recv_sem=weight_recv.at[weight_rank],
            device_id=device, device_id_type=MESH_IDS,
        )
        copy.start()
        sends.append(copy)
    for step in range(1, row_group):
        copy = pltpu.make_async_remote_copy(
            src_ref=ids_ref, dst_ref=ids_out.at[row_rank],
            send_sem=id_send.at[step - 1], recv_sem=id_recv.at[row_rank],
            device_id=row_peer(step), device_id_type=MESH_IDS,
        )
        copy.start()
        sends.append(copy)

    own_piece.wait()
    own_gain.wait()
    for step in range(1, x_count):
        source = lax.rem(x_index + x_count - step, x_count)
        for src, dst, send_sem, recv_sem in (
            (hidden_ref.at[pl.ds(0, quarter)], piece_vmem, piece_send, piece_recv),
            (gain_ref, gain_vmem, gain_send, gain_recv),
        ):
            pltpu.make_async_remote_copy(
                src_ref=src, dst_ref=dst.at[source] if dst is piece_vmem else dst.at[pl.ds(source * width, width)],
                send_sem=send_sem.at[step - 1], recv_sem=recv_sem.at[source],
                device_id=x_peer(x_count - step), device_id_type=MESH_IDS,
            ).wait_recv()
    squares = jnp.zeros((quarter, 1), jnp.float32)
    for part in range(x_count):
        values = piece_vmem[part].astype(jnp.float32)
        squares = squares + jnp.sum(values * values, axis=1, keepdims=True)
    scale = lax.rsqrt(squares / (x_count * width) + norm_epsilon)
    for part in range(x_count):
        values = piece_vmem[part].astype(jnp.float32)
        gain = gain_vmem[pl.ds(part * width, width)].astype(jnp.float32).reshape(1, width)
        normed_vmem[:, part * width:(part + 1) * width] = (values * scale * gain).astype(normed_vmem.dtype)
    own_row = pltpu.make_async_copy(normed_vmem, normed_out.at[row_rank], own_sems.at[0])
    own_row.start()
    own_row.wait()

    send_row(z_index, right, next_sem(), True)
    if left_steps > 0:
        send_row(z_index, left, next_sem(), True)
    send_row(z_index, partner, next_sem(), True)

    for step in range(1, right_steps + 1):
        from_left = ring_z(-step)
        onward = next_sem() if step < right_steps else None
        across = next_sem()
        for h in range(halves):
            wait_row(from_left, c_index, (h,))
            if onward is not None:
                send_row(from_left, right, onward, False, (h,))
            send_row(from_left, partner, across, False, (h,))
        if step <= left_steps:
            from_right = ring_z(step)
            onward = next_sem() if step < left_steps else None
            across = next_sem()
            for h in range(halves):
                wait_row(from_right, c_index, (h,))
                if onward is not None:
                    send_row(from_right, left, onward, False, (h,))
                send_row(from_right, partner, across, False, (h,))

    for copy in own:
        copy.wait()
    for step in range(z_count):
        wait_row(lax.rem(z_index + step, z_count), other_core)
    for step in range(1, weight_group):
        source = lax.rem(weight_rank + weight_group - step, weight_group)
        pltpu.make_async_remote_copy(
            src_ref=weight_ref, dst_ref=weight_out.at[source],
            send_sem=weight_send.at[0], recv_sem=weight_recv.at[source],
            device_id=weight_peer(step)[1], device_id_type=MESH_IDS,
        ).wait_recv()
    for step in range(1, row_group):
        source = lax.rem(row_rank + row_group - step, row_group)
        pltpu.make_async_remote_copy(
            src_ref=ids_ref, dst_ref=ids_out.at[source],
            send_sem=id_send.at[0], recv_sem=id_recv.at[source],
            device_id=row_peer(step), device_id_type=MESH_IDS,
        ).wait_recv()

    group = row_group
    rank = row_rank
    width = weight_out.shape[1]
    padded = weight_out.shape[2]
    spread[...] = jnp.zeros_like(spread)
    result[...] = jnp.zeros_like(result)

    own_stats = pltpu.make_async_copy(spread.at[rank], merged.at[rank], stat_sems.at[0])

    def stats_copy(slot):
        return pltpu.make_async_remote_copy(
            src_ref=spread.at[slot], dst_ref=merged.at[rank],
            send_sem=first_send.at[slot], recv_sem=first_recv.at[rank],
            device_id=(x_index, y_index, slot // c_count, slot % c_count), device_id_type=MESH_IDS,
        )

    def send_chunk(first_slot):
        for slot in range(first_slot, first_slot + slots_per_chunk):

            @pl.when(slot != rank)
            def _():
                stats_copy(slot).start()

            @pl.when(slot == rank)
            def _():
                own_stats.start()

    chunk = 128
    slots_per_chunk = chunk // quarter
    column = lax.broadcasted_iota(jnp.int32, (chunk, padded), 1)
    valid = column < vocab_local
    lane = lax.broadcasted_iota(jnp.int32, (chunk, 128), 1)
    for first in range(0, normed_out.shape[0] * quarter, chunk):
        blocks = []
        for y_block in range(y_count):
            total = jnp.zeros((chunk, padded), jnp.float32)
            for x_block in range(x_count):
                rows = normed_out[first // quarter:(first + chunk) // quarter, :, x_block * width:(x_block + 1) * width]
                total = total + jnp.dot(
                    rows.reshape(chunk, width),
                    weight_out[x_block * y_count + y_block],
                    preferred_element_type=jnp.float32,
                )
            blocks.append(total)
        id_rows = jnp.concatenate(
            [ids_out[slot] for slot in range(first // quarter, first // quarter + slots_per_chunk)], axis=0
        )
        ids_turned[...] = id_rows.astype(jnp.float32).T
        mine = ids_turned[pl.ds(pl.multiple_of(x_index * quarter, quarter), quarter), :]
        target = jnp.concatenate(
            [mine[:, part:part + 1] for part in range(slots_per_chunk)], axis=0
        ).astype(jnp.int32)
        peak = None
        for y_block, block in enumerate(blocks):
            block_peak = jnp.max(jnp.where(valid, block, -jnp.inf), axis=1, keepdims=True)
            peak = block_peak if peak is None else jnp.maximum(peak, block_peak)
        row_sum = jnp.zeros((chunk, 1), jnp.float32)
        row_weighted = jnp.zeros((chunk, 1), jnp.float32)
        row_picked = jnp.zeros((chunk, 1), jnp.float32)
        for y_block, block in enumerate(blocks):
            scaled = jnp.where(valid, jnp.exp(block - peak), 0.0)
            row_sum = row_sum + jnp.sum(scaled, axis=1, keepdims=True)
            row_weighted = row_weighted + jnp.sum(scaled * block, axis=1, keepdims=True)
            global_id = ((y_block * z_count + z_index) * c_count + c_index) * vocab_local + column
            hit = valid & (global_id == target)
            row_picked = row_picked + jnp.sum(jnp.where(hit, block, 0.0), axis=1, keepdims=True)
        table = jnp.where(
            lane == 0, peak,
            jnp.where(lane == 1, row_sum, jnp.where(lane == 2, row_weighted, jnp.where(lane == 3, row_picked, 0.0))),
        )
        lanes = table.T
        for part in range(slots_per_chunk):
            slot = first // quarter + part
            spread[slot, :, 0:quarter] = lanes[0:8, part * quarter:(part + 1) * quarter]
        if first > 0:
            send_chunk(first // quarter - slots_per_chunk)
    send_chunk(group - slots_per_chunk)

    own_stats.wait()

    def finish(step, carry):
        source = lax.rem(rank + group - step, group)
        pltpu.make_async_remote_copy(
            src_ref=spread.at[source], dst_ref=merged.at[source],
            send_sem=first_send.at[source], recv_sem=first_recv.at[source],
            device_id=row_peer(step), device_id_type=MESH_IDS,
        ).wait_recv()
        return carry

    lax.fori_loop(1, group, finish, 0)

    highest = merged[0, 0:1, :]
    for source in range(1, group):
        highest = jnp.maximum(highest, merged[source, 0:1, :])
    totals = jnp.zeros_like(highest)
    weighted = jnp.zeros_like(highest)
    picked = jnp.zeros_like(highest)
    for source in range(group):
        factor = jnp.exp(merged[source, 0:1, :] - highest)
        totals = totals + merged[source, 1:2, :] * factor
        weighted = weighted + merged[source, 2:3, :] * factor
        picked = picked + merged[source, 3:4, :]
    log_norm = highest + jnp.log(totals)

    block_tokens = x_count * quarter
    vert_index = (y_index * z_count + z_index) * c_count + c_index
    long_len = y_count * z_count * c_count * block_tokens // 2
    block_start = vert_index * block_tokens
    in_long = block_start < long_len
    sequence = jnp.where(in_long, 0, 1 + (block_start - long_len) // SHORT)
    live_length = lengths_ref[sequence]
    positions = block_start + x_index * quarter + lax.broadcasted_iota(jnp.int32, (1, 128), 1)
    offsets = jnp.where(in_long, positions, jnp.maximum(positions - long_len, 0) % SHORT)
    live = offsets < live_length
    result[0:1, :] = jnp.where(live, picked - log_norm, 0.0)
    result[1:2, :] = jnp.where(live, log_norm - weighted / totals, 0.0)

    mine = pltpu.make_async_copy(result, results_out.at[x_index], stat_sems.at[1])
    mine.start()
    copies = []
    for step in range(1, x_count):
        copy = pltpu.make_async_remote_copy(
            src_ref=result, dst_ref=results_out.at[x_index],
            send_sem=second_send.at[step - 1], recv_sem=second_recv.at[x_index],
            device_id=x_peer(step), device_id_type=MESH_IDS,
        )
        copy.start()
        copies.append(copy)
    mine.wait()
    for step in range(1, x_count):
        copies[step - 1].wait_send()
        source = lax.rem(x_index + x_count - step, x_count)
        pltpu.make_async_remote_copy(
            src_ref=result, dst_ref=results_out.at[source],
            send_sem=second_send.at[step - 1], recv_sem=second_recv.at[source],
            device_id=x_peer(x_count - step), device_id_type=MESH_IDS,
        ).wait_recv()
    for copy in sends + piece_copies:
        copy.wait_send()
    for slot in range(group):

        @pl.when(slot != rank)
        def _():
            stats_copy(slot).wait_send()


def score_all(hidden, gain, weight, ids, lengths, x_count, row_group, weight_group, vocab_local):
    quarter = hidden.shape[0] // x_count
    width = hidden.shape[1]
    any_spec = pl.BlockSpec(memory_space=pl.ANY)
    return pl.pallas_call(
        functools.partial(fused_kernel, vocab_local),
        out_shape=jax.ShapeDtypeStruct((x_count, 8, 128), jnp.float32),
        in_specs=[any_spec] * 4 + [pl.BlockSpec(memory_space=pltpu.SMEM)],
        out_specs=any_spec,
        scratch_shapes=[
            pltpu.VMEM((row_group, quarter, x_count * width), hidden.dtype),
            pltpu.VMEM((weight_group,) + weight.shape, weight.dtype),
            pltpu.VMEM((row_group,) + ids.shape, ids.dtype),
            pltpu.VMEM((x_count, quarter, width), hidden.dtype),
            pltpu.VMEM((x_count * gain.shape[0],), gain.dtype),
            pltpu.VMEM((quarter, x_count * width), hidden.dtype),
            pltpu.VMEM((row_group, 8, 128), jnp.float32),
            pltpu.VMEM((row_group, 8, 128), jnp.float32),
            pltpu.VMEM((8, 128), jnp.float32),
            pltpu.VMEM((ids.shape[1], 4), jnp.float32),
            pltpu.SemaphoreType.DMA((x_count - 1,)),
            pltpu.SemaphoreType.DMA((x_count,)),
            pltpu.SemaphoreType.DMA((x_count - 1,)),
            pltpu.SemaphoreType.DMA((x_count,)),
            pltpu.SemaphoreType.DMA(((row_group - 1) * 4,)),
            pltpu.SemaphoreType.DMA((row_group, 4)),
            pltpu.SemaphoreType.DMA((weight_group - 1,)),
            pltpu.SemaphoreType.DMA((weight_group,)),
            pltpu.SemaphoreType.DMA((row_group - 1,)),
            pltpu.SemaphoreType.DMA((row_group,)),
            pltpu.SemaphoreType.DMA((5,)),
            pltpu.SemaphoreType.DMA((row_group,)),
            pltpu.SemaphoreType.DMA((row_group,)),
            pltpu.SemaphoreType.DMA((x_count - 1,)),
            pltpu.SemaphoreType.DMA((x_count,)),
            pltpu.SemaphoreType.DMA((2,)),
        ],
        compiler_params=pltpu.CompilerParams(collective_id=0, has_side_effects=True),
    )(hidden, gain, weight, ids, lengths)


def per_device(hidden, norm_gain, head_weight, target_ids, seq_lengths):
    x_count = lax.axis_size("x")
    y_count = lax.axis_size("y")
    z_count = lax.axis_size("z")
    c_count = lax.axis_size("c")
    x_index = lax.axis_index("x")
    y_index = lax.axis_index("y")
    z_index = lax.axis_index("z")
    c_index = lax.axis_index("c")
    vert_count = y_count * z_count * c_count
    vert_index = (y_index * z_count + z_index) * c_count + c_index
    tok_local = hidden.shape[0]
    quarter = tok_local // x_count
    vocab_local = head_weight.shape[1]
    group_count = z_count * c_count

    results = score_all(
        hidden, norm_gain, head_weight, target_ids.reshape(1, -1), seq_lengths,
        x_count, group_count, x_count * y_count, vocab_local,
    )
    full_logprob = results[:, 0, :quarter].reshape(-1)
    full_entropy = results[:, 1, :quarter].reshape(-1)
    return (full_logprob, full_entropy)


def solution(mesh):
    wa_count, vert_count = mesh.devices.shape
    y_count = 4
    c_count = 2
    z_count = vert_count // (y_count * c_count)
    fine = Mesh(mesh.devices.reshape(wa_count, y_count, z_count, c_count), ("x",) + VERT)
    in_specs = (P(VERT, "x"), P("x"), P("x", VERT), P(VERT), P())
    out_specs = (P(VERT), P(VERT))
    return jax.shard_map(
        per_device, mesh=fine, in_specs=in_specs, out_specs=out_specs, check_vma=False
    )
```

```python
import functools

import jax
import jax.numpy as jnp
from jax import lax
from jax.experimental import pallas as pl
from jax.experimental.pallas import tpu as pltpu
from jax.sharding import Mesh
from jax.sharding import PartitionSpec as P

D = 1024
SHORT = 128


norm_epsilon = 1e-06

VERT = ("y", "z", "c")
TOKEN_AXES = ("z", "c")


def live_mask(positions, seq_lengths, long_len, short_len):
    is_long = positions < long_len
    beyond = jnp.maximum(positions - long_len, 0)
    seq_index = jnp.where(is_long, 0, 1 + beyond // short_len)
    offset = jnp.where(is_long, positions, beyond % short_len)
    return offset < jnp.take(seq_lengths, seq_index)


MESH_IDS = pl.DeviceIdType.MESH


def fused_kernel(
    vocab_local, hidden_ref, gain_ref, weight_ref, ids_ref, lengths_ref, results_out,
    normed_out, weight_out, ids_out, piece_vmem, gain_vmem, normed_vmem,
    spread, merged, result, ids_turned,
    piece_send, piece_recv, gain_send, gain_recv,
    row_send, row_recv, weight_send, weight_recv, id_send, id_recv, own_sems,
    first_send, first_recv, second_send, second_recv, stat_sems,
):
    x_count = lax.axis_size("x")
    y_count = lax.axis_size("y")
    z_count = lax.axis_size("z")
    c_count = lax.axis_size("c")
    x_index = lax.axis_index("x")
    y_index = lax.axis_index("y")
    z_index = lax.axis_index("z")
    c_index = lax.axis_index("c")
    row_group = z_count * c_count
    weight_group = x_count * y_count
    row_rank = z_index * c_count + c_index
    weight_rank = x_index * y_count + y_index
    other_core = 1 - c_index

    def row_peer(step):
        rank = lax.rem(row_rank + step, row_group)
        return (x_index, y_index, rank // c_count, rank % c_count)

    def weight_peer(step):
        rank = lax.rem(weight_rank + step, weight_group)
        return rank, (rank // y_count, rank % y_count, z_index, c_index)

    def ring_z(shift):
        return lax.rem(z_index + shift + z_count, z_count)

    barrier = pltpu.get_barrier_semaphore()
    for step in range(1, row_group):
        pl.semaphore_signal(barrier, inc=1, device_id=row_peer(step), device_id_type=MESH_IDS)
    for step in range(1, weight_group):
        pl.semaphore_signal(barrier, inc=1, device_id=weight_peer(step)[1], device_id_type=MESH_IDS)
    pl.semaphore_wait(barrier, row_group - 1 + weight_group - 1)

    quarter = piece_vmem.shape[1]
    width = piece_vmem.shape[2]

    def x_peer(step):
        return (lax.rem(x_index + step, x_count), y_index, z_index, c_index)

    own_piece = pltpu.make_async_copy(
        hidden_ref.at[pl.ds(x_index * quarter, quarter)], piece_vmem.at[x_index], own_sems.at[3]
    )
    own_gain = pltpu.make_async_copy(gain_ref, gain_vmem.at[pl.ds(x_index * width, width)], own_sems.at[4])
    own_piece.start()
    own_gain.start()
    piece_copies = []
    for step in range(1, x_count):
        target = lax.rem(x_index + step, x_count)
        for src, dst, send_sem, recv_sem in (
            (hidden_ref.at[pl.ds(target * quarter, quarter)], piece_vmem, piece_send, piece_recv),
            (gain_ref, gain_vmem, gain_send, gain_recv),
        ):
            copy = pltpu.make_async_remote_copy(
                src_ref=src, dst_ref=dst.at[x_index] if dst is piece_vmem else dst.at[pl.ds(x_index * width, width)],
                send_sem=send_sem.at[step - 1], recv_sem=recv_sem.at[x_index],
                device_id=x_peer(step), device_id_type=MESH_IDS,
            )
            copy.start()
            piece_copies.append(copy)

    own = [
        pltpu.make_async_copy(weight_ref, weight_out.at[weight_rank], own_sems.at[1]),
        pltpu.make_async_copy(ids_ref, ids_out.at[row_rank], own_sems.at[2]),
    ]
    for copy in own:
        copy.start()

    sends = []

    halves = 4
    half = quarter // halves

    def send_row(source_z, device, sem_index, from_input, parts=range(halves)):
        slot = source_z * c_count + c_index
        for h in parts:
            rows = pl.ds(h * half, half)
            copy = pltpu.make_async_remote_copy(
                src_ref=normed_out.at[slot, rows],
                dst_ref=normed_out.at[slot, rows],
                send_sem=row_send.at[sem_index * halves + h], recv_sem=row_recv.at[slot, h],
                device_id=device, device_id_type=MESH_IDS,
            )
            copy.start()
            sends.append(copy)

    def wait_row(source_z, source_core, parts=range(halves)):
        slot = source_z * c_count + source_core
        for h in parts:
            rows = pl.ds(h * half, half)
            pltpu.make_async_remote_copy(
                src_ref=normed_out.at[slot, rows], dst_ref=normed_out.at[slot, rows],
                send_sem=row_send.at[0], recv_sem=row_recv.at[slot, h],
                device_id=(x_index, y_index, z_index, other_core), device_id_type=MESH_IDS,
            ).wait_recv()

    right = (x_index, y_index, ring_z(1), c_index)
    left = (x_index, y_index, ring_z(-1), c_index)
    partner = (x_index, y_index, z_index, other_core)
    right_steps = z_count // 2
    left_steps = z_count - 1 - right_steps
    sem_count = [0]

    def next_sem():
        sem_count[0] += 1
        return sem_count[0] - 1

    for step in range(1, row_group):
        copy = pltpu.make_async_remote_copy(
            src_ref=ids_ref, dst_ref=ids_out.at[row_rank],
            send_sem=id_send.at[step - 1], recv_sem=id_recv.at[row_rank],
            device_id=row_peer(step), device_id_type=MESH_IDS,
        )
        copy.start()
        sends.append(copy)

    own_piece.wait()
    own_gain.wait()
    for step in range(1, x_count):
        source = lax.rem(x_index + x_count - step, x_count)
        for src, dst, send_sem, recv_sem in (
            (hidden_ref.at[pl.ds(0, quarter)], piece_vmem, piece_send, piece_recv),
            (gain_ref, gain_vmem, gain_send, gain_recv),
        ):
            pltpu.make_async_remote_copy(
                src_ref=src, dst_ref=dst.at[source] if dst is piece_vmem else dst.at[pl.ds(source * width, width)],
                send_sem=send_sem.at[step - 1], recv_sem=recv_sem.at[source],
                device_id=x_peer(x_count - step), device_id_type=MESH_IDS,
            ).wait_recv()
    squares = jnp.zeros((quarter, 1), jnp.float32)
    for part in range(x_count):
        values = piece_vmem[part].astype(jnp.float32)
        squares = squares + jnp.sum(values * values, axis=1, keepdims=True)
    scale = lax.rsqrt(squares / (x_count * width) + norm_epsilon)
    for part in range(x_count):
        values = piece_vmem[part].astype(jnp.float32)
        gain = gain_vmem[pl.ds(part * width, width)].astype(jnp.float32).reshape(1, width)
        normed_vmem[:, part * width:(part + 1) * width] = (values * scale * gain).astype(normed_vmem.dtype)
    own_row = pltpu.make_async_copy(normed_vmem, normed_out.at[row_rank], own_sems.at[0])
    own_row.start()
    own_row.wait()

    send_row(z_index, right, next_sem(), True)
    if left_steps > 0:
        send_row(z_index, left, next_sem(), True)
    send_row(z_index, partner, next_sem(), True)

    for step in range(1, weight_group):
        _, device = weight_peer(step)
        copy = pltpu.make_async_remote_copy(
            src_ref=weight_ref, dst_ref=weight_out.at[weight_rank],
            send_sem=weight_send.at[step - 1], recv_sem=weight_recv.at[weight_rank],
            device_id=device, device_id_type=MESH_IDS,
        )
        copy.start()
        sends.append(copy)

    for step in range(1, right_steps + 1):
        from_left = ring_z(-step)
        onward = next_sem() if step < right_steps else None
        across = next_sem()
        for h in range(halves):
            wait_row(from_left, c_index, (h,))
            if onward is not None:
                send_row(from_left, right, onward, False, (h,))
            send_row(from_left, partner, across, False, (h,))
        if step <= left_steps:
            from_right = ring_z(step)
            onward = next_sem() if step < left_steps else None
            across = next_sem()
            for h in range(halves):
                wait_row(from_right, c_index, (h,))
                if onward is not None:
                    send_row(from_right, left, onward, False, (h,))
                send_row(from_right, partner, across, False, (h,))

    for copy in own:
        copy.wait()
    for step in range(z_count):
        wait_row(lax.rem(z_index + step, z_count), other_core)
    for step in range(1, weight_group):
        source = lax.rem(weight_rank + weight_group - step, weight_group)
        pltpu.make_async_remote_copy(
            src_ref=weight_ref, dst_ref=weight_out.at[source],
            send_sem=weight_send.at[0], recv_sem=weight_recv.at[source],
            device_id=weight_peer(step)[1], device_id_type=MESH_IDS,
        ).wait_recv()
    for step in range(1, row_group):
        source = lax.rem(row_rank + row_group - step, row_group)
        pltpu.make_async_remote_copy(
            src_ref=ids_ref, dst_ref=ids_out.at[source],
            send_sem=id_send.at[0], recv_sem=id_recv.at[source],
            device_id=row_peer(step), device_id_type=MESH_IDS,
        ).wait_recv()

    group = row_group
    rank = row_rank
    width = weight_out.shape[1]
    padded = weight_out.shape[2]
    spread[...] = jnp.zeros_like(spread)
    result[...] = jnp.zeros_like(result)

    own_stats = pltpu.make_async_copy(spread.at[rank], merged.at[rank], stat_sems.at[0])

    def stats_copy(slot):
        return pltpu.make_async_remote_copy(
            src_ref=spread.at[slot], dst_ref=merged.at[rank],
            send_sem=first_send.at[slot], recv_sem=first_recv.at[rank],
            device_id=(x_index, y_index, slot // c_count, slot % c_count), device_id_type=MESH_IDS,
        )

    def send_chunk(first_slot):
        for slot in range(first_slot, first_slot + slots_per_chunk):

            @pl.when(slot != rank)
            def _():
                stats_copy(slot).start()

            @pl.when(slot == rank)
            def _():
                own_stats.start()

    chunk = 128
    slots_per_chunk = chunk // quarter
    column = lax.broadcasted_iota(jnp.int32, (chunk, padded), 1)
    valid = column < vocab_local
    lane = lax.broadcasted_iota(jnp.int32, (chunk, 128), 1)
    for first in range(0, normed_out.shape[0] * quarter, chunk):
        blocks = []
        for y_block in range(y_count):
            total = jnp.zeros((chunk, padded), jnp.float32)
            for x_block in range(x_count):
                rows = normed_out[first // quarter:(first + chunk) // quarter, :, x_block * width:(x_block + 1) * width]
                total = total + jnp.dot(
                    rows.reshape(chunk, width),
                    weight_out[x_block * y_count + y_block],
                    preferred_element_type=jnp.float32,
                )
            blocks.append(total)
        id_rows = jnp.concatenate(
            [ids_out[slot] for slot in range(first // quarter, first // quarter + slots_per_chunk)], axis=0
        )
        ids_turned[...] = id_rows.astype(jnp.float32).T
        mine = ids_turned[pl.ds(pl.multiple_of(x_index * quarter, quarter), quarter), :]
        target = jnp.concatenate(
            [mine[:, part:part + 1] for part in range(slots_per_chunk)], axis=0
        ).astype(jnp.int32)
        peak = None
        for y_block, block in enumerate(blocks):
            block_peak = jnp.max(jnp.where(valid, block, -jnp.inf), axis=1, keepdims=True)
            peak = block_peak if peak is None else jnp.maximum(peak, block_peak)
        row_sum = jnp.zeros((chunk, 1), jnp.float32)
        row_weighted = jnp.zeros((chunk, 1), jnp.float32)
        row_picked = jnp.zeros((chunk, 1), jnp.float32)
        for y_block, block in enumerate(blocks):
            scaled = jnp.where(valid, jnp.exp(block - peak), 0.0)
            row_sum = row_sum + jnp.sum(scaled, axis=1, keepdims=True)
            row_weighted = row_weighted + jnp.sum(scaled * block, axis=1, keepdims=True)
            global_id = ((y_block * z_count + z_index) * c_count + c_index) * vocab_local + column
            hit = valid & (global_id == target)
            row_picked = row_picked + jnp.sum(jnp.where(hit, block, 0.0), axis=1, keepdims=True)
        table = jnp.where(
            lane == 0, peak,
            jnp.where(lane == 1, row_sum, jnp.where(lane == 2, row_weighted, jnp.where(lane == 3, row_picked, 0.0))),
        )
        lanes = table.T
        for part in range(slots_per_chunk):
            slot = first // quarter + part
            spread[slot, :, 0:quarter] = lanes[0:8, part * quarter:(part + 1) * quarter]
        if first > 0:
            send_chunk(first // quarter - slots_per_chunk)
    send_chunk(group - slots_per_chunk)

    own_stats.wait()

    def finish(step, carry):
        source = lax.rem(rank + group - step, group)
        pltpu.make_async_remote_copy(
            src_ref=spread.at[source], dst_ref=merged.at[source],
            send_sem=first_send.at[source], recv_sem=first_recv.at[source],
            device_id=row_peer(step), device_id_type=MESH_IDS,
        ).wait_recv()
        return carry

    lax.fori_loop(1, group, finish, 0)

    highest = merged[0, 0:1, :]
    for source in range(1, group):
        highest = jnp.maximum(highest, merged[source, 0:1, :])
    totals = jnp.zeros_like(highest)
    weighted = jnp.zeros_like(highest)
    picked = jnp.zeros_like(highest)
    for source in range(group):
        factor = jnp.exp(merged[source, 0:1, :] - highest)
        totals = totals + merged[source, 1:2, :] * factor
        weighted = weighted + merged[source, 2:3, :] * factor
        picked = picked + merged[source, 3:4, :]
    log_norm = highest + jnp.log(totals)

    block_tokens = x_count * quarter
    vert_index = (y_index * z_count + z_index) * c_count + c_index
    long_len = y_count * z_count * c_count * block_tokens // 2
    block_start = vert_index * block_tokens
    in_long = block_start < long_len
    sequence = jnp.where(in_long, 0, 1 + (block_start - long_len) // SHORT)
    live_length = lengths_ref[sequence]
    positions = block_start + x_index * quarter + lax.broadcasted_iota(jnp.int32, (1, 128), 1)
    offsets = jnp.where(in_long, positions, jnp.maximum(positions - long_len, 0) % SHORT)
    live = offsets < live_length
    result[0:1, :] = jnp.where(live, picked - log_norm, 0.0)
    result[1:2, :] = jnp.where(live, log_norm - weighted / totals, 0.0)

    mine = pltpu.make_async_copy(result, results_out.at[x_index], stat_sems.at[1])
    mine.start()
    copies = []
    for step in range(1, x_count):
        copy = pltpu.make_async_remote_copy(
            src_ref=result, dst_ref=results_out.at[x_index],
            send_sem=second_send.at[step - 1], recv_sem=second_recv.at[x_index],
            device_id=x_peer(step), device_id_type=MESH_IDS,
        )
        copy.start()
        copies.append(copy)
    mine.wait()
    for step in range(1, x_count):
        copies[step - 1].wait_send()
        source = lax.rem(x_index + x_count - step, x_count)
        pltpu.make_async_remote_copy(
            src_ref=result, dst_ref=results_out.at[source],
            send_sem=second_send.at[step - 1], recv_sem=second_recv.at[source],
            device_id=x_peer(x_count - step), device_id_type=MESH_IDS,
        ).wait_recv()
    for copy in sends + piece_copies:
        copy.wait_send()
    for slot in range(group):

        @pl.when(slot != rank)
        def _():
            stats_copy(slot).wait_send()


def score_all(hidden, gain, weight, ids, lengths, x_count, row_group, weight_group, vocab_local):
    quarter = hidden.shape[0] // x_count
    width = hidden.shape[1]
    any_spec = pl.BlockSpec(memory_space=pl.ANY)
    return pl.pallas_call(
        functools.partial(fused_kernel, vocab_local),
        out_shape=jax.ShapeDtypeStruct((x_count, 8, 128), jnp.float32),
        in_specs=[any_spec] * 4 + [pl.BlockSpec(memory_space=pltpu.SMEM)],
        out_specs=any_spec,
        scratch_shapes=[
            pltpu.VMEM((row_group, quarter, x_count * width), hidden.dtype),
            pltpu.VMEM((weight_group,) + weight.shape, weight.dtype),
            pltpu.VMEM((row_group,) + ids.shape, ids.dtype),
            pltpu.VMEM((x_count, quarter, width), hidden.dtype),
            pltpu.VMEM((x_count * gain.shape[0],), gain.dtype),
            pltpu.VMEM((quarter, x_count * width), hidden.dtype),
            pltpu.VMEM((row_group, 8, 128), jnp.float32),
            pltpu.VMEM((row_group, 8, 128), jnp.float32),
            pltpu.VMEM((8, 128), jnp.float32),
            pltpu.VMEM((ids.shape[1], 4), jnp.float32),
            pltpu.SemaphoreType.DMA((x_count - 1,)),
            pltpu.SemaphoreType.DMA((x_count,)),
            pltpu.SemaphoreType.DMA((x_count - 1,)),
            pltpu.SemaphoreType.DMA((x_count,)),
            pltpu.SemaphoreType.DMA(((row_group - 1) * 4,)),
            pltpu.SemaphoreType.DMA((row_group, 4)),
            pltpu.SemaphoreType.DMA((weight_group - 1,)),
            pltpu.SemaphoreType.DMA((weight_group,)),
            pltpu.SemaphoreType.DMA((row_group - 1,)),
            pltpu.SemaphoreType.DMA((row_group,)),
            pltpu.SemaphoreType.DMA((5,)),
            pltpu.SemaphoreType.DMA((row_group,)),
            pltpu.SemaphoreType.DMA((row_group,)),
            pltpu.SemaphoreType.DMA((x_count - 1,)),
            pltpu.SemaphoreType.DMA((x_count,)),
            pltpu.SemaphoreType.DMA((2,)),
        ],
        compiler_params=pltpu.CompilerParams(collective_id=0, has_side_effects=True),
    )(hidden, gain, weight, ids, lengths)


def per_device(hidden, norm_gain, head_weight, target_ids, seq_lengths):
    x_count = lax.axis_size("x")
    y_count = lax.axis_size("y")
    z_count = lax.axis_size("z")
    c_count = lax.axis_size("c")
    x_index = lax.axis_index("x")
    y_index = lax.axis_index("y")
    z_index = lax.axis_index("z")
    c_index = lax.axis_index("c")
    vert_count = y_count * z_count * c_count
    vert_index = (y_index * z_count + z_index) * c_count + c_index
    tok_local = hidden.shape[0]
    quarter = tok_local // x_count
    vocab_local = head_weight.shape[1]
    group_count = z_count * c_count

    results = score_all(
        hidden, norm_gain, head_weight, target_ids.reshape(1, -1), seq_lengths,
        x_count, group_count, x_count * y_count, vocab_local,
    )
    full_logprob = results[:, 0, :quarter].reshape(-1)
    full_entropy = results[:, 1, :quarter].reshape(-1)
    return (full_logprob, full_entropy)


def solution(mesh):
    wa_count, vert_count = mesh.devices.shape
    y_count = 4
    c_count = 2
    z_count = vert_count // (y_count * c_count)
    fine = Mesh(mesh.devices.reshape(wa_count, y_count, z_count, c_count), ("x",) + VERT)
    in_specs = (P(VERT, "x"), P("x"), P("x", VERT), P(VERT), P())
    out_specs = (P(VERT), P(VERT))
    return jax.shard_map(
        per_device, mesh=fine, in_specs=in_specs, out_specs=out_specs, check_vma=False
    )
```
